32 devices in a mesh: fsdp: 32 (over z, y, x, core).
Axes of the slice: x: 2, y: 2, z: 4, core: 2. Of those that a mesh axis runs over, the one named last changes fastest.
Arguments:
- inputs: bfloat16 [4096, 1024], P('fsdp'), may hold values from -9 to 9
- live_keys: int32 [4096], P('fsdp'), may hold values from 0 to 1, as said below
- triple_weight: bfloat16 [1024, 3072], P('fsdp'), may hold values from -1 to 1
- query_bias: bfloat16 [1024], P('fsdp'), may hold values from -3 to 3
- value_bias: bfloat16 [1024], P('fsdp'), may hold values from -3 to 3
- output_weight: bfloat16 [1024, 1024], P('fsdp'), may hold values from -1.5 to 1.5
- output_bias: bfloat16 [1024], P('fsdp'), may hold values from -3 to 3
- first_gain: bfloat16 [1024], P('fsdp'), may hold values from 0.5 to 1.5
- first_shift: bfloat16 [1024], P('fsdp'), may hold values from -3 to 3
- expand_weight: bfloat16 [1024, 4096], P('fsdp'), may hold values from -0.1875 to 0.1875
- expand_bias: bfloat16 [4096], P('fsdp'), may hold values from -3 to 3
- shrink_weight: bfloat16 [4096, 1024], P('fsdp'), may hold values from -0.09375 to 0.09375
- shrink_bias: bfloat16 [1024], P('fsdp'), may hold values from -3 to 3
- second_gain: bfloat16 [1024], P('fsdp'), may hold values from 0.5 to 1.5
- second_shift: bfloat16 [1024], P('fsdp'), may hold values from -3 to 3
- cotangent: bfloat16 [4096, 1024], P('fsdp'), may hold values from -6 to 6
Outputs:
- layer_out: bfloat16 [4096, 1024], P('fsdp')
- input_grad: bfloat16 [4096, 1024], P('fsdp')
- triple_grad: float32 [1024, 3072], P('fsdp')
- query_bias_grad: float32 [1024], P('fsdp')
- value_bias_grad: float32 [1024], P('fsdp')
- output_grad: float32 [1024, 1024], P('fsdp')
- output_bias_grad: float32 [1024], P('fsdp')
- first_gain_grad: float32 [1024], P('fsdp')
- first_shift_grad: float32 [1024], P('fsdp')
- expand_grad: float32 [1024, 4096], P('fsdp')
- expand_bias_grad: float32 [4096], P('fsdp')
- shrink_grad: float32 [4096, 1024], P('fsdp')
- shrink_bias_grad: float32 [1024], P('fsdp')
- second_gain_grad: float32 [1024], P('fsdp')
- second_shift_grad: float32 [1024], P('fsdp')
The draws below stay inside these ranges and needn't reach their ends.
Inputs may be any that keep to these rules, and one draw needn't show every extreme that they name: `live_keys`: on each device the live rows come first: 2 to 128 of its 128 rows are live, and some device has all 128 live.
All inputs are finite; a program needn't handle non-finite values.
Results may differ from the reference program's by a relative error of at most 0.013.
The reference program's roundings to bfloat16 on the way count: a program that leaves them out, or rounds other values in their place, can miss the bound.
Values may be sent and summed in bfloat16 or wider, within the bound.
A program may use at most 256 MiB of HBM per device.

```python
import jax
import jax.numpy as jnp
from jax import lax

D = 1024
FF = 4096
HEADS = 16
TOK_DEV = 128
TOKENS = 4096


def draw_live_keys(key, part):
    groups = TOKENS // TOK_DEV
    base = jax.random.fold_in(key, 11)
    length_key, chosen_key = jax.random.split(base)
    lengths = jax.random.randint(length_key, (groups,), 2, TOK_DEV + 1).astype(jnp.int32)
    chosen = jax.random.randint(chosen_key, (), 0, groups).astype(jnp.int32)
    lengths = jnp.where(jnp.arange(groups, dtype=jnp.int32) == chosen, TOK_DEV, lengths)
    offsets = jnp.arange(TOK_DEV, dtype=jnp.int32)
    livemask = (offsets[None, :] < lengths[:, None]).astype(jnp.int32)
    return livemask.reshape(TOKENS)


def draw_inputs(key, part):
    groups = TOKENS // TOK_DEV
    base = jax.random.fold_in(key, 31)
    drawn_key = jax.random.fold_in(base, 0)
    values = jnp.clip(jax.random.normal(drawn_key, (groups, TOK_DEV, D), jnp.float32), -6.0, 6.0)
    return values.reshape(TOKENS, D).astype(jnp.bfloat16)


def draw_triple_weight(key, part):
    base = jax.random.fold_in(key, 23)
    query_key, other_key, value_key = jax.random.split(base, 3)
    query_block = jnp.clip(jax.random.normal(query_key, (D, D), jnp.float32), -6.0, 6.0)
    other_block = jnp.clip(jax.random.normal(other_key, (D, D), jnp.float32), -6.0, 6.0)
    value_block = jnp.clip(jax.random.normal(value_key, (D, D), jnp.float32), -6.0, 6.0)
    key_block = other_block
    whole = jnp.concatenate([query_block, key_block, value_block], axis=1) * D ** (-0.5)
    return whole.astype(jnp.bfloat16)


def strengthened(values, key, source, target, blocks, factor):
    def block_of(position):
        return (jnp.arange(values.shape[position]) // (values.shape[position] // blocks)).reshape((-1,) + (1,) * (values.ndim - 1 - position))

    near = jax.random.permutation(key, blocks)[block_of(target)]
    far = (block_of(target) + blocks // 2) % blocks
    return jnp.where((block_of(source) == near) | (block_of(source) == far), factor * values, values)


def shard_levels(own_key, dims, shards, smallest, largest):
    def one(dim, parts):
        draws = jax.random.uniform(jax.random.fold_in(jax.random.fold_in(own_key, 6), dim), (parts,), jnp.float32, smallest / len(shards), largest / len(shards))
        return jnp.repeat(jnp.exp(draws), dims[dim] // parts).reshape((-1,) + (1,) * (len(dims) - dim - 1))

    factor_of = one(*shards[0])
    for cut in shards[1:]:
        factor_of = factor_of * one(*cut)
    return factor_of


def normal_values(rng, dims, spread, most, shards=(), kind=jnp.bfloat16):
    values = jax.random.normal(rng, dims, jnp.float32) * spread
    if len(shards) > 0:
        values = shard_levels(rng, dims, shards, -0.22, 0.18) * values
    return jnp.clip(values, min=-most, max=most).astype(kind)


def bell_draw_with(stream_key, extent, scale, most, cuts, heavy, kind=jnp.bfloat16):
    values = scale * jax.random.normal(stream_key, extent, jnp.float32)
    if cuts:
        values = values * shard_levels(stream_key, extent, cuts, -0.22, 0.18)
    return jnp.clip(strengthened(values, jax.random.fold_in(stream_key, 3), *heavy), -most, most).astype(kind)


def setup_inputs(seed: int = 0) -> dict:
    key_of = jax.random.split(jax.random.key(seed), 17)
    inputs = draw_inputs(jax.random.fold_in(key_of[16], 71), 0)
    live_keys = draw_live_keys(jax.random.fold_in(key_of[16], 71), 0)
    triple_weight = draw_triple_weight(jax.random.fold_in(key_of[16], 71), 0)
    query_bias = normal_values(key_of[3], (D,), 0.5, 3.0, ((0, 32),))
    value_bias = normal_values(key_of[4], (D,), 0.5, 3.0, ((0, 32),))
    output_weight = normal_values(key_of[5], (D, D), (D // 64) ** -0.5, 1.5, ((0, 32),))
    output_bias = normal_values(key_of[6], (D,), 0.5, 3.0, ((0, 32),))
    first_gain = jnp.clip(1.0 + 0.1 * jax.random.normal(key_of[7], (D,), jnp.float32), 0.5, 1.5).astype(jnp.bfloat16)
    first_shift = normal_values(key_of[8], (D,), 0.5, 3.0, ((0, 32),))
    expand_weight = normal_values(key_of[9], (D, FF), D ** -0.5, 0.1875, ((0, 32),))
    expand_bias = normal_values(key_of[10], (FF,), 0.5, 3.0, ((0, 32),))
    shrink_weight = normal_values(key_of[11], (FF, D), FF ** -0.5, 0.09375, ((0, 32),))
    shrink_bias = normal_values(key_of[12], (D,), 0.5, 3.0, ((0, 32),))
    second_gain = jnp.clip(1.0 + 0.1 * jax.random.normal(key_of[13], (D,), jnp.float32), 0.5, 1.5).astype(jnp.bfloat16)
    second_shift = normal_values(key_of[14], (D,), 0.5, 3.0, ((0, 32),))
    cotangent = bell_draw_with(key_of[15], (TOKENS, D), 1.0, 6.0, ((0, 32),), (0, 1, 32, 2.75))
    return {"inputs": inputs, "live_keys": live_keys, "triple_weight": triple_weight, "query_bias": query_bias, "value_bias": value_bias, "output_weight": output_weight, "output_bias": output_bias, "first_gain": first_gain, "first_shift": first_shift, "expand_weight": expand_weight, "expand_bias": expand_bias, "shrink_weight": shrink_weight, "shrink_bias": shrink_bias, "second_gain": second_gain, "second_shift": second_shift, "cotangent": cotangent}


EPSILON = 1e-05
NEGATIVE = -1e+30
ROOT_HALF = 0.7071067811865476
INV_ROOT_TWO_PI = 0.3989422804014327

def batched(form, left, right):
    return jnp.einsum(form, left.astype(jnp.float32), right.astype(jnp.float32))

def layer_norm(hidden, gain, shift):
    center = hidden - lax.optimization_barrier(jnp.mean(hidden, axis=-1, keepdims=True))
    inv_std = lax.rsqrt(lax.optimization_barrier(jnp.mean(center * center, axis=-1, keepdims=True)) + EPSILON)
    normed = center * inv_std
    return (normed * gain.astype(jnp.float32) + shift.astype(jnp.float32), normed, inv_std)

def layer_norm_back(upstream, normed, inv_std, gain):
    scaled = upstream * gain.astype(jnp.float32)
    inner = scaled - lax.optimization_barrier(jnp.mean(scaled, axis=-1, keepdims=True)) - normed * lax.optimization_barrier(jnp.mean(scaled * normed, axis=-1, keepdims=True))
    return (inv_std * inner, lax.optimization_barrier(jnp.sum(upstream * normed, axis=0)), lax.optimization_barrier(jnp.sum(upstream, axis=0)))

def normal_cdf(values):
    return 0.5 * (1.0 + lax.erf(values * ROOT_HALF))

def masked_scores(query, keys, live):
    scores = batched('qhd,khd->hqk', query, keys)
    allowed = live == 1
    return jnp.where(allowed[None, None, :], scores, NEGATIVE)

def forward(params, tokens, live):
    triple_weight, query_bias, value_bias, output_weight, output_bias, first_gain, first_shift, expand_weight, expand_bias, shrink_weight, shrink_bias, second_gain, second_shift = params
    row_count = tokens.shape[0]
    width_all = tokens.shape[1]
    head_size = width_all // HEADS
    factor = head_size ** (-0.5)
    projected = jnp.dot(tokens, triple_weight, preferred_element_type=jnp.float32)
    query = ((projected[:, :width_all] + query_bias.astype(jnp.float32)) * factor).astype(jnp.bfloat16)
    keys = projected[:, width_all:2 * width_all].astype(jnp.bfloat16)
    values = (projected[:, 2 * width_all:] + value_bias.astype(jnp.float32)).astype(jnp.bfloat16)
    query = query.reshape(row_count, HEADS, head_size)
    keys = keys.reshape(row_count, HEADS, head_size)
    values = values.reshape(row_count, HEADS, head_size)
    scores = masked_scores(query, keys, live)
    top = lax.optimization_barrier(jnp.max(scores, axis=-1, keepdims=True))
    expo = jnp.exp(scores - top)
    total = lax.optimization_barrier(jnp.sum(expo, axis=-1, keepdims=True))
    log_total = top + jnp.log(total)
    probs = (expo / total).astype(jnp.bfloat16)
    context = batched('hqk,khd->qhd', probs, values).astype(jnp.bfloat16).reshape(row_count, width_all)
    first_in = tokens.astype(jnp.float32) + jnp.dot(context, output_weight, preferred_element_type=jnp.float32) + output_bias.astype(jnp.float32)
    middle, first_norm, first_rate = layer_norm(first_in, first_gain, first_shift)
    mid_low = middle.astype(jnp.bfloat16)
    pre_act = jnp.dot(mid_low, expand_weight, preferred_element_type=jnp.float32) + expand_bias.astype(jnp.float32)
    act_low = (pre_act * normal_cdf(pre_act)).astype(jnp.bfloat16)
    second_in = middle + jnp.dot(act_low, shrink_weight, preferred_element_type=jnp.float32) + shrink_bias.astype(jnp.float32)
    result, second_norm, second_rate = layer_norm(second_in, second_gain, second_shift)
    saved = (tokens, live, query, keys, values, log_total, context, first_norm, first_rate, mid_low, pre_act, act_low, second_norm, second_rate)
    return (result.astype(jnp.bfloat16), saved)

def back_upper(params, saved, upstream):
    triple_weight, query_bias, value_bias, output_weight, output_bias, first_gain, first_shift, expand_weight, expand_bias, shrink_weight, shrink_bias, second_gain, second_shift = params
    tokens, live, query, keys, values, log_total, context, first_norm, first_rate, mid_low, pre_act, act_low, second_norm, second_rate = saved
    d_second, second_gain_grad, second_shift_grad = layer_norm_back(upstream.astype(jnp.float32), second_norm, second_rate, second_gain)
    d_second_low = d_second.astype(jnp.bfloat16)
    shrink_grad = jnp.dot(act_low.T, d_second_low, preferred_element_type=jnp.float32)
    shrink_bias_grad = lax.optimization_barrier(jnp.sum(d_second, axis=0))
    d_act = jnp.dot(d_second_low, shrink_weight.T, preferred_element_type=jnp.float32)
    slope = normal_cdf(pre_act) + pre_act * jnp.exp(-0.5 * pre_act * pre_act) * INV_ROOT_TWO_PI
    d_pre = d_act * slope
    expand_bias_grad = lax.optimization_barrier(jnp.sum(d_pre, axis=0))
    d_pre_low = d_pre.astype(jnp.bfloat16)
    expand_grad = jnp.dot(mid_low.T, d_pre_low, preferred_element_type=jnp.float32)
    d_mid = d_second + jnp.dot(d_pre_low, expand_weight.T, preferred_element_type=jnp.float32)
    d_first, first_gain_grad, first_shift_grad = layer_norm_back(d_mid, first_norm, first_rate, first_gain)
    grads = (first_gain_grad, first_shift_grad, expand_grad, expand_bias_grad, shrink_grad, shrink_bias_grad, second_gain_grad, second_shift_grad)
    return (grads, d_first)

def back_lower(params, saved, d_first):
    triple_weight, query_bias, value_bias, output_weight, output_bias, first_gain, first_shift, expand_weight, expand_bias, shrink_weight, shrink_bias, second_gain, second_shift = params
    tokens, live, query, keys, values, log_total, context, first_norm, first_rate, mid_low, pre_act, act_low, second_norm, second_rate = saved
    row_count = tokens.shape[0]
    width_all = tokens.shape[1]
    head_size = width_all // HEADS
    factor = head_size ** (-0.5)
    d_first_low = d_first.astype(jnp.bfloat16)
    output_grad = jnp.dot(context.T, d_first_low, preferred_element_type=jnp.float32)
    output_bias_grad = lax.optimization_barrier(jnp.sum(d_first, axis=0))
    d_context = jnp.dot(d_first_low, output_weight.T, preferred_element_type=jnp.float32).astype(jnp.bfloat16)
    d_context = d_context.reshape(row_count, HEADS, head_size)
    scores = masked_scores(query, keys, live)
    probs = jnp.exp(scores - log_total)
    probs_low = probs.astype(jnp.bfloat16)
    d_values = batched('hqk,qhd->khd', probs_low, d_context)
    d_probs = batched('qhd,khd->hqk', d_context, values)
    inner = lax.optimization_barrier(jnp.sum(probs * d_probs, axis=-1, keepdims=True))
    d_scores = (probs * (d_probs - inner)).astype(jnp.bfloat16)
    d_query = factor * batched('hqk,khd->qhd', d_scores, keys)
    d_keys = batched('hqk,qhd->khd', d_scores, query)
    d_query = d_query.reshape(row_count, width_all)
    d_keys = d_keys.reshape(row_count, width_all)
    d_values = d_values.reshape(row_count, width_all)
    d_proj = jnp.concatenate([d_query, d_keys, d_values], axis=1).astype(jnp.bfloat16)
    triple_grad = jnp.dot(tokens.T, d_proj, preferred_element_type=jnp.float32)
    query_bias_grad = lax.optimization_barrier(jnp.sum(d_query, axis=0))
    value_bias_grad = lax.optimization_barrier(jnp.sum(d_values, axis=0))
    input_grad = (d_first + jnp.dot(d_proj, triple_weight.T, preferred_element_type=jnp.float32)).astype(jnp.bfloat16)
    grads = (triple_grad, query_bias_grad, value_bias_grad, output_grad, output_bias_grad)
    return (grads, input_grad)

def reference(inputs, live_keys, triple_weight, query_bias, value_bias, output_weight, output_bias, first_gain, first_shift, expand_weight, expand_bias, shrink_weight, shrink_bias, second_gain, second_shift, cotangent):
    params = (triple_weight, query_bias, value_bias, output_weight, output_bias, first_gain, first_shift, expand_weight, expand_bias, shrink_weight, shrink_bias, second_gain, second_shift)
    groups = TOKENS // TOK_DEV
    series = (inputs.reshape(groups, TOK_DEV, D), live_keys.reshape(groups, TOK_DEV), cotangent.reshape(groups, TOK_DEV, D))
    zeros = tuple((jnp.zeros(item.shape, jnp.float32) for item in params))

    def advance(carry, element):
        tokens, live, upstream = element
        result, saved = forward(params, tokens, live)
        upper, d_first = back_upper(params, saved, upstream)
        lower, input_grad = back_lower(params, saved, d_first)
        grads = lower + upper
        return (tuple((old + new for old, new in zip(carry, grads))), (result, input_grad))
    totals, (results, input_grads) = lax.scan(advance, zeros, series)
    return (results.reshape(TOKENS, D), input_grads.reshape(TOKENS, D), totals[0], totals[1], totals[2], totals[3], totals[4], totals[5], totals[6], totals[7], totals[8], totals[9], totals[10], totals[11], totals[12])
```

```python
import jax
import jax.numpy as jnp
from jax import lax
from jax.experimental import pallas as pl
from jax.experimental.pallas import tpu as pltpu
from jax.sharding import PartitionSpec as P

HEADS = 16


EPSILON = 1e-05
NEGATIVE = -1e30
ROOT_HALF = 0.7071067811865476
INV_ROOT_TWO_PI = 0.3989422804014327


def batched(form, left, right):
    return jnp.einsum(form, left, right, preferred_element_type=jnp.float32)


def layer_norm(hidden, gain, shift):
    center = hidden - jnp.mean(hidden, axis=-1, keepdims=True)
    inv_std = lax.rsqrt(jnp.mean(center * center, axis=-1, keepdims=True) + EPSILON)
    normed = center * inv_std
    return (normed * gain.astype(jnp.float32) + shift.astype(jnp.float32), normed, inv_std)


def layer_norm_back(upstream, normed, inv_std, gain):
    scaled = upstream * gain.astype(jnp.float32)
    inner = (
        scaled
        - jnp.mean(scaled, axis=-1, keepdims=True)
        - normed * jnp.mean(scaled * normed, axis=-1, keepdims=True)
    )
    return (inv_std * inner, jnp.sum(upstream * normed, axis=0), jnp.sum(upstream, axis=0))


def normal_cdf(values):
    return 0.5 * (1.0 + lax.erf(values * ROOT_HALF))


def masked_scores(query, keys, live):
    scores = batched("qhd,khd->hqk", query, keys)
    allowed = live == 1
    return jnp.where(allowed[None, None, :], scores, NEGATIVE)


def forward(params, tokens, live):
    (
        triple_weight,
        query_bias,
        value_bias,
        output_weight,
        output_bias,
        first_gain,
        first_shift,
        expand_weight,
        expand_bias,
        shrink_weight,
        shrink_bias,
        second_gain,
        second_shift,
    ) = params
    row_count = tokens.shape[0]
    width_all = tokens.shape[1]
    head_size = width_all // HEADS
    factor = head_size ** (-0.5)
    projected = jnp.dot(tokens, triple_weight, preferred_element_type=jnp.float32)
    query = ((projected[:, :width_all] + query_bias.astype(jnp.float32)) * factor).astype(
        jnp.bfloat16
    )
    keys = projected[:, width_all : 2 * width_all].astype(jnp.bfloat16)
    values = (projected[:, 2 * width_all :] + value_bias.astype(jnp.float32)).astype(jnp.bfloat16)
    query = query.reshape(row_count, HEADS, head_size)
    keys = keys.reshape(row_count, HEADS, head_size)
    values = values.reshape(row_count, HEADS, head_size)
    scores = masked_scores(query, keys, live)
    top = jnp.max(scores, axis=-1, keepdims=True)
    expo = jnp.exp(scores - top)
    total = jnp.sum(expo, axis=-1, keepdims=True)
    log_total = top + jnp.log(total)
    probs = (expo / total).astype(jnp.bfloat16)
    context = (
        batched("hqk,khd->qhd", probs, values).astype(jnp.bfloat16).reshape(row_count, width_all)
    )
    first_in = (
        tokens.astype(jnp.float32)
        + jnp.dot(context, output_weight, preferred_element_type=jnp.float32)
        + output_bias.astype(jnp.float32)
    )
    middle, first_norm, first_rate = layer_norm(first_in, first_gain, first_shift)
    mid_low = middle.astype(jnp.bfloat16)
    pre_act = jnp.dot(
        mid_low, expand_weight, preferred_element_type=jnp.float32
    ) + expand_bias.astype(jnp.float32)
    act_low = (pre_act * normal_cdf(pre_act)).astype(jnp.bfloat16)
    second_in = (
        middle
        + jnp.dot(act_low, shrink_weight, preferred_element_type=jnp.float32)
        + shrink_bias.astype(jnp.float32)
    )
    result, second_norm, second_rate = layer_norm(second_in, second_gain, second_shift)
    saved = (
        tokens,
        live,
        query,
        keys,
        values,
        log_total,
        context,
        first_norm,
        first_rate,
        mid_low,
        pre_act,
        act_low,
        second_norm,
        second_rate,
    )
    return (result.astype(jnp.bfloat16), saved)


def back_upper(params, saved, upstream):
    (
        triple_weight,
        query_bias,
        value_bias,
        output_weight,
        output_bias,
        first_gain,
        first_shift,
        expand_weight,
        expand_bias,
        shrink_weight,
        shrink_bias,
        second_gain,
        second_shift,
    ) = params
    (
        tokens,
        live,
        query,
        keys,
        values,
        log_total,
        context,
        first_norm,
        first_rate,
        mid_low,
        pre_act,
        act_low,
        second_norm,
        second_rate,
    ) = saved
    d_second, second_gain_grad, second_shift_grad = layer_norm_back(
        upstream.astype(jnp.float32), second_norm, second_rate, second_gain
    )
    d_second_low = d_second.astype(jnp.bfloat16)
    shrink_bias_grad = jnp.sum(d_second, axis=0)
    d_act = jnp.dot(d_second_low, shrink_weight.T, preferred_element_type=jnp.float32)
    slope = normal_cdf(pre_act) + pre_act * jnp.exp(-0.5 * pre_act * pre_act) * INV_ROOT_TWO_PI
    d_pre = d_act * slope
    expand_bias_grad = jnp.sum(d_pre, axis=0)
    d_pre_low = d_pre.astype(jnp.bfloat16)
    d_mid = d_second + jnp.dot(d_pre_low, expand_weight.T, preferred_element_type=jnp.float32)
    d_first, first_gain_grad, first_shift_grad = layer_norm_back(
        d_mid, first_norm, first_rate, first_gain
    )
    small = (
        first_gain_grad,
        first_shift_grad,
        expand_bias_grad,
        shrink_bias_grad,
        second_gain_grad,
        second_shift_grad,
    )
    pairs = ((mid_low, d_pre_low), (act_low, d_second_low))
    return (small, pairs, d_first)


def back_lower(params, saved, d_first):
    (
        triple_weight,
        query_bias,
        value_bias,
        output_weight,
        output_bias,
        first_gain,
        first_shift,
        expand_weight,
        expand_bias,
        shrink_weight,
        shrink_bias,
        second_gain,
        second_shift,
    ) = params
    (
        tokens,
        live,
        query,
        keys,
        values,
        log_total,
        context,
        first_norm,
        first_rate,
        mid_low,
        pre_act,
        act_low,
        second_norm,
        second_rate,
    ) = saved
    row_count = tokens.shape[0]
    width_all = tokens.shape[1]
    head_size = width_all // HEADS
    factor = head_size ** (-0.5)
    d_first_low = d_first.astype(jnp.bfloat16)
    output_bias_grad = jnp.sum(d_first, axis=0)
    d_context = jnp.dot(d_first_low, output_weight.T, preferred_element_type=jnp.float32).astype(
        jnp.bfloat16
    )
    d_context = d_context.reshape(row_count, HEADS, head_size)
    scores = masked_scores(query, keys, live)
    probs = jnp.exp(scores - log_total)
    probs_low = probs.astype(jnp.bfloat16)
    d_values = batched("hqk,qhd->khd", probs_low, d_context)
    d_probs = batched("qhd,khd->hqk", d_context, values)
    inner = jnp.sum(probs * d_probs, axis=-1, keepdims=True)
    d_scores = (probs * (d_probs - inner)).astype(jnp.bfloat16)
    d_query = factor * batched("hqk,khd->qhd", d_scores, keys)
    d_keys = batched("hqk,qhd->khd", d_scores, query)
    d_query = d_query.reshape(row_count, width_all)
    d_keys = d_keys.reshape(row_count, width_all)
    d_values = d_values.reshape(row_count, width_all)
    d_proj = jnp.concatenate([d_query, d_keys, d_values], axis=1).astype(jnp.bfloat16)
    query_bias_grad = jnp.sum(d_query, axis=0)
    value_bias_grad = jnp.sum(d_values, axis=0)
    input_grad = (
        d_first + jnp.dot(d_proj, triple_weight.T, preferred_element_type=jnp.float32)
    ).astype(jnp.bfloat16)
    small = (query_bias_grad, value_bias_grad, output_bias_grad)
    pairs = ((tokens, d_proj), (context, d_first_low))
    return (small, pairs, input_grad)


def swap(value, bit, count):
    return lax.ppermute(value, "fsdp", [(i, i ^ (1 << bit)) for i in range(count)])


def own_bit(bit):
    return (lax.axis_index("fsdp") >> bit) & 1


def place(base, value, places, levels):
    starts = [0] * base.ndim
    for bit, at in places:
        starts[levels - 1 - bit] = at
    return lax.dynamic_update_slice(base, value, starts)


def grown(value, bits, levels):
    shape = list(value.shape)
    for bit in bits:
        shape[levels - 1 - bit] = 2
    return jnp.zeros(shape, value.dtype)


def join(own, other, bit, levels):
    mine = own_bit(bit)
    base = place(grown(own, (bit,), levels), own, ((bit, mine),), levels)
    return place(base, other, ((bit, 1 - mine),), levels)


def orders(levels):
    ring = list(range(1, levels))
    return [ring[k * len(ring) // 3 :] + ring[: k * len(ring) // 3] for k in range(3)]


def collect(shard, order, count):
    levels = count.bit_length() - 1
    held = shard.reshape((1,) * levels + shard.shape)
    steps = list(reversed(order))
    for bit in steps[:-1]:
        held = join(held, swap(held, bit, count), bit, levels)
    bit = steps[-1]
    across = swap(held, bit, count)
    beside = swap(held, 0, count)
    corner = swap(across, 0, count)
    mine, core = own_bit(bit), own_bit(0)
    full = grown(held, (bit, 0), levels)
    full = place(full, held, ((bit, mine), (0, core)), levels)
    full = place(full, beside, ((bit, mine), (0, 1 - core)), levels)
    full = place(full, across, ((bit, 1 - mine), (0, core)), levels)
    held = place(full, corner, ((bit, 1 - mine), (0, 1 - core)), levels)
    return held.reshape((count * shard.shape[0],) + shard.shape[1:])


def halve(terms, order, count, last):
    levels = count.bit_length() - 1
    for bit in order:
        axis = terms.ndim - 3 - bit if last else terms.ndim - 2 - bit
        mine = own_bit(bit)
        keep = lax.dynamic_slice_in_dim(terms, mine, 1, axis)
        send = lax.dynamic_slice_in_dim(terms, 1 - mine, 1, axis)
        total = keep.astype(jnp.float32) + swap(send, bit, count).astype(jnp.float32)
        terms = total if bit == order[-1] else total.astype(terms.dtype)
    return terms.reshape(terms.shape[-2:])


def by_core(left, count):
    parts = left.reshape(left.shape[0], count // 2, 2, left.shape[1] // count)
    core = own_bit(0)
    pick = lambda at: lax.dynamic_index_in_dim(parts, at, 2, keepdims=False).reshape(
        left.shape[0], left.shape[1] // 2
    )
    return (pick(core), pick(1 - core))


def pair_up(left, right, count):
    mine, other = by_core(left, count)
    return (
        jnp.concatenate([mine, swap(other, 0, count)], axis=0),
        jnp.concatenate([right, swap(right, 0, count)], axis=0),
    )


def summed_grad(left, right, pieces, count):
    levels = count.bit_length() - 1
    results = []
    offset = 0
    for extent, order in pieces:
        term = jnp.einsum(
            "tk,tw->kw",
            left,
            right[:, offset : offset + extent],
            preferred_element_type=jnp.float32,
        ).astype(jnp.bfloat16)
        term = term.reshape((2,) * (levels - 1) + (left.shape[1] * 2 // count, extent))
        results.append(halve(term, order, count, False))
        offset = offset + extent
    return results[0] if len(results) == 1 else jnp.concatenate(results, axis=1)


def body(
    inputs,
    live_keys,
    triple_weight,
    query_bias,
    value_bias,
    output_weight,
    output_bias,
    first_gain,
    first_shift,
    expand_weight,
    expand_bias,
    shrink_weight,
    shrink_bias,
    second_gain,
    second_shift,
    cotangent,
):
    count = lax.axis_size("fsdp")
    levels = count.bit_length() - 1
    width = inputs.shape[1]
    ways = orders(levels)
    vectors = (
        query_bias,
        value_bias,
        output_bias,
        first_gain,
        first_shift,
        expand_bias,
        shrink_bias,
        second_gain,
        second_shift,
    )
    packed = collect(jnp.concatenate(vectors)[None, :], ways[0], count)
    wide = []
    offset = 0
    for vector in vectors:
        wide.append(packed[:, offset : offset + vector.shape[0]].reshape(-1))
        offset = offset + vector.shape[0]
    gathered = (
        collect(triple_weight, ways[2], count),
        wide[0],
        wide[1],
        collect(output_weight, ways[0], count),
        wide[2],
        wide[3],
        wide[4],
        collect(expand_weight, ways[0], count),
        wide[5],
        collect(shrink_weight, ways[1], count),
        wide[6],
        wide[7],
        wide[8],
    )
    layer_out, saved = forward(gathered, inputs, live_keys)
    upper_small, upper_pairs, d_first = back_upper(gathered, saved, cotangent)
    lower_small, lower_pairs, input_grad = back_lower(gathered, saved, d_first)
    hidden = expand_weight.shape[1]
    shrink_grad = summed_grad(
        *pair_up(*upper_pairs[1], count),
        ((width * 3 // 4, ways[1]), (width // 4, ways[2])),
        count,
    )
    expand_grad = summed_grad(
        *pair_up(*upper_pairs[0], count),
        ((hidden * 3 // 4, ways[0]), (hidden // 4, ways[2])),
        count,
    )
    output_grad = summed_grad(*pair_up(*lower_pairs[1], count), ((width, ways[1]),), count)
    triple_grad = summed_grad(
        *pair_up(*lower_pairs[0], count),
        ((width, ways[0]), (width, ways[1]), (width, ways[2])),
        count,
    )
    sums = lower_small + upper_small
    terms = jnp.concatenate([item.reshape(count, -1) for item in sums], axis=1)
    terms = terms.reshape((2,) * levels + (1, terms.shape[1]))
    owned = halve(terms, list(range(levels)), count, True)[0]
    small = []
    offset = 0
    for item in sums:
        extent = item.shape[0] // count
        small.append(owned[offset : offset + extent])
        offset = offset + extent
    return (
        layer_out,
        input_grad,
        triple_grad,
        small[0],
        small[1],
        output_grad,
        small[2],
        small[3],
        small[4],
        expand_grad,
        small[5],
        shrink_grad,
        small[6],
        small[7],
        small[8],
    )


PLANES = 4
CHIPS = 4
GROUP = 2 * CHIPS
MESH = pl.DeviceIdType.MESH


def nn(left, right):
    return lax.dot_general(
        left, right, (((1,), (0,)), ((), ())), preferred_element_type=jnp.float32
    )


def nt(left, right):
    return lax.dot_general(
        left, right, (((1,), (1,)), ((), ())), preferred_element_type=jnp.float32
    )


def tn(left, right):
    return lax.dot_general(
        left, right, (((0,), (0,)), ((), ())), preferred_element_type=jnp.float32
    )


def flat(value):
    return value.reshape((-1, value.shape[-1]))


def normalize(hidden):
    center = hidden - jnp.mean(hidden, axis=-1, keepdims=True)
    rate = lax.rsqrt(jnp.mean(center * center, axis=-1, keepdims=True) + EPSILON)
    return center * rate, rate


def normalize_back(upstream, normed, rate, gain):
    scaled = upstream * gain
    inner = (
        scaled
        - jnp.mean(scaled, axis=-1, keepdims=True)
        - normed * jnp.mean(scaled * normed, axis=-1, keepdims=True)
    )
    return (
        rate * inner,
        jnp.sum(upstream * normed, axis=0, keepdims=True),
        jnp.sum(upstream, axis=0, keepdims=True),
    )


COPIES = {}
for _name, _many in (
    ("v", 3), ("vz", 3), ("vs", 1), ("t", 3), ("tz", 3), ("ts", 4), ("e", 3), ("ez", 3),
    ("es", 4), ("oz", 3), ("os", 4), ("sz", 3), ("ss", 4), ("x", 3), ("r1", 3), ("m", 3),
    ("r2", 3), ("d2", 3), ("r3", 3), ("d1", 3), ("r4", 3), ("gss", 1), ("ges", 1),
    ("gos", 1), ("gts", 1), ("gsz", 3), ("gez", 3), ("goz", 3), ("gtz", 3), ("gep", 3),
    ("gtp", 3), ("a", 3), ("bz", 3), ("bs", 1),
):
    COPIES[_name] = (sum(many for _, many in COPIES.values()), _many)
COPY_COUNT = sum(many for _, many in COPIES.values())


def plane_kernel(
    x_ref, live_ref, t_ref, vec_ref, eb_ref, o_ref, e_ref, s_ref, ct_ref,
    lo_ref, ig_ref, tg_ref, og_ref, eg_ref, sg_ref, small_ref, ebg_ref,
    vbuf, vfull, vchip, vhid, tsend, tbuf, esend, ebuf, obuf, sbuf, xg, mg, d2g, d1g,
    rsend, rrecv, keep, qkv, pbuf, ctx, slope, act, dpre, dproj, norm1, rate1, mid, dtok,
    gs_own, gs_out, gs_in, gs_zout, gs_zin,
    ge_own, ge_out, ge_in, ge_zout, ge_zin, ge_pout, ge_pin,
    go_own, go_out, go_in, go_zout, go_zin,
    gt_own, gt_out, gt_in, gt_zout, gt_zin, gt_pout, gt_pin,
    apart, ain, bpart, bin_, bsum, bsib, send_sem, recv_sem,
):
    me = lax.axis_index("fsdp")
    core = lax.rem(me, 2)
    chip = lax.rem(me // 2, CHIPS)
    plane = me // GROUP
    sibling = me + 1 - 2 * core

    def flip(base, k):
        return lax.rem(base + k, 2) + 2 * lax.rem(base // 2 + k // 2, 2)

    def chip_at(k):
        return flip(chip, k)

    def plane_at(k):
        return flip(plane, k)

    def mate(k):
        return plane * GROUP + chip_at(k) * 2 + core

    def above(k):
        return plane_at(k) * GROUP + chip * 2 + core

    def copy(name, at, source, target, device):
        spot = COPIES[name][0] + at
        return pltpu.make_async_remote_copy(
            src_ref=source,
            dst_ref=target,
            send_sem=send_sem.at[spot],
            recv_sem=recv_sem.at[spot],
            device_id=(device,),
            device_id_type=MESH,
        )

    moves = {
        "v": lambda k: copy(
            "v", k - 1, vbuf.at[plane, chip, core], vbuf.at[plane, chip, core], mate(k)
        ),
        "vz": lambda k: copy(
            "vz", k - 1, vbuf.at[plane, :, core], vbuf.at[plane, :, core], above(k)
        ),
        "vs": lambda k: copy("vs", 0, vbuf.at[:, :, core], vbuf.at[:, :, core], sibling),
        "t": lambda k: copy(
            "t", k - 1, tsend.at[chip_at(k)], tbuf.at[plane, chip, core], mate(k)
        ),
        "tz": lambda k: copy(
            "tz", k - 1, tbuf.at[plane, :, core], tbuf.at[plane, :, core], above(k)
        ),
        "ts": lambda k: copy(
            "ts", k, tbuf.at[plane_at(k), :, core], tbuf.at[plane_at(k), :, core], sibling
        ),
        "e": lambda k: copy(
            "e", k - 1, esend.at[chip_at(k)], ebuf.at[plane, chip, core], mate(k)
        ),
        "ez": lambda k: copy(
            "ez", k - 1, ebuf.at[plane, :, core], ebuf.at[plane, :, core], above(k)
        ),
        "es": lambda k: copy(
            "es", k, ebuf.at[plane_at(k), :, core], ebuf.at[plane_at(k), :, core], sibling
        ),
        "oz": lambda k: copy(
            "oz", k - 1, obuf.at[plane, core], obuf.at[plane, core], above(k)
        ),
        "os": lambda k: copy(
            "os", k, obuf.at[plane_at(k), core], obuf.at[plane_at(k), core], sibling
        ),
        "sz": lambda k: copy(
            "sz", k - 1, sbuf.at[plane, core], sbuf.at[plane, core], above(k)
        ),
        "ss": lambda k: copy(
            "ss", k, sbuf.at[plane_at(k), core], sbuf.at[plane_at(k), core], sibling
        ),
        "x": lambda k: copy("x", k - 1, x_ref, xg.at[k], mate(k)),
        "m": lambda k: copy("m", k - 1, mg.at[0], mg.at[k], mate(k)),
        "d2": lambda k: copy("d2", k - 1, d2g.at[0], d2g.at[k], mate(k)),
        "d1": lambda k: copy("d1", k - 1, d1g.at[0], d1g.at[k], mate(k)),
        "gss": lambda k: copy("gss", 0, gs_out, gs_in, sibling),
        "ges": lambda k: copy("ges", 0, ge_out, ge_in, sibling),
        "gos": lambda k: copy("gos", 0, go_out, go_in, sibling),
        "gts": lambda k: copy("gts", 0, gt_out, gt_in, sibling),
        "gsz": lambda k: copy("gsz", k - 1, gs_zout.at[k - 1], gs_zin.at[k - 1], above(k)),
        "gez": lambda k: copy("gez", k - 1, ge_zout.at[k - 1], ge_zin.at[k - 1], above(k)),
        "goz": lambda k: copy("goz", k - 1, go_zout.at[k - 1], go_zin.at[k - 1], above(k)),
        "gtz": lambda k: copy("gtz", k - 1, gt_zout.at[k - 1], gt_zin.at[k - 1], above(k)),
        "gep": lambda k: copy("gep", k - 1, ge_pout.at[chip_at(k)], ge_pin.at[chip], mate(k)),
        "gtp": lambda k: copy("gtp", k - 1, gt_pout.at[chip_at(k)], gt_pin.at[chip], mate(k)),
        "a": lambda k: copy("a", k - 1, apart, ain.at[k - 1], mate(k)),
        "bz": lambda k: copy("bz", k - 1, bpart, bin_.at[k - 1], above(k)),
        "bs": lambda k: copy("bs", 0, bsum, bsib, sibling),
    }
    for turn in range(4):
        name = "r%d" % (turn + 1)
        moves[name] = lambda k, name=name, turn=turn: copy(
            name, k - 1, rsend.at[turn, k - 1], rrecv.at[turn, k - 1], mate(k)
        )

    def span(name):
        many = COPIES[name][1]
        return range(1, 4) if many == 3 else range(many)

    def start(name):
        for k in span(name):
            moves[name](k).start()

    def arrive(name):
        for k in span(name):
            moves[name](k).wait_recv()

    barrier = pltpu.get_barrier_semaphore()
    for k in range(1, 4):
        for device in (mate(k), above(k)):
            pl.semaphore_signal(barrier, inc=1, device_id=(device,), device_id_type=MESH)
    pl.semaphore_signal(barrier, inc=1, device_id=(sibling,), device_id_type=MESH)

    vec = vec_ref[...]
    lane = lax.broadcasted_iota(jnp.int32, (8, 128), 1) // 32
    row = lax.broadcasted_iota(jnp.int32, (8, 128), 0)
    by_row = lax.rem(chip, 2) * 2 + core
    by_head = lax.rem(plane, 2) * 2 + core
    spread = jnp.concatenate([vec, vec, vec, vec], axis=1)
    spread = jnp.where(lane == jnp.where(row < 2, by_head, by_row), spread, 0.0)
    own_rows = vbuf.at[plane, chip, core]
    own_rows[0:8, :] = spread
    own_rows[8:9, :] = eb_ref[...]
    own_rows[9:10, :] = live_ref[...]
    own_rows[10:16, :] = jnp.zeros((6, 128), jnp.float32)
    width = x_ref.shape[1]
    part = width // PLANES
    piece = part // CHIPS
    for other in range(CHIPS):
        tsend[other] = jnp.concatenate(
            [
                t_ref[:, kind * width + zz * part + other * piece :][:, :piece]
                for kind in range(3)
                for zz in range(PLANES)
            ],
            axis=1,
        )
        for zz in range(PLANES):
            esend[other, :, zz * part : (zz + 1) * part] = e_ref[
                :, (zz * CHIPS + other) * part : (zz * CHIPS + other + 1) * part
            ]
    tbuf[plane, chip, core] = tsend[chip]
    ebuf[plane, chip, core] = esend[chip]
    pl.semaphore_wait(barrier, 7)

    start("v")
    start("t")
    xg[0] = x_ref[...]
    obuf[plane, core] = o_ref[...]
    sbuf[plane, core] = s_ref[...]
    arrive("v")
    start("vz")
    arrive("t")
    start("tz")
    start("x")
    start("e")
    moves["ts"](0).start()
    moves["os"](0).start()
    moves["ss"](0).start()
    arrive("vz")
    start("vs")
    for k in (1, 2, 3):
        moves["tz"](k).wait_recv()
        moves["ts"](k).start()
    start("oz")
    arrive("e")
    start("ez")
    moves["es"](0).start()
    start("sz")
    arrive("vs")
    for block in range(8):
        total = None
        for i in range(4):
            term = vbuf[block // 2, (block % 2) * 2 + i // 2, i % 2]
            total = term if total is None else total + term
        vfull[:, 128 * block : 128 * block + 128] = total
        vhid[:, 128 * block : 128 * block + 128] = vbuf[block // 2, chip, block % 2][8:16]
    for half in range(2):
        vchip[:, 128 * half : 128 * half + 128] = (
            vbuf[2 * half, chip, 0]
            + vbuf[2 * half, chip, 1]
            + vbuf[2 * half + 1, chip, 0]
            + vbuf[2 * half + 1, chip, 1]
        )
    arrive("ts")
    arrive("x")
    for k in (1, 2, 3):
        moves["oz"](k).wait_recv()
        moves["os"](k).start()
    arrive("os")

    head = width // HEADS
    factor = head ** (-0.5)
    heads = range(PLANES)

    def attend(step, carry):
        k = 3 - step
        tokens = xg[k]
        proj = nn(tokens[:, :part], flat(tbuf[0]))
        for zz in range(1, PLANES):
            proj = proj + nn(tokens[:, zz * part : (zz + 1) * part], flat(tbuf[zz]))
        query = ((proj[:, :part] + vchip[0:1, :]) * factor).astype(jnp.bfloat16)
        keys = proj[:, part : 2 * part].astype(jnp.bfloat16)
        values = (proj[:, 2 * part :] + vchip[1:2, :]).astype(jnp.bfloat16)
        qkv[k, :, :part] = query
        qkv[k, :, part : 2 * part] = keys
        qkv[k, :, 2 * part :] = values
        live = vbuf[plane, chip_at(k), core][9:10, :] > 0.5
        joined = []
        for h in heads:
            cols = slice(h * head, (h + 1) * head)
            scores = jnp.where(live, nt(query[:, cols], keys[:, cols]), NEGATIVE)
            expo = jnp.exp(scores - jnp.max(scores, axis=-1, keepdims=True))
            probs = expo / jnp.sum(expo, axis=-1, keepdims=True)
            pbuf[k, h] = probs
            joined.append(nn(probs.astype(jnp.bfloat16), values[:, cols]))
        context = jnp.concatenate(joined, axis=1).astype(jnp.bfloat16)
        ctx[k] = context
        term = nn(context, flat(obuf[...]))

        @pl.when(k > 0)
        def _():
            rsend[0, k - 1] = term.astype(jnp.bfloat16)
            moves["r1"](k).start()

        @pl.when(k == 0)
        def _():
            keep[...] = term

        return carry

    lax.fori_loop(0, 4, attend, 0)

    def collected(turn):
        total = keep[...]
        for k in (1, 2, 3):
            moves["r%d" % (turn + 1)](k).wait_recv()
            total = total + rrecv[turn, k - 1].astype(jnp.float32)
        return total

    first_in = x_ref[...].astype(jnp.float32) + collected(0) + vfull[2:3, :]
    normed, rate = normalize(first_in)
    norm1[...] = normed
    rate1[...] = jnp.broadcast_to(rate, rate1.shape)
    middle = normed * vfull[3:4, :] + vfull[4:5, :]
    mid[...] = middle
    mg[0] = middle.astype(jnp.bfloat16)
    start("m")

    for k in (1, 2, 3):
        moves["ez"](k).wait_recv()
        moves["es"](k).start()
    arrive("es")
    for k in (1, 2, 3):
        moves["sz"](k).wait_recv()
        moves["ss"](k).start()
    arrive("ss")

    def feed(k, carry):
        @pl.when(k > 0)
        def _():
            moves["m"](k).wait_recv()

        low = mg[k]
        pre = vhid[0:1, :] + nn(low[:, :part], flat(ebuf[0]))
        for zz in range(1, PLANES):
            pre = pre + nn(low[:, zz * part : (zz + 1) * part], flat(ebuf[zz]))
        cdf = normal_cdf(pre)
        slope[k] = cdf + pre * jnp.exp(-0.5 * pre * pre) * INV_ROOT_TWO_PI
        active = (pre * cdf).astype(jnp.bfloat16)
        act[k] = active
        term = nn(active[:, :part], flat(sbuf[0]))
        for zz in range(1, PLANES):
            term = term + nn(active[:, zz * part : (zz + 1) * part], flat(sbuf[zz]))

        @pl.when(k > 0)
        def _():
            rsend[1, k - 1] = term.astype(jnp.bfloat16)
            moves["r2"](k).start()

        @pl.when(k == 0)
        def _():
            keep[...] = term

        return carry

    lax.fori_loop(0, 4, feed, 0)

    second_in = mid[...] + collected(1) + vfull[5:6, :]
    normed, rate = normalize(second_in)
    lo_ref[...] = (normed * vfull[6:7, :] + vfull[7:8, :]).astype(jnp.bfloat16)
    d_second, gain_sum, shift_sum = normalize_back(
        ct_ref[...].astype(jnp.float32), normed, rate, vfull[6:7, :]
    )
    dtok[...] = d_second
    d2g[0] = d_second.astype(jnp.bfloat16)
    start("d2")
    apart[0:2, :] = jnp.zeros((2, width), jnp.float32)
    apart[5:6, :] = jnp.sum(d_second, axis=0, keepdims=True)
    apart[6:7, :] = gain_sum
    apart[7:8, :] = shift_sum
    bpart[8:16, :] = jnp.zeros((8, width), jnp.float32)

    def feed_back(k, carry):
        @pl.when(k > 0)
        def _():
            moves["d2"](k).wait_recv()

        low = d2g[k]
        d_act = jnp.concatenate([nt(low, flat(sbuf[zz])) for zz in range(PLANES)], axis=1)
        d_pre = d_act * slope[k]
        bpart[8:9, :] += jnp.sum(d_pre, axis=0, keepdims=True)
        d_pre_low = d_pre.astype(jnp.bfloat16)
        dpre[k] = d_pre_low
        term = jnp.concatenate([nt(d_pre_low, flat(ebuf[zz])) for zz in range(PLANES)], axis=1)

        @pl.when(k > 0)
        def _():
            rsend[2, k - 1] = term.astype(jnp.bfloat16)
            moves["r3"](k).start()

        @pl.when(k == 0)
        def _():
            keep[...] = term

        return carry

    lax.fori_loop(0, 4, feed_back, 0)

    def weigh(left, right, own, out, lead):
        for zz in range(PLANES):
            term = tn(flat(left(zz)), right)
            term = term.reshape(lead + (2, term.shape[0] // (2 * (lead + (1,))[0]), -1))
            first, second = (term[:, 0], term[:, 1]) if lead else (term[0], term[1])
            own[zz] = jnp.where(core == 0, first, second)
            out[zz] = jnp.where(core == 0, second, first).astype(jnp.bfloat16)

    def across(own, came, zout, name):
        for k in (1, 2, 3):
            zz = plane_at(k)
            zout[k - 1] = (own[zz] + came[zz].astype(jnp.float32)).astype(jnp.bfloat16)
            moves[name](k).start()

    def gathered_sum(own, came, zin, name):
        total = own[plane] + came[plane].astype(jnp.float32)
        for k in (1, 2, 3):
            moves[name](k).wait_recv()
            total = total + zin[k - 1].astype(jnp.float32)
        return total

    weigh(
        lambda zz: act[:, :, zz * part : (zz + 1) * part], flat(d2g[...]), gs_own, gs_out, ()
    )
    start("gss")
    weigh(
        lambda zz: mg[:, :, zz * part : (zz + 1) * part],
        flat(dpre[...]),
        ge_own,
        ge_out,
        (CHIPS,),
    )
    start("ges")
    arrive("gss")
    across(gs_own, gs_in, gs_zout, "gsz")
    arrive("ges")
    across(ge_own, ge_in, ge_zout, "gez")

    d_mid = dtok[...] + collected(2)
    d_first, gain_sum, shift_sum = normalize_back(
        d_mid, norm1[...], rate1[:, 0:1], vfull[3:4, :]
    )
    dtok[...] = d_first
    d1g[0] = d_first.astype(jnp.bfloat16)
    start("d1")
    apart[2:3, :] = jnp.sum(d_first, axis=0, keepdims=True)
    apart[3:4, :] = gain_sum
    apart[4:5, :] = shift_sum
    start("a")
    bpart[0:8, :] = jnp.zeros((8, width), jnp.float32)

    def attend_back(k, carry):
        @pl.when(k > 0)
        def _():
            moves["d1"](k).wait_recv()

        d_context = nt(d1g[k], flat(obuf[...])).astype(jnp.bfloat16)
        query, keys, values = (qkv[k, :, i * part : (i + 1) * part] for i in range(3))
        d_query, d_keys, d_values = [], [], []
        for h in heads:
            cols = slice(h * head, (h + 1) * head)
            probs = pbuf[k, h]
            d_values.append(tn(probs.astype(jnp.bfloat16), d_context[:, cols]))
            d_probs = nt(d_context[:, cols], values[:, cols])
            inner = jnp.sum(probs * d_probs, axis=-1, keepdims=True)
            d_scores = (probs * (d_probs - inner)).astype(jnp.bfloat16)
            d_query.append(factor * nn(d_scores, keys[:, cols]))
            d_keys.append(tn(d_scores, query[:, cols]))
        d_query = jnp.concatenate(d_query, axis=1)
        d_values = jnp.concatenate(d_values, axis=1)
        bpart[0:1, :part] += jnp.sum(d_query, axis=0, keepdims=True)
        bpart[1:2, :part] += jnp.sum(d_values, axis=0, keepdims=True)
        low = jnp.concatenate([d_query] + d_keys + [d_values], axis=1).astype(jnp.bfloat16)
        dproj[k] = low
        term = jnp.concatenate([nt(low, flat(tbuf[zz])) for zz in range(PLANES)], axis=1)

        @pl.when(k > 0)
        def _():
            rsend[3, k - 1] = term.astype(jnp.bfloat16)
            moves["r4"](k).start()

        @pl.when(k == 0)
        def _():
            keep[...] = term

        return carry

    lax.fori_loop(0, 4, attend_back, 0)

    weigh(
        lambda zz: xg[:, :, zz * part : (zz + 1) * part],
        flat(dproj[...]),
        gt_own,
        gt_out,
        (CHIPS,),
    )
    start("gts")
    d_first_all = flat(d1g[...])
    for zz in range(PLANES):
        pair = flat(ctx[...])[:, zz * head : (zz + 1) * head]
        term = tn(pair, d_first_all)
        first, second = term[: head // 2], term[head // 2 :]
        go_own[zz] = jnp.where(core == 0, first, second)
        go_out[zz] = jnp.where(core == 0, second, first).astype(jnp.bfloat16)
    start("gos")
    total = apart[...]
    for k in (1, 2, 3):
        moves["a"](k).wait_recv()
        total = total + ain[k - 1]
    bpart[0:8, :] += total
    start("bz")
    arrive("gts")
    across(gt_own, gt_in, gt_zout, "gtz")
    arrive("gos")
    across(go_own, go_in, go_zout, "goz")

    ig_ref[...] = (dtok[...] + collected(3)).astype(jnp.bfloat16)
    sg_ref[...] = gathered_sum(gs_own, gs_in, gs_zin, "gsz")

    def hand_out(total, pout, pin, name):
        low = total.astype(jnp.bfloat16)
        pout[...] = low
        pin[chip] = pout[chip]
        start(name)

    hand_out(gathered_sum(ge_own, ge_in, ge_zin, "gez"), ge_pout, ge_pin, "gep")
    total = bpart[...]
    for k in (1, 2, 3):
        moves["bz"](k).wait_recv()
        total = total + bin_[k - 1]
    bsum[...] = total
    start("bs")
    hand_out(gathered_sum(gt_own, gt_in, gt_zin, "gtz"), gt_pout, gt_pin, "gtp")
    og_ref[...] = gathered_sum(go_own, go_in, go_zin, "goz")
    arrive("bs")
    bsum_all = bsum.at[...]

    def own_lanes(rows, block, at):
        cols = pl.ds(pl.multiple_of(block * 128, 128), 128)
        wide = bsum_all[rows, cols] + bsib[rows, cols]
        out = jnp.zeros((wide.shape[0], 32), jnp.float32)
        for i in range(4):
            out = out + jnp.where(at == i, wide[:, 32 * i : 32 * i + 32], 0.0)
        return out

    by_rows = own_lanes(slice(0, 8), plane * 2 + chip // 2, by_row)
    by_heads = own_lanes(slice(0, 8), plane // 2, by_head)
    rows = lax.broadcasted_iota(jnp.int32, (8, 32), 0)
    small_ref[...] = jnp.where(rows < 2, by_heads, by_rows)
    cols = pl.ds(pl.multiple_of((plane * 2 + core) * 128, 128), 128)
    ebg_ref[...] = bsum[8:9, cols] + bsib[8:9, cols]
    arrive("gep")
    for other in range(CHIPS):
        for zz in range(PLANES):
            at = (zz * CHIPS + other) * part
            eg_ref[:, at : at + part] = ge_pin[
                other, :, zz * part : (zz + 1) * part
            ].astype(jnp.float32)
    arrive("gtp")
    for kind in range(3):
        for zz in range(PLANES):
            at = kind * width + zz * part
            tg_ref[:, at : at + part] = jnp.concatenate(
                [
                    gt_pin[other, :, kind * part + zz * piece :][:, :piece]
                    for other in range(CHIPS)
                ],
                axis=1,
            ).astype(jnp.float32)
    for name in COPIES:
        for k in span(name):
            moves[name](k).wait_send()


def plane_body(
    inputs,
    live_keys,
    triple_weight,
    query_bias,
    value_bias,
    output_weight,
    output_bias,
    first_gain,
    first_shift,
    expand_weight,
    expand_bias,
    shrink_weight,
    shrink_bias,
    second_gain,
    second_shift,
    cotangent,
):
    rows, width = inputs.shape
    own = triple_weight.shape[0]
    part = width // PLANES
    hidden = expand_weight.shape[1] // CHIPS
    low, full = jnp.bfloat16, jnp.float32
    vectors = (
        query_bias,
        value_bias,
        output_bias,
        first_gain,
        first_shift,
        shrink_bias,
        second_gain,
        second_shift,
    )
    at = lax.broadcasted_iota(jnp.int32, (8, own), 0)
    vec = jnp.zeros((8, own), full)
    for i, vector in enumerate(vectors):
        vec = jnp.where(at == i, vector.astype(full)[None, :], vec)
    shrink = shrink_weight.shape[0]
    outs = (
        ((rows, width), low),
        ((rows, width), low),
        (triple_weight.shape, full),
        (output_weight.shape, full),
        (expand_weight.shape, full),
        (shrink_weight.shape, full),
        ((8, own), full),
        ((1, 128), full),
    )
    P4, C4 = PLANES, CHIPS
    scratch = [
        ((P4, C4, 2, 16, 128), full),
        ((16, width), full),
        ((16, part), full),
        ((8, hidden), full),
        ((C4, own, 3 * part), low),
        ((P4, C4, 2, own, 3 * part), low),
        ((C4, own, hidden), low),
        ((P4, C4, 2, own, hidden), low),
        ((P4, 2, own, width), low),
        ((P4, 2, shrink, width), low),
        ((C4, rows, width), low),
        ((C4, rows, width), low),
        ((C4, rows, width), low),
        ((C4, rows, width), low),
        ((4, 3, rows, width), low),
        ((4, 3, rows, width), low),
        ((rows, width), full),
        ((C4, rows, 3 * part), low),
        ((C4, P4, rows, rows), full),
        ((C4, rows, part), low),
        ((C4, rows, hidden), full),
        ((C4, rows, hidden), low),
        ((C4, rows, hidden), low),
        ((C4, rows, 3 * part), low),
        ((rows, width), full),
        ((rows, 128), full),
        ((rows, width), full),
        ((rows, width), full),
        ((P4, shrink, width), full),
        ((P4, shrink, width), low),
        ((P4, shrink, width), low),
        ((3, shrink, width), low),
        ((3, shrink, width), low),
        ((P4, C4, own, hidden), full),
        ((P4, C4, own, hidden), low),
        ((P4, C4, own, hidden), low),
        ((3, C4, own, hidden), low),
        ((3, C4, own, hidden), low),
        ((C4, own, hidden), low),
        ((C4, own, hidden), low),
        ((P4, own, width), full),
        ((P4, own, width), low),
        ((P4, own, width), low),
        ((3, own, width), low),
        ((3, own, width), low),
        ((P4, C4, own, 3 * part), full),
        ((P4, C4, own, 3 * part), low),
        ((P4, C4, own, 3 * part), low),
        ((3, C4, own, 3 * part), low),
        ((3, C4, own, 3 * part), low),
        ((C4, own, 3 * part), low),
        ((C4, own, 3 * part), low),
        ((8, width), full),
        ((3, 8, width), full),
        ((16, width), full),
        ((3, 16, width), full),
        ((16, width), full),
        ((16, width), full),
    ]
    result = pl.pallas_call(
        plane_kernel,
        out_shape=[jax.ShapeDtypeStruct(*item) for item in outs],
        in_specs=[pl.BlockSpec(memory_space=pltpu.VMEM)] * 9,
        out_specs=[pl.BlockSpec(memory_space=pltpu.VMEM)] * len(outs),
        scratch_shapes=[pltpu.VMEM(*item) for item in scratch]
        + [pltpu.SemaphoreType.DMA((COPY_COUNT,))] * 2,
        compiler_params=pltpu.CompilerParams(
            collective_id=0, has_side_effects=True, vmem_limit_bytes=60 * 2**20
        ),
        cost_estimate=pl.CostEstimate(
            flops=6 * rows * width * 12 * width,
            bytes_accessed=16 * 2**20,
            transcendentals=rows * hidden * 8,
        ),
        name="plane_layer",
    )(
        inputs,
        live_keys.astype(full)[None, :],
        triple_weight,
        vec,
        expand_bias.astype(full)[None, :],
        output_weight,
        expand_weight,
        shrink_weight,
        cotangent,
    )
    layer_out, input_grad, triple_grad, output_grad, expand_grad, shrink_grad = result[:6]
    small, expand_bias_grad = result[6:]
    return (
        layer_out,
        input_grad,
        triple_grad,
        small[0],
        small[1],
        output_grad,
        small[2],
        small[3],
        small[4],
        expand_grad,
        expand_bias_grad[0],
        shrink_grad,
        small[5],
        small[6],
        small[7],
    )


def solution(mesh):
    placed = (
        P("fsdp", None),
        P("fsdp"),
        P("fsdp", None),
        P("fsdp"),
        P("fsdp"),
        P("fsdp", None),
        P("fsdp"),
        P("fsdp"),
        P("fsdp"),
        P("fsdp", None),
        P("fsdp"),
        P("fsdp", None),
        P("fsdp"),
        P("fsdp"),
        P("fsdp"),
        P("fsdp", None),
    )
    return jax.shard_map(
        plane_body if mesh.shape["fsdp"] == PLANES * GROUP else body,
        mesh=mesh,
        in_specs=placed,
        out_specs=(
            P("fsdp", None),
            P("fsdp", None),
            P("fsdp", None),
            P("fsdp"),
            P("fsdp"),
            P("fsdp", None),
            P("fsdp"),
            P("fsdp"),
            P("fsdp"),
            P("fsdp", None),
            P("fsdp"),
            P("fsdp", None),
            P("fsdp"),
            P("fsdp"),
            P("fsdp"),
        ),
        check_vma=False,
    )
```

```python
import jax
import jax.numpy as jnp
from jax import lax
from jax.experimental import pallas as pl
from jax.experimental.pallas import tpu as pltpu
from jax.sharding import PartitionSpec as P

HEADS = 16


EPSILON = 1e-05
NEGATIVE = -1e30
ROOT_HALF = 0.7071067811865476
INV_ROOT_TWO_PI = 0.3989422804014327


def batched(form, left, right):
    return jnp.einsum(form, left, right, preferred_element_type=jnp.float32)


def layer_norm(hidden, gain, shift):
    center = hidden - jnp.mean(hidden, axis=-1, keepdims=True)
    inv_std = lax.rsqrt(jnp.mean(center * center, axis=-1, keepdims=True) + EPSILON)
    normed = center * inv_std
    return (normed * gain.astype(jnp.float32) + shift.astype(jnp.float32), normed, inv_std)


def layer_norm_back(upstream, normed, inv_std, gain):
    scaled = upstream * gain.astype(jnp.float32)
    inner = (
        scaled
        - jnp.mean(scaled, axis=-1, keepdims=True)
        - normed * jnp.mean(scaled * normed, axis=-1, keepdims=True)
    )
    return (inv_std * inner, jnp.sum(upstream * normed, axis=0), jnp.sum(upstream, axis=0))


def normal_cdf(values):
    return 0.5 * (1.0 + lax.erf(values * ROOT_HALF))


def masked_scores(query, keys, live):
    scores = batched("qhd,khd->hqk", query, keys)
    allowed = live == 1
    return jnp.where(allowed[None, None, :], scores, NEGATIVE)


def forward(params, tokens, live):
    (
        triple_weight,
        query_bias,
        value_bias,
        output_weight,
        output_bias,
        first_gain,
        first_shift,
        expand_weight,
        expand_bias,
        shrink_weight,
        shrink_bias,
        second_gain,
        second_shift,
    ) = params
    row_count = tokens.shape[0]
    width_all = tokens.shape[1]
    head_size = width_all // HEADS
    factor = head_size ** (-0.5)
    projected = jnp.dot(tokens, triple_weight, preferred_element_type=jnp.float32)
    query = ((projected[:, :width_all] + query_bias.astype(jnp.float32)) * factor).astype(
        jnp.bfloat16
    )
    keys = projected[:, width_all : 2 * width_all].astype(jnp.bfloat16)
    values = (projected[:, 2 * width_all :] + value_bias.astype(jnp.float32)).astype(jnp.bfloat16)
    query = query.reshape(row_count, HEADS, head_size)
    keys = keys.reshape(row_count, HEADS, head_size)
    values = values.reshape(row_count, HEADS, head_size)
    scores = masked_scores(query, keys, live)
    top = jnp.max(scores, axis=-1, keepdims=True)
    expo = jnp.exp(scores - top)
    total = jnp.sum(expo, axis=-1, keepdims=True)
    log_total = top + jnp.log(total)
    probs = (expo / total).astype(jnp.bfloat16)
    context = (
        batched("hqk,khd->qhd", probs, values).astype(jnp.bfloat16).reshape(row_count, width_all)
    )
    first_in = (
        tokens.astype(jnp.float32)
        + jnp.dot(context, output_weight, preferred_element_type=jnp.float32)
        + output_bias.astype(jnp.float32)
    )
    middle, first_norm, first_rate = layer_norm(first_in, first_gain, first_shift)
    mid_low = middle.astype(jnp.bfloat16)
    pre_act = jnp.dot(
        mid_low, expand_weight, preferred_element_type=jnp.float32
    ) + expand_bias.astype(jnp.float32)
    act_low = (pre_act * normal_cdf(pre_act)).astype(jnp.bfloat16)
    second_in = (
        middle
        + jnp.dot(act_low, shrink_weight, preferred_element_type=jnp.float32)
        + shrink_bias.astype(jnp.float32)
    )
    result, second_norm, second_rate = layer_norm(second_in, second_gain, second_shift)
    saved = (
        tokens,
        live,
        query,
        keys,
        values,
        log_total,
        context,
        first_norm,
        first_rate,
        mid_low,
        pre_act,
        act_low,
        second_norm,
        second_rate,
    )
    return (result.astype(jnp.bfloat16), saved)


def back_upper(params, saved, upstream):
    (
        triple_weight,
        query_bias,
        value_bias,
        output_weight,
        output_bias,
        first_gain,
        first_shift,
        expand_weight,
        expand_bias,
        shrink_weight,
        shrink_bias,
        second_gain,
        second_shift,
    ) = params
    (
        tokens,
        live,
        query,
        keys,
        values,
        log_total,
        context,
        first_norm,
        first_rate,
        mid_low,
        pre_act,
        act_low,
        second_norm,
        second_rate,
    ) = saved
    d_second, second_gain_grad, second_shift_grad = layer_norm_back(
        upstream.astype(jnp.float32), second_norm, second_rate, second_gain
    )
    d_second_low = d_second.astype(jnp.bfloat16)
    shrink_bias_grad = jnp.sum(d_second, axis=0)
    d_act = jnp.dot(d_second_low, shrink_weight.T, preferred_element_type=jnp.float32)
    slope = normal_cdf(pre_act) + pre_act * jnp.exp(-0.5 * pre_act * pre_act) * INV_ROOT_TWO_PI
    d_pre = d_act * slope
    expand_bias_grad = jnp.sum(d_pre, axis=0)
    d_pre_low = d_pre.astype(jnp.bfloat16)
    d_mid = d_second + jnp.dot(d_pre_low, expand_weight.T, preferred_element_type=jnp.float32)
    d_first, first_gain_grad, first_shift_grad = layer_norm_back(
        d_mid, first_norm, first_rate, first_gain
    )
    small = (
        first_gain_grad,
        first_shift_grad,
        expand_bias_grad,
        shrink_bias_grad,
        second_gain_grad,
        second_shift_grad,
    )
    pairs = ((mid_low, d_pre_low), (act_low, d_second_low))
    return (small, pairs, d_first)


def back_lower(params, saved, d_first):
    (
        triple_weight,
        query_bias,
        value_bias,
        output_weight,
        output_bias,
        first_gain,
        first_shift,
        expand_weight,
        expand_bias,
        shrink_weight,
        shrink_bias,
        second_gain,
        second_shift,
    ) = params
    (
        tokens,
        live,
        query,
        keys,
        values,
        log_total,
        context,
        first_norm,
        first_rate,
        mid_low,
        pre_act,
        act_low,
        second_norm,
        second_rate,
    ) = saved
    row_count = tokens.shape[0]
    width_all = tokens.shape[1]
    head_size = width_all // HEADS
    factor = head_size ** (-0.5)
    d_first_low = d_first.astype(jnp.bfloat16)
    output_bias_grad = jnp.sum(d_first, axis=0)
    d_context = jnp.dot(d_first_low, output_weight.T, preferred_element_type=jnp.float32).astype(
        jnp.bfloat16
    )
    d_context = d_context.reshape(row_count, HEADS, head_size)
    scores = masked_scores(query, keys, live)
    probs = jnp.exp(scores - log_total)
    probs_low = probs.astype(jnp.bfloat16)
    d_values = batched("hqk,qhd->khd", probs_low, d_context)
    d_probs = batched("qhd,khd->hqk", d_context, values)
    inner = jnp.sum(probs * d_probs, axis=-1, keepdims=True)
    d_scores = (probs * (d_probs - inner)).astype(jnp.bfloat16)
    d_query = factor * batched("hqk,khd->qhd", d_scores, keys)
    d_keys = batched("hqk,qhd->khd", d_scores, query)
    d_query = d_query.reshape(row_count, width_all)
    d_keys = d_keys.reshape(row_count, width_all)
    d_values = d_values.reshape(row_count, width_all)
    d_proj = jnp.concatenate([d_query, d_keys, d_values], axis=1).astype(jnp.bfloat16)
    query_bias_grad = jnp.sum(d_query, axis=0)
    value_bias_grad = jnp.sum(d_values, axis=0)
    input_grad = (
        d_first + jnp.dot(d_proj, triple_weight.T, preferred_element_type=jnp.float32)
    ).astype(jnp.bfloat16)
    small = (query_bias_grad, value_bias_grad, output_bias_grad)
    pairs = ((tokens, d_proj), (context, d_first_low))
    return (small, pairs, input_grad)


def swap(value, bit, count):
    return lax.ppermute(value, "fsdp", [(i, i ^ (1 << bit)) for i in range(count)])


def own_bit(bit):
    return (lax.axis_index("fsdp") >> bit) & 1


def place(base, value, places, levels):
    starts = [0] * base.ndim
    for bit, at in places:
        starts[levels - 1 - bit] = at
    return lax.dynamic_update_slice(base, value, starts)


def grown(value, bits, levels):
    shape = list(value.shape)
    for bit in bits:
        shape[levels - 1 - bit] = 2
    return jnp.zeros(shape, value.dtype)


def join(own, other, bit, levels):
    mine = own_bit(bit)
    base = place(grown(own, (bit,), levels), own, ((bit, mine),), levels)
    return place(base, other, ((bit, 1 - mine),), levels)


def orders(levels):
    ring = list(range(1, levels))
    return [ring[k * len(ring) // 3 :] + ring[: k * len(ring) // 3] for k in range(3)]


def collect(shard, order, count):
    levels = count.bit_length() - 1
    held = shard.reshape((1,) * levels + shard.shape)
    steps = list(reversed(order))
    for bit in steps[:-1]:
        held = join(held, swap(held, bit, count), bit, levels)
    bit = steps[-1]
    across = swap(held, bit, count)
    beside = swap(held, 0, count)
    corner = swap(across, 0, count)
    mine, core = own_bit(bit), own_bit(0)
    full = grown(held, (bit, 0), levels)
    full = place(full, held, ((bit, mine), (0, core)), levels)
    full = place(full, beside, ((bit, mine), (0, 1 - core)), levels)
    full = place(full, across, ((bit, 1 - mine), (0, core)), levels)
    held = place(full, corner, ((bit, 1 - mine), (0, 1 - core)), levels)
    return held.reshape((count * shard.shape[0],) + shard.shape[1:])


def halve(terms, order, count, last):
    levels = count.bit_length() - 1
    for bit in order:
        axis = terms.ndim - 3 - bit if last else terms.ndim - 2 - bit
        mine = own_bit(bit)
        keep = lax.dynamic_slice_in_dim(terms, mine, 1, axis)
        send = lax.dynamic_slice_in_dim(terms, 1 - mine, 1, axis)
        total = keep.astype(jnp.float32) + swap(send, bit, count).astype(jnp.float32)
        terms = total if bit == order[-1] else total.astype(terms.dtype)
    return terms.reshape(terms.shape[-2:])


def by_core(left, count):
    parts = left.reshape(left.shape[0], count // 2, 2, left.shape[1] // count)
    core = own_bit(0)
    pick = lambda at: lax.dynamic_index_in_dim(parts, at, 2, keepdims=False).reshape(
        left.shape[0], left.shape[1] // 2
    )
    return (pick(core), pick(1 - core))


def pair_up(left, right, count):
    mine, other = by_core(left, count)
    return (
        jnp.concatenate([mine, swap(other, 0, count)], axis=0),
        jnp.concatenate([right, swap(right, 0, count)], axis=0),
    )


def summed_grad(left, right, pieces, count):
    levels = count.bit_length() - 1
    results = []
    offset = 0
    for extent, order in pieces:
        term = jnp.einsum(
            "tk,tw->kw",
            left,
            right[:, offset : offset + extent],
            preferred_element_type=jnp.float32,
        ).astype(jnp.bfloat16)
        term = term.reshape((2,) * (levels - 1) + (left.shape[1] * 2 // count, extent))
        results.append(halve(term, order, count, False))
        offset = offset + extent
    return results[0] if len(results) == 1 else jnp.concatenate(results, axis=1)


def body(
    inputs,
    live_keys,
    triple_weight,
    query_bias,
    value_bias,
    output_weight,
    output_bias,
    first_gain,
    first_shift,
    expand_weight,
    expand_bias,
    shrink_weight,
    shrink_bias,
    second_gain,
    second_shift,
    cotangent,
):
    count = lax.axis_size("fsdp")
    levels = count.bit_length() - 1
    width = inputs.shape[1]
    ways = orders(levels)
    vectors = (
        query_bias,
        value_bias,
        output_bias,
        first_gain,
        first_shift,
        expand_bias,
        shrink_bias,
        second_gain,
        second_shift,
    )
    packed = collect(jnp.concatenate(vectors)[None, :], ways[0], count)
    wide = []
    offset = 0
    for vector in vectors:
        wide.append(packed[:, offset : offset + vector.shape[0]].reshape(-1))
        offset = offset + vector.shape[0]
    gathered = (
        collect(triple_weight, ways[2], count),
        wide[0],
        wide[1],
        collect(output_weight, ways[0], count),
        wide[2],
        wide[3],
        wide[4],
        collect(expand_weight, ways[0], count),
        wide[5],
        collect(shrink_weight, ways[1], count),
        wide[6],
        wide[7],
        wide[8],
    )
    layer_out, saved = forward(gathered, inputs, live_keys)
    upper_small, upper_pairs, d_first = back_upper(gathered, saved, cotangent)
    lower_small, lower_pairs, input_grad = back_lower(gathered, saved, d_first)
    hidden = expand_weight.shape[1]
    shrink_grad = summed_grad(
        *pair_up(*upper_pairs[1], count),
        ((width * 3 // 4, ways[1]), (width // 4, ways[2])),
        count,
    )
    expand_grad = summed_grad(
        *pair_up(*upper_pairs[0], count),
        ((hidden * 3 // 4, ways[0]), (hidden // 4, ways[2])),
        count,
    )
    output_grad = summed_grad(*pair_up(*lower_pairs[1], count), ((width, ways[1]),), count)
    triple_grad = summed_grad(
        *pair_up(*lower_pairs[0], count),
        ((width, ways[0]), (width, ways[1]), (width, ways[2])),
        count,
    )
    sums = lower_small + upper_small
    terms = jnp.concatenate([item.reshape(count, -1) for item in sums], axis=1)
    terms = terms.reshape((2,) * levels + (1, terms.shape[1]))
    owned = halve(terms, list(range(levels)), count, True)[0]
    small = []
    offset = 0
    for item in sums:
        extent = item.shape[0] // count
        small.append(owned[offset : offset + extent])
        offset = offset + extent
    return (
        layer_out,
        input_grad,
        triple_grad,
        small[0],
        small[1],
        output_grad,
        small[2],
        small[3],
        small[4],
        expand_grad,
        small[5],
        shrink_grad,
        small[6],
        small[7],
        small[8],
    )


PLANES = 4
CHIPS = 4
GROUP = 2 * CHIPS
MESH = pl.DeviceIdType.MESH


def nn(left, right):
    return lax.dot_general(
        left, right, (((1,), (0,)), ((), ())), preferred_element_type=jnp.float32
    )


def nt(left, right):
    return lax.dot_general(
        left, right, (((1,), (1,)), ((), ())), preferred_element_type=jnp.float32
    )


def tn(left, right):
    return lax.dot_general(
        left, right, (((0,), (0,)), ((), ())), preferred_element_type=jnp.float32
    )


def share(plane, chip):
    return chip % 2 + 2 * (plane % 2) + 4 * (chip // 2) + 8 * (plane // 2)


def flat(value):
    return value.reshape((-1, value.shape[-1]))


def normalize(hidden):
    center = hidden - jnp.mean(hidden, axis=-1, keepdims=True)
    rate = lax.rsqrt(jnp.mean(center * center, axis=-1, keepdims=True) + EPSILON)
    return center * rate, rate


def normalize_back(upstream, normed, rate, gain):
    scaled = upstream * gain
    inner = (
        scaled
        - jnp.mean(scaled, axis=-1, keepdims=True)
        - normed * jnp.mean(scaled * normed, axis=-1, keepdims=True)
    )
    return (
        rate * inner,
        jnp.sum(upstream * normed, axis=0, keepdims=True),
        jnp.sum(upstream, axis=0, keepdims=True),
    )


COPIES = {}
COPY_COUNT = 0
for _names, _ks in (
    (("v", "vz", "t", "tz", "tw", "e", "ez", "oz", "sz", "x"), (1, 2, 3)),
    (("r1", "r2", "r3", "r4", "gsz", "gez", "goz", "gtz", "gep", "gtp", "a", "bz"), (1, 2, 3)),
    (("m", "d2", "d1"), (1, 2, 3, 4)),
    (("ts", "es", "os", "ss"), (0, 1, 2, 3)),
    (("vs", "gss", "ges", "gos", "gts", "bs"), (0,)),
):
    for _name in _names:
        COPIES[_name] = (COPY_COUNT - _ks[0], _ks)
        COPY_COUNT += len(_ks)


def plane_kernel(
    x_hbm, live_hbm, t_hbm, o_hbm, e_hbm, s_hbm, ct_hbm,
    vec0, vec1, vec2, vec3, vec4, vec5, vec6, vec7, eb_hbm,
    lo_hbm, ig_hbm, tg_hbm, og_hbm, eg_hbm, sg_hbm, small_ref, ebg_ref,
    t_ref, e_ref, ct_ref, live_ref, low0, low1, low2, low3, low4, low5, low6, low7, eb_ref,
    lo_ref, ig_ref, tg_ref, og_ref, eg_ref, sg_ref, vbuf, vfull, vchip, vhid, tsend, tbuf, esend, ebuf, obuf, sbuf, xg, mg, d2g, d1g,
    rsend, rrecv, keep, qkv, pbuf, ctx, slope, act, dpre, dproj, norm1, rate1, mid, dtok,
    gs_own, gs_out, gs_in, gs_zout, gs_zin,
    ge_own, ge_out, ge_in, ge_zout, ge_zin, ge_pout, ge_pin,
    go_own, go_out, go_in, go_zout, go_zin,
    gt_own, gt_out, gt_in, gt_zout, gt_zin, gt_pout, gt_pin,
    apart, ain, bpart, bin_, bsum, bsib, send_sem, recv_sem, load_sem, store_sem,
):
    me = lax.axis_index("fsdp")
    core = lax.rem(me, 2)
    chip = lax.rem(me // 2, 2) + 2 * lax.rem(me // 8, 2)
    plane = lax.rem(me // 4, 2) + 2 * (me // 16)
    sibling = me + 1 - 2 * core

    def flip(base, k):
        return lax.rem(base + k, 2) + 2 * lax.rem(base // 2 + k // 2, 2)

    def chip_at(k):
        return flip(chip, k)

    def plane_at(k):
        return flip(plane, k)

    def device_of(plane, chip, core):
        high = 16 * (plane // 2) + 8 * (chip // 2)
        return high + 4 * lax.rem(plane, 2) + 2 * lax.rem(chip, 2) + core

    def mate(k):
        return device_of(plane, chip_at(k), core)

    def above(k):
        return device_of(plane_at(k), chip, core)

    def rows_of(plane, chip):
        return plane // 2, chip // 2, lax.rem(plane, 2), lax.rem(chip, 2), core

    def plane_rows(plane, half=slice(None)):
        return plane // 2, half, lax.rem(plane, 2), slice(None), core

    def origin(k):
        return plane_at(2) if k == 3 else plane

    def onward(k):
        return above(1) if k == 3 else above(k)

    def copy(name, k, source, target, device):
        spot = COPIES[name][0] + k
        return pltpu.make_async_remote_copy(
            src_ref=source,
            dst_ref=target,
            send_sem=send_sem.at[spot],
            recv_sem=recv_sem.at[spot],
            device_id=(device,),
            device_id_type=MESH,
        )

    def shared(name, k, own, held):
        if k < 3:
            return copy(name, k, own, held.at[k], mate(k))
        half = own.shape[0] // 2
        rows = slice((k - 3) * half, (k - 2) * half)
        return copy(name, k, held.at[k - 2, rows], held.at[3, rows], mate(5 - k))

    moves = {
        "v": lambda k: copy(
            "v", k, vbuf.at[plane, chip, core], vbuf.at[plane, chip, core], mate(k)
        ),
        "vz": lambda k: copy(
            "vz", k, vbuf.at[plane, :, core], vbuf.at[plane, :, core], above(k)
        ),
        "vs": lambda k: copy("vs", 0, vbuf.at[:, :, core], vbuf.at[:, :, core], sibling),
        "t": lambda k: copy(
            "t", k, tsend.at[chip_at(k)], tbuf.at[*rows_of(plane, chip)], mate(k)
        ),
        "tz": lambda k: copy(
            "tz",
            k,
            tbuf.at[*plane_rows(origin(k), 0)],
            tbuf.at[*plane_rows(origin(k), 0)],
            onward(k),
        ),
        "ts": lambda k: copy(
            "ts",
            k,
            tbuf.at[*plane_rows(plane_at(k))],
            tbuf.at[*plane_rows(plane_at(k))],
            sibling,
        ),
        "e": lambda k: copy(
            "e", k, esend.at[chip_at(k)], ebuf.at[*rows_of(plane, chip)], mate(k)
        ),
        "ez": lambda k: copy(
            "ez",
            k,
            ebuf.at[*plane_rows(origin(k))],
            ebuf.at[*plane_rows(origin(k))],
            onward(k),
        ),
        "es": lambda k: copy(
            "es",
            k,
            ebuf.at[*plane_rows(plane_at(k))],
            ebuf.at[*plane_rows(plane_at(k))],
            sibling,
        ),
        "oz": lambda k: copy(
            "oz", k, obuf.at[origin(k), core], obuf.at[origin(k), core], onward(k)
        ),
        "os": lambda k: copy(
            "os", k, obuf.at[plane_at(k), core], obuf.at[plane_at(k), core], sibling
        ),
        "sz": lambda k: copy(
            "sz", k, sbuf.at[origin(k), core], sbuf.at[origin(k), core], onward(k)
        ),
        "ss": lambda k: copy(
            "ss", k, sbuf.at[plane_at(k), core], sbuf.at[plane_at(k), core], sibling
        ),
        "tw": lambda k: copy(
            "tw",
            k,
            tbuf.at[*plane_rows(origin(k), 1)],
            tbuf.at[*plane_rows(origin(k), 1)],
            onward(k),
        ),
        "x": lambda k: copy(
            "x", k, xg.at[2 if k == 3 else 0], xg.at[k], mate(1 if k == 3 else k)
        ),
        "m": lambda k: shared("m", k, mg.at[0], mg),
        "d2": lambda k: shared("d2", k, d2g.at[0], d2g),
        "d1": lambda k: shared("d1", k, d1g.at[0], d1g),
        "gss": lambda k: copy("gss", 0, gs_out, gs_in, sibling),
        "ges": lambda k: copy("ges", 0, ge_out, ge_in, sibling),
        "gos": lambda k: copy("gos", 0, go_out, go_in, sibling),
        "gts": lambda k: copy("gts", 0, gt_out, gt_in, sibling),
        "gsz": lambda k: copy("gsz", k, gs_zout.at[k - 1], gs_zin.at[k - 1], onward(k)),
        "gez": lambda k: copy("gez", k, ge_zout.at[k - 1], ge_zin.at[k - 1], onward(k)),
        "goz": lambda k: copy("goz", k, go_zout.at[k - 1], go_zin.at[k - 1], onward(k)),
        "gtz": lambda k: copy("gtz", k, gt_zout.at[k - 1], gt_zin.at[k - 1], onward(k)),
        "gep": lambda k: copy("gep", k, ge_pout.at[chip_at(k)], ge_pin.at[chip], mate(k)),
        "gtp": lambda k: copy("gtp", k, gt_pout.at[chip_at(k)], gt_pin.at[chip], mate(k)),
        "a": lambda k: copy("a", k, apart, ain.at[k - 1], mate(k)),
        "bz": lambda k: copy("bz", k, bpart, bin_.at[k - 1], above(k)),
        "bs": lambda k: copy("bs", 0, bsum, bsib, sibling),
    }
    for turn in range(4):
        name = "r%d" % (turn + 1)
        moves[name] = lambda k, name=name, turn=turn: copy(
            name, k, rsend.at[turn, k - 1], rrecv.at[turn, k - 1], mate(k)
        )
    moves["r1"] = lambda k: copy(
        "r1", k, rsend.at[0, k - 1], rrecv.at[0, k - 1], mate(1 if k == 3 else k)
    )

    def span(name):
        return COPIES[name][1]

    def start(name):
        for k in span(name):
            moves[name](k).start()

    def arrive(name):
        for k in span(name):
            moves[name](k).wait_recv()

    def send_out(name):
        moves[name](2).start()
        moves[name](1).start()

    def pass_on(name, beside):
        moves[name](2).wait_recv()
        moves[name](3).start()
        moves[beside](2).start()

    def take_in(name, beside):
        for k in (1, 3):
            moves[name](k).wait_recv()
            moves[beside](k).start()

    def take(name, k):
        @pl.when(k == 1)
        def _():
            moves[name](1).wait_recv()
            moves[name](3).start()

        @pl.when(k == 2)
        def _():
            moves[name](2).wait_recv()
            moves[name](4).start()

        @pl.when(k == 3)
        def _():
            moves[name](3).wait_recv()
            moves[name](4).wait_recv()

    def offer(name):
        moves[name](1).start()
        moves[name](2).start()

    barrier = pltpu.get_barrier_semaphore()
    for k in range(1, 4):
        for device in (mate(k), above(k)):
            pl.semaphore_signal(barrier, inc=1, device_id=(device,), device_id_type=MESH)
    pl.semaphore_signal(barrier, inc=1, device_id=(sibling,), device_id_type=MESH)

    sources = (
        t_hbm, vec0, vec1, vec2, vec3, vec4, vec5, vec6, vec7, eb_hbm, live_hbm,
        e_hbm, x_hbm, o_hbm, s_hbm, ct_hbm,
    )
    targets = (
        t_ref, low0, low1, low2, low3, low4, low5, low6, low7, eb_ref, live_ref,
        e_ref, xg.at[0], obuf.at[plane, core], sbuf.at[plane, core], ct_ref,
    )
    loads = [
        pltpu.make_async_copy(source, target, load_sem.at[i])
        for i, (source, target) in enumerate(zip(sources, targets))
    ]
    for load in loads:
        load.start()
    pairs = (
        (lo_ref, lo_hbm), (ig_ref, ig_hbm), (tg_ref, tg_hbm), (og_ref, og_hbm),
        (eg_ref, eg_hbm), (sg_ref, sg_hbm),
    )
    stores = [
        pltpu.make_async_copy(source, target, store_sem.at[i])
        for i, (source, target) in enumerate(pairs)
    ]

    for load in loads[:11]:
        load.wait()
    row = lax.broadcasted_iota(jnp.int32, (8, 32), 0)
    vec = jnp.zeros((8, 32), jnp.float32)
    for i, item in enumerate((low0, low1, low2, low3, low4, low5, low6, low7)):
        vec = jnp.where(row == i, item[...].astype(jnp.float32), vec)
    lane = lax.broadcasted_iota(jnp.int32, (8, 128), 1) // 32
    row = lax.broadcasted_iota(jnp.int32, (8, 128), 0)
    by_row = lax.rem(chip, 2) * 2 + core
    by_head = lax.rem(plane, 2) * 2 + core
    spread = jnp.concatenate([vec, vec, vec, vec], axis=1)
    spread = jnp.where(lane == jnp.where(row < 2, by_head, by_row), spread, 0.0)
    own_rows = vbuf.at[plane, chip, core]
    own_rows[0:8, :] = spread
    own_rows[8:9, :] = eb_ref[...].astype(jnp.float32)
    own_rows[9:10, :] = live_ref[...].astype(jnp.float32)
    own_rows[10:16, :] = jnp.zeros((6, 128), jnp.float32)
    width = x_hbm.shape[1]
    part = width // PLANES
    piece = part // CHIPS
    for other in range(CHIPS):
        tsend[other] = jnp.concatenate(
            [
                t_ref[:, kind * width + share(zz, other) * piece :][:, :piece]
                for kind in range(3)
                for zz in range(PLANES)
            ],
            axis=1,
        )
    loads[11].wait()
    for other in range(CHIPS):
        for zz in range(PLANES):
            esend[other, :, zz * part : (zz + 1) * part] = e_ref[
                :, share(zz, other) * part : (share(zz, other) + 1) * part
            ]
    tbuf[rows_of(plane, chip)] = tsend[chip]
    ebuf[rows_of(plane, chip)] = esend[chip]
    for load in loads[12:15]:
        load.wait()
    pl.semaphore_wait(barrier, 7)

    start("t")
    start("v")
    offer("x")
    start("e")
    send_out("oz")
    moves["os"](0).start()
    moves["ss"](0).start()
    arrive("t")
    send_out("tz")
    send_out("tw")
    moves["ts"](0).start()
    arrive("v")
    start("vz")
    pass_on("oz", "os")
    moves["x"](2).wait_recv()
    moves["x"](3).start()
    moves["tz"](2).wait_recv()
    moves["tz"](3).start()
    moves["tw"](2).wait_recv()
    moves["tw"](3).start()
    moves["ts"](2).start()
    arrive("e")
    moves["ez"](2).start()
    moves["es"](0).start()
    take_in("oz", "os")
    arrive("vz")
    start("vs")
    for k in (1, 3):
        moves["tz"](k).wait_recv()
        moves["tw"](k).wait_recv()
        moves["ts"](k).start()
    moves["ez"](1).start()
    moves["sz"](2).start()
    arrive("vs")
    for block in range(8):
        total = None
        for i in range(4):
            near = block % 2 + 2 * (block // 4)
            term = vbuf[near, i // 2 + 2 * (block // 2 % 2), i % 2]
            total = term if total is None else total + term
        vfull[:, 128 * block : 128 * block + 128] = total
        vhid[:, 128 * block : 128 * block + 128] = vbuf[block // 2, chip, block % 2][8:16]
    for half in range(2):
        vchip[:, 128 * half : 128 * half + 128] = (
            vbuf[2 * half, chip, 0]
            + vbuf[2 * half, chip, 1]
            + vbuf[2 * half + 1, chip, 0]
            + vbuf[2 * half + 1, chip, 1]
        )
    arrive("os")
    arrive("ts")

    head = width // HEADS
    factor = head ** (-0.5)
    heads = range(PLANES)

    moves["x"](1).wait_recv()
    moves["x"](3).wait_recv()

    def attend(step, carry):
        k = 3 - step
        tokens = xg[k]
        proj = nn(tokens[:, :part], flat(tbuf[0, 0]))
        for zz in range(1, PLANES):
            proj = proj + nn(tokens[:, zz * part : (zz + 1) * part], flat(tbuf[zz // 2, zz % 2]))
        query = ((proj[:, :part] + vchip[0:1, :]) * factor).astype(jnp.bfloat16)
        keys = proj[:, part : 2 * part].astype(jnp.bfloat16)
        values = (proj[:, 2 * part :] + vchip[1:2, :]).astype(jnp.bfloat16)
        qkv[k, :, :part] = query
        qkv[k, :, part : 2 * part] = keys
        qkv[k, :, 2 * part :] = values
        live = vbuf[plane, chip_at(k), core][9:10, :] > 0.5
        joined = []
        for h in heads:
            cols = slice(h * head, (h + 1) * head)
            scores = jnp.where(live, nt(query[:, cols], keys[:, cols]), NEGATIVE)
            expo = jnp.exp(scores - jnp.max(scores, axis=-1, keepdims=True))
            probs = expo / jnp.sum(expo, axis=-1, keepdims=True)
            pbuf[k, h] = probs
            joined.append(nn(probs.astype(jnp.bfloat16), values[:, cols]))
        context = jnp.concatenate(joined, axis=1).astype(jnp.bfloat16)
        ctx[k] = context
        term = nn(context, flat(obuf[...]))

        @pl.when(k == 0)
        def _():
            keep[...] = term

        @pl.when(k == 1)
        def _():
            rsend[0, 0] = term.astype(jnp.bfloat16)
            moves["r1"](1).start()

        @pl.when(k == 2)
        def _():
            mid[...] = term

        @pl.when(k == 3)
        def _():
            rsend[0, 2] = term.astype(jnp.bfloat16)
            moves["r1"](3).start()

        return carry

    lax.fori_loop(0, 4, attend, 0)
    moves["r1"](3).wait_recv()
    rsend[0, 1] = (mid[...] + rrecv[0, 2].astype(jnp.float32)).astype(jnp.bfloat16)
    moves["r1"](2).start()
    pass_on("ez", "es")
    moves["sz"](1).start()
    pass_on("sz", "ss")

    def collected(turn):
        total = keep[...]
        for k in (1, 2, 3) if turn else (1, 2):
            moves["r%d" % (turn + 1)](k).wait_recv()
            total = total + rrecv[turn, k - 1].astype(jnp.float32)
        return total

    first_in = xg[0].astype(jnp.float32) + collected(0) + vfull[2:3, :]
    normed, rate = normalize(first_in)
    norm1[...] = normed
    rate1[...] = jnp.broadcast_to(rate, rate1.shape)
    middle = normed * vfull[3:4, :] + vfull[4:5, :]
    mid[...] = middle
    mg[0] = middle.astype(jnp.bfloat16)
    offer("m")

    take_in("ez", "es")
    arrive("es")

    def feed(k, carry):
        take("m", k)

        low = mg[k]
        pre = vhid[0:1, :] + nn(low[:, :part], flat(ebuf[0, 0]))
        for zz in range(1, PLANES):
            pre = pre + nn(low[:, zz * part : (zz + 1) * part], flat(ebuf[zz // 2, zz % 2]))
        cdf = normal_cdf(pre)
        slope[k] = cdf + pre * jnp.exp(-0.5 * pre * pre) * INV_ROOT_TWO_PI
        active = (pre * cdf).astype(jnp.bfloat16)
        act[k] = active

        @pl.when(k == 0)
        def _():
            take_in("sz", "ss")
            arrive("ss")

        term = nn(active[:, :part], flat(sbuf[0]))
        for zz in range(1, PLANES):
            term = term + nn(active[:, zz * part : (zz + 1) * part], flat(sbuf[zz]))

        @pl.when(k > 0)
        def _():
            rsend[1, k - 1] = term.astype(jnp.bfloat16)
            moves["r2"](k).start()

        @pl.when(k == 0)
        def _():
            keep[...] = term

        return carry

    lax.fori_loop(0, 4, feed, 0)

    second_in = mid[...] + collected(1) + vfull[5:6, :]
    normed, rate = normalize(second_in)
    lo_ref[...] = (normed * vfull[6:7, :] + vfull[7:8, :]).astype(jnp.bfloat16)
    stores[0].start()
    loads[15].wait()
    d_second, gain_sum, shift_sum = normalize_back(
        ct_ref[...].astype(jnp.float32), normed, rate, vfull[6:7, :]
    )
    dtok[...] = d_second
    d2g[0] = d_second.astype(jnp.bfloat16)
    offer("d2")
    apart[0:2, :] = jnp.zeros((2, width), jnp.float32)
    apart[5:6, :] = jnp.sum(d_second, axis=0, keepdims=True)
    apart[6:7, :] = gain_sum
    apart[7:8, :] = shift_sum
    bpart[8:16, :] = jnp.zeros((8, width), jnp.float32)

    def feed_back(k, carry):
        take("d2", k)

        low = d2g[k]
        d_act = jnp.concatenate([nt(low, flat(sbuf[zz])) for zz in range(PLANES)], axis=1)
        d_pre = d_act * slope[k]
        bpart[8:9, :] += jnp.sum(d_pre, axis=0, keepdims=True)
        d_pre_low = d_pre.astype(jnp.bfloat16)
        dpre[k] = d_pre_low
        term = jnp.concatenate([nt(d_pre_low, flat(ebuf[zz // 2, zz % 2])) for zz in range(PLANES)], axis=1)

        @pl.when(k > 0)
        def _():
            rsend[2, k - 1] = term.astype(jnp.bfloat16)
            moves["r3"](k).start()

        @pl.when(k == 0)
        def _():
            keep[...] = term

        return carry

    lax.fori_loop(0, 4, feed_back, 0)

    def mine(term, axis):
        first, second = lax.index_in_dim(term, 0, axis, False), lax.index_in_dim(term, 1, axis, False)
        return (
            jnp.where(core == 0, first, second),
            jnp.where(core == 0, second, first).astype(jnp.bfloat16),
        )

    def weigh_hidden(left, right, own, out):
        for zz in range(PLANES):
            term = tn(flat(left[:, :, zz * part : (zz + 1) * part]), right)
            own[zz], out[zz] = mine(term.reshape(2, -1, term.shape[-1]), 0)

    def weigh_width(left, right, own, out):
        for zz in range(PLANES):
            term = tn(flat(left[:, :, zz * part : (zz + 1) * part]), right)
            held, given = mine(term.reshape(2, 2, 2, -1, term.shape[-1]), 2)
            for y in range(2):
                spot = y + 2 * (zz // 2), slice(2 * (zz % 2), 2 * (zz % 2) + 2)
                own[spot], out[spot] = held[y], given[y]

    def across(own, came, zout, name, k):
        total = own[plane_at(k)] + came[plane_at(k)].astype(jnp.float32)
        zout[k - 1] = total.astype(jnp.bfloat16)
        moves[name](k).start()

    def across_far(own, came, zout, zin, name):
        moves[name](3).wait_recv()
        zz = plane_at(2)
        total = own[zz] + came[zz].astype(jnp.float32) + zin[2].astype(jnp.float32)
        zout[1] = total.astype(jnp.bfloat16)
        moves[name](2).start()

    def gathered_sum(own, came, zin, name):
        total = own[plane] + came[plane].astype(jnp.float32)
        for k in (1, 2):
            moves[name](k).wait_recv()
            total = total + zin[k - 1].astype(jnp.float32)
        return total

    weigh_hidden(act, flat(d2g[...]), gs_own, gs_out)
    start("gss")
    weigh_width(mg, flat(dpre[...]), ge_own, ge_out)
    start("ges")
    arrive("gss")
    across(gs_own, gs_in, gs_zout, "gsz", 3)
    arrive("ges")
    across(ge_own, ge_in, ge_zout, "gez", 3)

    d_mid = dtok[...] + collected(2)
    d_first, gain_sum, shift_sum = normalize_back(
        d_mid, norm1[...], rate1[:, 0:1], vfull[3:4, :]
    )
    dtok[...] = d_first
    d1g[0] = d_first.astype(jnp.bfloat16)
    offer("d1")
    apart[2:3, :] = jnp.sum(d_first, axis=0, keepdims=True)
    apart[3:4, :] = gain_sum
    apart[4:5, :] = shift_sum
    start("a")
    bpart[0:8, :] = jnp.zeros((8, width), jnp.float32)

    def attend_back(k, carry):
        take("d1", k)

        d_context = nt(d1g[k], flat(obuf[...])).astype(jnp.bfloat16)
        query, keys, values = (qkv[k, :, i * part : (i + 1) * part] for i in range(3))
        d_query, d_keys, d_values = [], [], []
        for h in heads:
            cols = slice(h * head, (h + 1) * head)
            probs = pbuf[k, h]
            d_values.append(tn(probs.astype(jnp.bfloat16), d_context[:, cols]))
            d_probs = nt(d_context[:, cols], values[:, cols])
            inner = jnp.sum(probs * d_probs, axis=-1, keepdims=True)
            d_scores = (probs * (d_probs - inner)).astype(jnp.bfloat16)
            d_query.append(factor * nn(d_scores, keys[:, cols]))
            d_keys.append(tn(d_scores, query[:, cols]))
        d_query = jnp.concatenate(d_query, axis=1)
        d_values = jnp.concatenate(d_values, axis=1)
        bpart[0:1, :part] += jnp.sum(d_query, axis=0, keepdims=True)
        bpart[1:2, :part] += jnp.sum(d_values, axis=0, keepdims=True)
        low = jnp.concatenate([d_query] + d_keys + [d_values], axis=1).astype(jnp.bfloat16)
        dproj[k] = low
        term = jnp.concatenate([nt(low, flat(tbuf[zz // 2, zz % 2])) for zz in range(PLANES)], axis=1)

        @pl.when(k > 0)
        def _():
            rsend[3, k - 1] = term.astype(jnp.bfloat16)
            moves["r4"](k).start()

        @pl.when(k == 0)
        def _():
            keep[...] = term
            across_far(gs_own, gs_in, gs_zout, gs_zin, "gsz")
            across(gs_own, gs_in, gs_zout, "gsz", 1)

        @pl.when(k == 1)
        def _():
            across_far(ge_own, ge_in, ge_zout, ge_zin, "gez")
            across(ge_own, ge_in, ge_zout, "gez", 1)

        return carry

    lax.fori_loop(0, 4, attend_back, 0)

    weigh_width(xg, flat(dproj[...]), gt_own, gt_out)
    start("gts")
    d_first_all = flat(d1g[...])
    for zz in range(PLANES):
        pair = flat(ctx[...])[:, zz * head : (zz + 1) * head]
        term = tn(pair, d_first_all)
        first, second = term[: head // 2], term[head // 2 :]
        go_own[zz] = jnp.where(core == 0, first, second)
        go_out[zz] = jnp.where(core == 0, second, first).astype(jnp.bfloat16)
    start("gos")
    total = apart[...]
    for k in (1, 2, 3):
        moves["a"](k).wait_recv()
        total = total + ain[k - 1]
    bpart[0:8, :] += total
    start("bz")
    arrive("gts")
    across(gt_own, gt_in, gt_zout, "gtz", 3)
    arrive("gos")
    across(go_own, go_in, go_zout, "goz", 3)
    across_far(gt_own, gt_in, gt_zout, gt_zin, "gtz")
    across(gt_own, gt_in, gt_zout, "gtz", 1)
    across(go_own, go_in, go_zout, "goz", 1)
    across_far(go_own, go_in, go_zout, go_zin, "goz")

    ig_ref[...] = (dtok[...] + collected(3)).astype(jnp.bfloat16)
    stores[1].start()
    sg_ref[...] = gathered_sum(gs_own, gs_in, gs_zin, "gsz")
    stores[5].start()

    def hand_out(total, pout, pin, name):
        low = total.astype(jnp.bfloat16)
        pout[...] = low
        pin[chip] = pout[chip]
        start(name)

    hand_out(gathered_sum(ge_own, ge_in, ge_zin, "gez"), ge_pout, ge_pin, "gep")
    total = bpart[...]
    for k in (1, 2, 3):
        moves["bz"](k).wait_recv()
        total = total + bin_[k - 1]
    bsum[...] = total
    start("bs")
    hand_out(gathered_sum(gt_own, gt_in, gt_zin, "gtz"), gt_pout, gt_pin, "gtp")
    og_ref[...] = gathered_sum(go_own, go_in, go_zin, "goz")
    stores[3].start()
    arrive("bs")
    bsum_all = bsum.at[...]

    def own_lanes(rows, block, at):
        cols = pl.ds(pl.multiple_of(block * 128, 128), 128)
        wide = bsum_all[rows, cols] + bsib[rows, cols]
        out = jnp.zeros((wide.shape[0], 32), jnp.float32)
        for i in range(4):
            out = out + jnp.where(at == i, wide[:, 32 * i : 32 * i + 32], 0.0)
        return out

    by_rows = own_lanes(
        slice(0, 8), lax.rem(plane, 2) + 2 * (chip // 2) + 4 * (plane // 2), by_row
    )
    by_heads = own_lanes(slice(0, 8), plane // 2, by_head)
    rows = lax.broadcasted_iota(jnp.int32, (8, 32), 0)
    small_ref[...] = jnp.where(rows < 2, by_heads, by_rows)
    cols = pl.ds(pl.multiple_of((plane * 2 + core) * 128, 128), 128)
    ebg_ref[...] = bsum[8:9, cols] + bsib[8:9, cols]
    arrive("gep")
    for other in range(CHIPS):
        for zz in range(PLANES):
            at = share(zz, other) * part
            eg_ref[:, at : at + part] = ge_pin[
                other, :, zz * part : (zz + 1) * part
            ].astype(jnp.float32)
    stores[4].start()
    arrive("gtp")
    holder = {share(zz, other): (zz, other) for zz in range(PLANES) for other in range(CHIPS)}
    for kind in range(3):
        for first in range(0, HEADS, 2):
            at = kind * width + first * piece
            tg_ref[:, at : at + 2 * piece] = jnp.concatenate(
                [
                    gt_pin[other, :, kind * part + zz * piece :][:, :piece]
                    for zz, other in (holder[first], holder[first + 1])
                ],
                axis=1,
            ).astype(jnp.float32)
    stores[2].start()
    for name in COPIES:
        for k in span(name):
            moves[name](k).wait_send()
    for store in stores:
        store.wait()


def hand_over(*refs):
    small_ref, ebg_ref = refs[6:8]
    outs = refs[8:-1]
    moved = [
        pltpu.make_async_copy(refs[i], outs[i], refs[-1].at[i]) for i in range(6)
    ]
    for item in moved:
        item.start()
    for i in range(8):
        outs[6 + i][...] = small_ref[i : i + 1, :]
    outs[14][...] = ebg_ref[...]
    for item in moved:
        item.wait()


def plane_body(
    inputs,
    live_keys,
    triple_weight,
    query_bias,
    value_bias,
    output_weight,
    output_bias,
    first_gain,
    first_shift,
    expand_weight,
    expand_bias,
    shrink_weight,
    shrink_bias,
    second_gain,
    second_shift,
    cotangent,
):
    rows, width = inputs.shape
    own = triple_weight.shape[0]
    part = width // PLANES
    hidden = expand_weight.shape[1] // CHIPS
    low, full = jnp.bfloat16, jnp.float32
    vectors = (
        query_bias,
        value_bias,
        output_bias,
        first_gain,
        first_shift,
        shrink_bias,
        second_gain,
        second_shift,
    )
    shrink = shrink_weight.shape[0]
    outs = (
        ((rows, width), low),
        ((rows, width), low),
        (triple_weight.shape, full),
        (output_weight.shape, full),
        (expand_weight.shape, full),
        (shrink_weight.shape, full),
        ((8, own), full),
        ((1, 128), full),
    )
    P4, C4 = PLANES, CHIPS
    scratch = [
        (triple_weight.shape, low),
        (expand_weight.shape, low),
        ((rows, width), low),
        ((1, rows), jnp.int32),
    ]
    scratch += [((1, own), low)] * 8 + [((1, shrink), low)] + list(outs[:6])
    scratch += [
        ((P4, C4, 2, 16, 128), full),
        ((16, width), full),
        ((16, part), full),
        ((8, hidden), full),
        ((C4, own, 3 * part), low),
        ((2, 2, 2, 2, 2, own, 3 * part), low),
        ((C4, own, hidden), low),
        ((2, 2, 2, 2, 2, own, hidden), low),
        ((P4, 2, own, width), low),
        ((P4, 2, shrink, width), low),
        ((C4, rows, width), low),
        ((C4, rows, width), low),
        ((C4, rows, width), low),
        ((C4, rows, width), low),
        ((4, 3, rows, width), low),
        ((4, 3, rows, width), low),
        ((rows, width), full),
        ((C4, rows, 3 * part), low),
        ((C4, P4, rows, rows), full),
        ((C4, rows, part), low),
        ((C4, rows, hidden), full),
        ((C4, rows, hidden), low),
        ((C4, rows, hidden), low),
        ((C4, rows, 3 * part), low),
        ((rows, width), full),
        ((rows, 128), full),
        ((rows, width), full),
        ((rows, width), full),
        ((P4, shrink, width), full),
        ((P4, shrink, width), low),
        ((P4, shrink, width), low),
        ((3, shrink, width), low),
        ((3, shrink, width), low),
        ((P4, C4, own, hidden), full),
        ((P4, C4, own, hidden), low),
        ((P4, C4, own, hidden), low),
        ((3, C4, own, hidden), low),
        ((3, C4, own, hidden), low),
        ((C4, own, hidden), low),
        ((C4, own, hidden), low),
        ((P4, own, width), full),
        ((P4, own, width), low),
        ((P4, own, width), low),
        ((3, own, width), low),
        ((3, own, width), low),
        ((P4, C4, own, 3 * part), full),
        ((P4, C4, own, 3 * part), low),
        ((P4, C4, own, 3 * part), low),
        ((3, C4, own, 3 * part), low),
        ((3, C4, own, 3 * part), low),
        ((C4, own, 3 * part), low),
        ((C4, own, 3 * part), low),
        ((8, width), full),
        ((3, 8, width), full),
        ((16, width), full),
        ((3, 16, width), full),
        ((16, width), full),
        ((16, width), full),
    ]
    anywhere = pl.BlockSpec(memory_space=pl.ANY)
    inside = pl.BlockSpec(memory_space=pltpu.VMEM)
    given = (
        inputs,
        live_keys[None, :],
        triple_weight,
        output_weight,
        expand_weight,
        shrink_weight,
        cotangent,
    )
    given += tuple(vector[None, :] for vector in vectors) + (expand_bias[None, :],)
    result = pl.pallas_call(
        plane_kernel,
        out_shape=[jax.ShapeDtypeStruct(*item) for item in outs],
        in_specs=[anywhere] * len(given),
        out_specs=[anywhere] * 6 + [inside] * 2,
        scratch_shapes=[pltpu.VMEM(*item) for item in scratch]
        + [pltpu.SemaphoreType.DMA((COPY_COUNT,))] * 2
        + [pltpu.SemaphoreType.DMA((16,)), pltpu.SemaphoreType.DMA((6,))],
        compiler_params=pltpu.CompilerParams(
            collective_id=0, has_side_effects=True, vmem_limit_bytes=60 * 2**20
        ),
        cost_estimate=pl.CostEstimate(
            flops=6 * rows * width * 12 * width,
            bytes_accessed=16 * 2**20,
            transcendentals=rows * hidden * 8,
        ),
        name="plane_layer",
    )(*given)
    ends = list(outs[:6]) + [((1, own), full)] * 8 + [((1, shrink), full)]
    done = pl.pallas_call(
        hand_over,
        out_shape=[jax.ShapeDtypeStruct(*item) for item in ends],
        in_specs=[inside] * 8,
        out_specs=[anywhere] * 6 + [inside] * 9,
        scratch_shapes=[pltpu.SemaphoreType.DMA((6,))],
        name="hand_over",
    )(*result)
    layer_out, input_grad, triple_grad, output_grad, expand_grad, shrink_grad = done[:6]
    small = [item[0] for item in done[6:]]
    return (
        layer_out,
        input_grad,
        triple_grad,
        small[0],
        small[1],
        output_grad,
        small[2],
        small[3],
        small[4],
        expand_grad,
        small[8],
        shrink_grad,
        small[5],
        small[6],
        small[7],
    )


def solution(mesh):
    placed = (
        P("fsdp", None),
        P("fsdp"),
        P("fsdp", None),
        P("fsdp"),
        P("fsdp"),
        P("fsdp", None),
        P("fsdp"),
        P("fsdp"),
        P("fsdp"),
        P("fsdp", None),
        P("fsdp"),
        P("fsdp", None),
        P("fsdp"),
        P("fsdp"),
        P("fsdp"),
        P("fsdp", None),
    )
    return jax.shard_map(
        plane_body if mesh.shape["fsdp"] == PLANES * GROUP else body,
        mesh=mesh,
        in_specs=placed,
        out_specs=(
            P("fsdp", None),
            P("fsdp", None),
            P("fsdp", None),
            P("fsdp"),
            P("fsdp"),
            P("fsdp", None),
            P("fsdp"),
            P("fsdp"),
            P("fsdp"),
            P("fsdp", None),
            P("fsdp"),
            P("fsdp", None),
            P("fsdp"),
            P("fsdp"),
            P("fsdp"),
        ),
        check_vma=False,
    )
```

```python
import jax
import jax.numpy as jnp
from jax import lax
from jax.experimental import pallas as pl
from jax.experimental.pallas import tpu as pltpu
from jax.sharding import PartitionSpec as P

HEADS = 16


EPSILON = 1e-05
NEGATIVE = -1e30
ROOT_HALF = 0.7071067811865476
INV_ROOT_TWO_PI = 0.3989422804014327


def batched(form, left, right):
    return jnp.einsum(form, left, right, preferred_element_type=jnp.float32)


def layer_norm(hidden, gain, shift):
    center = hidden - jnp.mean(hidden, axis=-1, keepdims=True)
    inv_std = lax.rsqrt(jnp.mean(center * center, axis=-1, keepdims=True) + EPSILON)
    normed = center * inv_std
    return (normed * gain.astype(jnp.float32) + shift.astype(jnp.float32), normed, inv_std)


def layer_norm_back(upstream, normed, inv_std, gain):
    scaled = upstream * gain.astype(jnp.float32)
    inner = (
        scaled
        - jnp.mean(scaled, axis=-1, keepdims=True)
        - normed * jnp.mean(scaled * normed, axis=-1, keepdims=True)
    )
    return (inv_std * inner, jnp.sum(upstream * normed, axis=0), jnp.sum(upstream, axis=0))


def normal_cdf(values):
    return 0.5 * (1.0 + lax.erf(values * ROOT_HALF))


def masked_scores(query, keys, live):
    scores = batched("qhd,khd->hqk", query, keys)
    allowed = live == 1
    return jnp.where(allowed[None, None, :], scores, NEGATIVE)


def forward(params, tokens, live):
    (
        triple_weight,
        query_bias,
        value_bias,
        output_weight,
        output_bias,
        first_gain,
        first_shift,
        expand_weight,
        expand_bias,
        shrink_weight,
        shrink_bias,
        second_gain,
        second_shift,
    ) = params
    row_count = tokens.shape[0]
    width_all = tokens.shape[1]
    head_size = width_all // HEADS
    factor = head_size ** (-0.5)
    projected = jnp.dot(tokens, triple_weight, preferred_element_type=jnp.float32)
    query = ((projected[:, :width_all] + query_bias.astype(jnp.float32)) * factor).astype(
        jnp.bfloat16
    )
    keys = projected[:, width_all : 2 * width_all].astype(jnp.bfloat16)
    values = (projected[:, 2 * width_all :] + value_bias.astype(jnp.float32)).astype(jnp.bfloat16)
    query = query.reshape(row_count, HEADS, head_size)
    keys = keys.reshape(row_count, HEADS, head_size)
    values = values.reshape(row_count, HEADS, head_size)
    scores = masked_scores(query, keys, live)
    top = jnp.max(scores, axis=-1, keepdims=True)
    expo = jnp.exp(scores - top)
    total = jnp.sum(expo, axis=-1, keepdims=True)
    log_total = top + jnp.log(total)
    probs = (expo / total).astype(jnp.bfloat16)
    context = (
        batched("hqk,khd->qhd", probs, values).astype(jnp.bfloat16).reshape(row_count, width_all)
    )
    first_in = (
        tokens.astype(jnp.float32)
        + jnp.dot(context, output_weight, preferred_element_type=jnp.float32)
        + output_bias.astype(jnp.float32)
    )
    middle, first_norm, first_rate = layer_norm(first_in, first_gain, first_shift)
    mid_low = middle.astype(jnp.bfloat16)
    pre_act = jnp.dot(
        mid_low, expand_weight, preferred_element_type=jnp.float32
    ) + expand_bias.astype(jnp.float32)
    act_low = (pre_act * normal_cdf(pre_act)).astype(jnp.bfloat16)
    second_in = (
        middle
        + jnp.dot(act_low, shrink_weight, preferred_element_type=jnp.float32)
        + shrink_bias.astype(jnp.float32)
    )
    result, second_norm, second_rate = layer_norm(second_in, second_gain, second_shift)
    saved = (
        tokens,
        live,
        query,
        keys,
        values,
        log_total,
        context,
        first_norm,
        first_rate,
        mid_low,
        pre_act,
        act_low,
        second_norm,
        second_rate,
    )
    return (result.astype(jnp.bfloat16), saved)


def back_upper(params, saved, upstream):
    (
        triple_weight,
        query_bias,
        value_bias,
        output_weight,
        output_bias,
        first_gain,
        first_shift,
        expand_weight,
        expand_bias,
        shrink_weight,
        shrink_bias,
        second_gain,
        second_shift,
    ) = params
    (
        tokens,
        live,
        query,
        keys,
        values,
        log_total,
        context,
        first_norm,
        first_rate,
        mid_low,
        pre_act,
        act_low,
        second_norm,
        second_rate,
    ) = saved
    d_second, second_gain_grad, second_shift_grad = layer_norm_back(
        upstream.astype(jnp.float32), second_norm, second_rate, second_gain
    )
    d_second_low = d_second.astype(jnp.bfloat16)
    shrink_bias_grad = jnp.sum(d_second, axis=0)
    d_act = jnp.dot(d_second_low, shrink_weight.T, preferred_element_type=jnp.float32)
    slope = normal_cdf(pre_act) + pre_act * jnp.exp(-0.5 * pre_act * pre_act) * INV_ROOT_TWO_PI
    d_pre = d_act * slope
    expand_bias_grad = jnp.sum(d_pre, axis=0)
    d_pre_low = d_pre.astype(jnp.bfloat16)
    d_mid = d_second + jnp.dot(d_pre_low, expand_weight.T, preferred_element_type=jnp.float32)
    d_first, first_gain_grad, first_shift_grad = layer_norm_back(
        d_mid, first_norm, first_rate, first_gain
    )
    small = (
        first_gain_grad,
        first_shift_grad,
        expand_bias_grad,
        shrink_bias_grad,
        second_gain_grad,
        second_shift_grad,
    )
    pairs = ((mid_low, d_pre_low), (act_low, d_second_low))
    return (small, pairs, d_first)


def back_lower(params, saved, d_first):
    (
        triple_weight,
        query_bias,
        value_bias,
        output_weight,
        output_bias,
        first_gain,
        first_shift,
        expand_weight,
        expand_bias,
        shrink_weight,
        shrink_bias,
        second_gain,
        second_shift,
    ) = params
    (
        tokens,
        live,
        query,
        keys,
        values,
        log_total,
        context,
        first_norm,
        first_rate,
        mid_low,
        pre_act,
        act_low,
        second_norm,
        second_rate,
    ) = saved
    row_count = tokens.shape[0]
    width_all = tokens.shape[1]
    head_size = width_all // HEADS
    factor = head_size ** (-0.5)
    d_first_low = d_first.astype(jnp.bfloat16)
    output_bias_grad = jnp.sum(d_first, axis=0)
    d_context = jnp.dot(d_first_low, output_weight.T, preferred_element_type=jnp.float32).astype(
        jnp.bfloat16
    )
    d_context = d_context.reshape(row_count, HEADS, head_size)
    scores = masked_scores(query, keys, live)
    probs = jnp.exp(scores - log_total)
    probs_low = probs.astype(jnp.bfloat16)
    d_values = batched("hqk,qhd->khd", probs_low, d_context)
    d_probs = batched("qhd,khd->hqk", d_context, values)
    inner = jnp.sum(probs * d_probs, axis=-1, keepdims=True)
    d_scores = (probs * (d_probs - inner)).astype(jnp.bfloat16)
    d_query = factor * batched("hqk,khd->qhd", d_scores, keys)
    d_keys = batched("hqk,qhd->khd", d_scores, query)
    d_query = d_query.reshape(row_count, width_all)
    d_keys = d_keys.reshape(row_count, width_all)
    d_values = d_values.reshape(row_count, width_all)
    d_proj = jnp.concatenate([d_query, d_keys, d_values], axis=1).astype(jnp.bfloat16)
    query_bias_grad = jnp.sum(d_query, axis=0)
    value_bias_grad = jnp.sum(d_values, axis=0)
    input_grad = (
        d_first + jnp.dot(d_proj, triple_weight.T, preferred_element_type=jnp.float32)
    ).astype(jnp.bfloat16)
    small = (query_bias_grad, value_bias_grad, output_bias_grad)
    pairs = ((tokens, d_proj), (context, d_first_low))
    return (small, pairs, input_grad)


def swap(value, bit, count):
    return lax.ppermute(value, "fsdp", [(i, i ^ (1 << bit)) for i in range(count)])


def own_bit(bit):
    return (lax.axis_index("fsdp") >> bit) & 1


def place(base, value, places, levels):
    starts = [0] * base.ndim
    for bit, at in places:
        starts[levels - 1 - bit] = at
    return lax.dynamic_update_slice(base, value, starts)


def grown(value, bits, levels):
    shape = list(value.shape)
    for bit in bits:
        shape[levels - 1 - bit] = 2
    return jnp.zeros(shape, value.dtype)


def join(own, other, bit, levels):
    mine = own_bit(bit)
    base = place(grown(own, (bit,), levels), own, ((bit, mine),), levels)
    return place(base, other, ((bit, 1 - mine),), levels)


def orders(levels):
    ring = list(range(1, levels))
    return [ring[k * len(ring) // 3 :] + ring[: k * len(ring) // 3] for k in range(3)]


def collect(shard, order, count):
    levels = count.bit_length() - 1
    held = shard.reshape((1,) * levels + shard.shape)
    steps = list(reversed(order))
    for bit in steps[:-1]:
        held = join(held, swap(held, bit, count), bit, levels)
    bit = steps[-1]
    across = swap(held, bit, count)
    beside = swap(held, 0, count)
    corner = swap(across, 0, count)
    mine, core = own_bit(bit), own_bit(0)
    full = grown(held, (bit, 0), levels)
    full = place(full, held, ((bit, mine), (0, core)), levels)
    full = place(full, beside, ((bit, mine), (0, 1 - core)), levels)
    full = place(full, across, ((bit, 1 - mine), (0, core)), levels)
    held = place(full, corner, ((bit, 1 - mine), (0, 1 - core)), levels)
    return held.reshape((count * shard.shape[0],) + shard.shape[1:])


def halve(terms, order, count, last):
    levels = count.bit_length() - 1
    for bit in order:
        axis = terms.ndim - 3 - bit if last else terms.ndim - 2 - bit
        mine = own_bit(bit)
        keep = lax.dynamic_slice_in_dim(terms, mine, 1, axis)
        send = lax.dynamic_slice_in_dim(terms, 1 - mine, 1, axis)
        total = keep.astype(jnp.float32) + swap(send, bit, count).astype(jnp.float32)
        terms = total if bit == order[-1] else total.astype(terms.dtype)
    return terms.reshape(terms.shape[-2:])


def by_core(left, count):
    parts = left.reshape(left.shape[0], count // 2, 2, left.shape[1] // count)
    core = own_bit(0)
    pick = lambda at: lax.dynamic_index_in_dim(parts, at, 2, keepdims=False).reshape(
        left.shape[0], left.shape[1] // 2
    )
    return (pick(core), pick(1 - core))


def pair_up(left, right, count):
    mine, other = by_core(left, count)
    return (
        jnp.concatenate([mine, swap(other, 0, count)], axis=0),
        jnp.concatenate([right, swap(right, 0, count)], axis=0),
    )


def summed_grad(left, right, pieces, count):
    levels = count.bit_length() - 1
    results = []
    offset = 0
    for extent, order in pieces:
        term = jnp.einsum(
            "tk,tw->kw",
            left,
            right[:, offset : offset + extent],
            preferred_element_type=jnp.float32,
        ).astype(jnp.bfloat16)
        term = term.reshape((2,) * (levels - 1) + (left.shape[1] * 2 // count, extent))
        results.append(halve(term, order, count, False))
        offset = offset + extent
    return results[0] if len(results) == 1 else jnp.concatenate(results, axis=1)


def body(
    inputs,
    live_keys,
    triple_weight,
    query_bias,
    value_bias,
    output_weight,
    output_bias,
    first_gain,
    first_shift,
    expand_weight,
    expand_bias,
    shrink_weight,
    shrink_bias,
    second_gain,
    second_shift,
    cotangent,
):
    count = lax.axis_size("fsdp")
    levels = count.bit_length() - 1
    width = inputs.shape[1]
    ways = orders(levels)
    vectors = (
        query_bias,
        value_bias,
        output_bias,
        first_gain,
        first_shift,
        expand_bias,
        shrink_bias,
        second_gain,
        second_shift,
    )
    packed = collect(jnp.concatenate(vectors)[None, :], ways[0], count)
    wide = []
    offset = 0
    for vector in vectors:
        wide.append(packed[:, offset : offset + vector.shape[0]].reshape(-1))
        offset = offset + vector.shape[0]
    gathered = (
        collect(triple_weight, ways[2], count),
        wide[0],
        wide[1],
        collect(output_weight, ways[0], count),
        wide[2],
        wide[3],
        wide[4],
        collect(expand_weight, ways[0], count),
        wide[5],
        collect(shrink_weight, ways[1], count),
        wide[6],
        wide[7],
        wide[8],
    )
    layer_out, saved = forward(gathered, inputs, live_keys)
    upper_small, upper_pairs, d_first = back_upper(gathered, saved, cotangent)
    lower_small, lower_pairs, input_grad = back_lower(gathered, saved, d_first)
    hidden = expand_weight.shape[1]
    shrink_grad = summed_grad(
        *pair_up(*upper_pairs[1], count),
        ((width * 3 // 4, ways[1]), (width // 4, ways[2])),
        count,
    )
    expand_grad = summed_grad(
        *pair_up(*upper_pairs[0], count),
        ((hidden * 3 // 4, ways[0]), (hidden // 4, ways[2])),
        count,
    )
    output_grad = summed_grad(*pair_up(*lower_pairs[1], count), ((width, ways[1]),), count)
    triple_grad = summed_grad(
        *pair_up(*lower_pairs[0], count),
        ((width, ways[0]), (width, ways[1]), (width, ways[2])),
        count,
    )
    sums = lower_small + upper_small
    terms = jnp.concatenate([item.reshape(count, -1) for item in sums], axis=1)
    terms = terms.reshape((2,) * levels + (1, terms.shape[1]))
    owned = halve(terms, list(range(levels)), count, True)[0]
    small = []
    offset = 0
    for item in sums:
        extent = item.shape[0] // count
        small.append(owned[offset : offset + extent])
        offset = offset + extent
    return (
        layer_out,
        input_grad,
        triple_grad,
        small[0],
        small[1],
        output_grad,
        small[2],
        small[3],
        small[4],
        expand_grad,
        small[5],
        shrink_grad,
        small[6],
        small[7],
        small[8],
    )


PLANES = 4
CHIPS = 4
GROUP = 2 * CHIPS
MESH = pl.DeviceIdType.MESH


def nn(left, right):
    return lax.dot_general(
        left, right, (((1,), (0,)), ((), ())), preferred_element_type=jnp.float32
    )


def nt(left, right):
    return lax.dot_general(
        left, right, (((1,), (1,)), ((), ())), preferred_element_type=jnp.float32
    )


def tn(left, right):
    return lax.dot_general(
        left, right, (((0,), (0,)), ((), ())), preferred_element_type=jnp.float32
    )


def share(plane, chip):
    return chip % 2 + 2 * (plane % 2) + 4 * (chip // 2) + 8 * (plane // 2)


def flat(value):
    return value.reshape((-1, value.shape[-1]))


def normalize(hidden):
    center = hidden - jnp.mean(hidden, axis=-1, keepdims=True)
    rate = lax.rsqrt(jnp.mean(center * center, axis=-1, keepdims=True) + EPSILON)
    return center * rate, rate


def normalize_back(upstream, normed, rate, gain):
    scaled = upstream * gain
    inner = (
        scaled
        - jnp.mean(scaled, axis=-1, keepdims=True)
        - normed * jnp.mean(scaled * normed, axis=-1, keepdims=True)
    )
    return (
        rate * inner,
        jnp.sum(upstream * normed, axis=0, keepdims=True),
        jnp.sum(upstream, axis=0, keepdims=True),
    )


COPIES = {}
COPY_COUNT = 0
for _names, _ks in (
    (("v", "vz", "t", "tz", "tw", "e", "ez", "oz", "sz", "x"), (1, 2, 3)),
    (("r1", "r2", "r3", "r4", "gsz", "gez", "goz", "gtz", "gty", "gep", "gtp", "a", "bz"), (1, 2, 3)),
    (("m", "d2", "d1"), (1, 2, 3, 4, 5, 6)),
    (("ts", "es", "os", "ss"), (0, 1, 2, 3)),
    (("gts",), (0, 1)),
    (("vs", "gss", "ges", "gos", "bs"), (0,)),
):
    for _name in _names:
        COPIES[_name] = (COPY_COUNT - _ks[0], _ks)
        COPY_COUNT += len(_ks)


def plane_kernel(
    x_hbm, live_hbm, t_hbm, o_hbm, e_hbm, s_hbm, ct_hbm,
    vec0, vec1, vec2, vec3, vec4, vec5, vec6, vec7, eb_hbm,
    lo_hbm, ig_hbm, tg_hbm, og_hbm, eg_hbm, sg_hbm, small_ref, ebg_ref,
    t_ref, e_ref, ct_ref, live_ref, low0, low1, low2, low3, low4, low5, low6, low7, eb_ref,
    lo_ref, ig_ref, tg_ref, og_ref, eg_ref, sg_ref, vbuf, vfull, vchip, vhid, tsend, tbuf, esend, ebuf, obuf, sbuf, xg, mg, d2g, d1g,
    rsend, rrecv, keep, qkv, pbuf, ctx, slope, act, dpre, dproj, norm1, rate1, mid, dtok,
    gs_own, gs_out, gs_in, gs_zout, gs_zin,
    ge_own, ge_out, ge_in, ge_zout, ge_zin, ge_pout, ge_pin,
    go_own, go_out, go_in, go_zout, go_zin,
    gt_own, gt_out, gt_in, gt_zout, gt_zin, gt_pout, gt_pin,
    apart, ain, bpart, bin_, bsum, bsib, send_sem, recv_sem, load_sem, store_sem,
):
    me = lax.axis_index("fsdp")
    core = lax.rem(me, 2)
    chip = lax.rem(me // 2, 2) + 2 * lax.rem(me // 8, 2)
    plane = lax.rem(me // 4, 2) + 2 * (me // 16)
    sibling = me + 1 - 2 * core

    def flip(base, k):
        return lax.rem(base + k, 2) + 2 * lax.rem(base // 2 + k // 2, 2)

    def chip_at(k):
        return flip(chip, k)

    def plane_at(k):
        return flip(plane, k)

    def device_of(plane, chip, core):
        high = 16 * (plane // 2) + 8 * (chip // 2)
        return high + 4 * lax.rem(plane, 2) + 2 * lax.rem(chip, 2) + core

    def mate(k):
        return device_of(plane, chip_at(k), core)

    def above(k):
        return device_of(plane_at(k), chip, core)

    def rows_of(plane, chip):
        return plane // 2, chip // 2, lax.rem(plane, 2), lax.rem(chip, 2), core

    def plane_rows(plane, half=slice(None)):
        return plane // 2, half, lax.rem(plane, 2), slice(None), core

    def origin(k):
        return plane_at(2) if k == 3 else plane

    def onward(k):
        return above(1) if k == 3 else above(k)

    def copy(name, k, source, target, device):
        spot = COPIES[name][0] + k
        return pltpu.make_async_remote_copy(
            src_ref=source,
            dst_ref=target,
            send_sem=send_sem.at[spot],
            recv_sem=recv_sem.at[spot],
            device_id=(device,),
            device_id_type=MESH,
        )

    def shared(name, k, held):
        half = held.shape[1] // 2
        first, last = slice(0, half), slice(half, 2 * half)
        rows = first if k in (1, 3, 6) else last
        if k in (3, 4):
            return copy(name, k, held.at[k - 2, rows], held.at[3, rows], mate(5 - k))
        to = 1 if k in (1, 5) else 2
        return copy(name, k, held.at[0, rows], held.at[to, rows], mate(to))

    moves = {
        "v": lambda k: copy(
            "v", k, vbuf.at[plane, chip, core], vbuf.at[plane, chip, core], mate(k)
        ),
        "vz": lambda k: copy(
            "vz", k, vbuf.at[plane, :, core], vbuf.at[plane, :, core], above(k)
        ),
        "vs": lambda k: copy("vs", 0, vbuf.at[:, :, core], vbuf.at[:, :, core], sibling),
        "t": lambda k: copy(
            "t", k, tsend.at[chip_at(k)], tbuf.at[*rows_of(plane, chip)], mate(k)
        ),
        "tz": lambda k: copy(
            "tz",
            k,
            tbuf.at[*plane_rows(origin(k), 0)],
            tbuf.at[*plane_rows(origin(k), 0)],
            onward(k),
        ),
        "ts": lambda k: copy(
            "ts",
            k,
            tbuf.at[*plane_rows(plane_at(k))],
            tbuf.at[*plane_rows(plane_at(k))],
            sibling,
        ),
        "e": lambda k: copy(
            "e", k, esend.at[chip_at(k)], ebuf.at[*rows_of(plane, chip)], mate(k)
        ),
        "ez": lambda k: copy(
            "ez",
            k,
            ebuf.at[*plane_rows(origin(k))],
            ebuf.at[*plane_rows(origin(k))],
            onward(k),
        ),
        "es": lambda k: copy(
            "es",
            k,
            ebuf.at[*plane_rows(plane_at(k))],
            ebuf.at[*plane_rows(plane_at(k))],
            sibling,
        ),
        "oz": lambda k: copy(
            "oz", k, obuf.at[origin(k), core], obuf.at[origin(k), core], onward(k)
        ),
        "os": lambda k: copy(
            "os", k, obuf.at[plane_at(k), core], obuf.at[plane_at(k), core], sibling
        ),
        "sz": lambda k: copy(
            "sz", k, sbuf.at[origin(k), core], sbuf.at[origin(k), core], onward(k)
        ),
        "ss": lambda k: copy(
            "ss", k, sbuf.at[plane_at(k), core], sbuf.at[plane_at(k), core], sibling
        ),
        "tw": lambda k: copy(
            "tw",
            k,
            tbuf.at[*plane_rows(origin(k), 1)],
            tbuf.at[*plane_rows(origin(k), 1)],
            onward(k),
        ),
        "x": lambda k: copy(
            "x", k, xg.at[2 if k == 3 else 0], xg.at[k], mate(1 if k == 3 else k)
        ),
        "m": lambda k: shared("m", k, mg),
        "d2": lambda k: shared("d2", k, d2g),
        "d1": lambda k: shared("d1", k, d1g),
        "gss": lambda k: copy("gss", 0, gs_out, gs_in, sibling),
        "ges": lambda k: copy("ges", 0, ge_out, ge_in, sibling),
        "gos": lambda k: copy("gos", 0, go_out, go_in, sibling),
        "gts": lambda k: copy(
            "gts", k, gt_out.at[:, 2 * k : 2 * k + 2], gt_in.at[:, 2 * k : 2 * k + 2], sibling
        ),
        "gsz": lambda k: copy("gsz", k, gs_zout.at[k - 1], gs_zin.at[k - 1], onward(k)),
        "gez": lambda k: copy("gez", k, ge_zout.at[k - 1], ge_zin.at[k - 1], onward(k)),
        "goz": lambda k: copy("goz", k, go_zout.at[k - 1], go_zin.at[k - 1], onward(k)),
        "gtz": lambda k: copy(
            "gtz", k, gt_zout.at[k - 1, 0:2], gt_zin.at[k - 1, 0:2], onward(k)
        ),
        "gty": lambda k: copy(
            "gty", k, gt_zout.at[k - 1, 2:4], gt_zin.at[k - 1, 2:4], onward(k)
        ),
        "gep": lambda k: copy("gep", k, ge_pout.at[chip_at(k)], ge_pin.at[chip], mate(k)),
        "gtp": lambda k: copy("gtp", k, gt_pout.at[chip_at(k)], gt_pin.at[chip], mate(k)),
        "a": lambda k: copy("a", k, apart, ain.at[k - 1], mate(k)),
        "bz": lambda k: copy("bz", k, bpart, bin_.at[k - 1], above(k)),
        "bs": lambda k: copy("bs", 0, bsum, bsib, sibling),
    }
    for turn in range(4):
        name = "r%d" % (turn + 1)
        moves[name] = lambda k, name=name, turn=turn: copy(
            name, k, rsend.at[turn, k - 1], rrecv.at[turn, k - 1], mate(k)
        )
    moves["r1"] = lambda k: copy(
        "r1", k, rsend.at[0, k - 1], rrecv.at[0, k - 1], mate(1 if k == 3 else k)
    )

    def span(name):
        return COPIES[name][1]

    def start(name):
        for k in span(name):
            moves[name](k).start()

    def arrive(name):
        for k in span(name):
            moves[name](k).wait_recv()

    def send_out(name):
        moves[name](2).start()
        moves[name](1).start()

    def pass_on(name, beside):
        moves[name](2).wait_recv()
        moves[name](3).start()
        moves[beside](2).start()

    def take_in(name, beside):
        for k in (1, 3):
            moves[name](k).wait_recv()
            moves[beside](k).start()

    def take(name, k):
        @pl.when(k == 1)
        def _():
            for i in (1, 2):
                moves[name](i).wait_recv()
                moves[name](i + 2).start()
            moves[name](5).wait_recv()

        @pl.when(k == 2)
        def _():
            moves[name](6).wait_recv()

        @pl.when(k == 3)
        def _():
            moves[name](3).wait_recv()
            moves[name](4).wait_recv()

    def offer(name):
        for k in (1, 2, 5, 6):
            moves[name](k).start()

    barrier = pltpu.get_barrier_semaphore()
    for k in range(1, 4):
        for device in (mate(k), above(k)):
            pl.semaphore_signal(barrier, inc=1, device_id=(device,), device_id_type=MESH)
    pl.semaphore_signal(barrier, inc=1, device_id=(sibling,), device_id_type=MESH)

    sources = (
        t_hbm, vec0, vec1, vec2, vec3, vec4, vec5, vec6, vec7, eb_hbm, live_hbm,
        e_hbm, x_hbm, o_hbm, s_hbm, ct_hbm,
    )
    targets = (
        t_ref, low0, low1, low2, low3, low4, low5, low6, low7, eb_ref, live_ref,
        e_ref, xg.at[0], obuf.at[plane, core], sbuf.at[plane, core], ct_ref,
    )
    loads = [
        pltpu.make_async_copy(source, target, load_sem.at[i])
        for i, (source, target) in enumerate(zip(sources, targets))
    ]
    for load in loads:
        load.start()
    pairs = (
        (lo_ref, lo_hbm), (ig_ref, ig_hbm), (tg_ref, tg_hbm), (og_ref, og_hbm),
        (eg_ref, eg_hbm), (sg_ref, sg_hbm),
    )
    stores = [
        pltpu.make_async_copy(source, target, store_sem.at[i])
        for i, (source, target) in enumerate(pairs)
    ]

    for load in loads[:11]:
        load.wait()
    row = lax.broadcasted_iota(jnp.int32, (8, 32), 0)
    vec = jnp.zeros((8, 32), jnp.float32)
    for i, item in enumerate((low0, low1, low2, low3, low4, low5, low6, low7)):
        vec = jnp.where(row == i, item[...].astype(jnp.float32), vec)
    lane = lax.broadcasted_iota(jnp.int32, (8, 128), 1) // 32
    row = lax.broadcasted_iota(jnp.int32, (8, 128), 0)
    by_row = lax.rem(chip, 2) * 2 + core
    by_head = lax.rem(plane, 2) * 2 + core
    spread = jnp.concatenate([vec, vec, vec, vec], axis=1)
    spread = jnp.where(lane == jnp.where(row < 2, by_head, by_row), spread, 0.0)
    own_rows = vbuf.at[plane, chip, core]
    own_rows[0:8, :] = spread
    own_rows[8:9, :] = eb_ref[...].astype(jnp.float32)
    own_rows[9:10, :] = live_ref[...].astype(jnp.float32)
    own_rows[10:16, :] = jnp.zeros((6, 128), jnp.float32)
    width = x_hbm.shape[1]
    part = width // PLANES
    piece = part // CHIPS
    for other in range(CHIPS):
        tsend[other] = jnp.concatenate(
            [
                t_ref[:, kind * width + share(zz, other) * piece :][:, :piece]
                for kind in range(3)
                for zz in range(PLANES)
            ],
            axis=1,
        )
    tbuf[rows_of(plane, chip)] = tsend[chip]
    for load in loads[12:15]:
        load.wait()
    pl.semaphore_wait(barrier, 7)

    start("t")
    start("v")
    loads[11].wait()
    for other in range(CHIPS):
        for zz in range(PLANES):
            esend[other, :, zz * part : (zz + 1) * part] = e_ref[
                :, share(zz, other) * part : (share(zz, other) + 1) * part
            ]
    ebuf[rows_of(plane, chip)] = esend[chip]
    moves["os"](0).start()
    moves["ss"](0).start()
    arrive("t")
    send_out("tz")
    send_out("tw")
    moves["x"](1).start()
    moves["x"](2).start()
    moves["ts"](0).start()
    start("e")
    arrive("v")
    start("vz")
    moves["tz"](2).wait_recv()
    moves["tz"](3).start()
    moves["x"](2).wait_recv()
    moves["x"](3).start()
    moves["tw"](2).wait_recv()
    moves["tw"](3).start()
    moves["ts"](2).start()
    send_out("oz")
    arrive("e")
    moves["ez"](2).start()
    moves["es"](0).start()
    arrive("vz")
    start("vs")
    for k in (1, 3):
        moves["tz"](k).wait_recv()
        moves["tw"](k).wait_recv()
        moves["ts"](k).start()
    pass_on("oz", "os")
    moves["ez"](1).start()
    moves["sz"](2).start()
    arrive("vs")
    for block in range(8):
        total = None
        for i in range(4):
            near = block % 2 + 2 * (block // 4)
            term = vbuf[near, i // 2 + 2 * (block // 2 % 2), i % 2]
            total = term if total is None else total + term
        vfull[:, 128 * block : 128 * block + 128] = total
        vhid[:, 128 * block : 128 * block + 128] = vbuf[block // 2, chip, block % 2][8:16]
    for half in range(2):
        vchip[:, 128 * half : 128 * half + 128] = (
            vbuf[2 * half, chip, 0]
            + vbuf[2 * half, chip, 1]
            + vbuf[2 * half + 1, chip, 0]
            + vbuf[2 * half + 1, chip, 1]
        )
    take_in("oz", "os")
    arrive("os")
    arrive("ts")

    head = width // HEADS
    factor = head ** (-0.5)
    heads = range(PLANES)

    moves["x"](1).wait_recv()
    moves["x"](3).wait_recv()

    def attend(step, carry):
        k = 3 - step
        tokens = xg[k]
        proj = nn(tokens[:, :part], flat(tbuf[0, 0]))
        for zz in range(1, PLANES):
            proj = proj + nn(tokens[:, zz * part : (zz + 1) * part], flat(tbuf[zz // 2, zz % 2]))
        query = ((proj[:, :part] + vchip[0:1, :]) * factor).astype(jnp.bfloat16)
        keys = proj[:, part : 2 * part].astype(jnp.bfloat16)
        values = (proj[:, 2 * part :] + vchip[1:2, :]).astype(jnp.bfloat16)
        qkv[k, :, :part] = query
        qkv[k, :, part : 2 * part] = keys
        qkv[k, :, 2 * part :] = values
        live = vbuf[plane, chip_at(k), core][9:10, :] > 0.5
        joined = []
        for h in heads:
            cols = slice(h * head, (h + 1) * head)
            scores = jnp.where(live, nt(query[:, cols], keys[:, cols]), NEGATIVE)
            expo = jnp.exp(scores - jnp.max(scores, axis=-1, keepdims=True))
            probs = expo / jnp.sum(expo, axis=-1, keepdims=True)
            pbuf[k, h] = probs
            joined.append(nn(probs.astype(jnp.bfloat16), values[:, cols]))
        context = jnp.concatenate(joined, axis=1).astype(jnp.bfloat16)
        ctx[k] = context
        term = nn(context, flat(obuf[...]))

        @pl.when(k == 0)
        def _():
            keep[...] = term

        @pl.when(k == 1)
        def _():
            rsend[0, 0] = term.astype(jnp.bfloat16)
            moves["r1"](1).start()

        @pl.when(k == 2)
        def _():
            mid[...] = term

        @pl.when(k == 3)
        def _():
            rsend[0, 2] = term.astype(jnp.bfloat16)
            moves["r1"](3).start()

        return carry

    lax.fori_loop(0, 4, attend, 0)
    moves["r1"](3).wait_recv()
    rsend[0, 1] = (mid[...] + rrecv[0, 2].astype(jnp.float32)).astype(jnp.bfloat16)
    moves["r1"](2).start()
    pass_on("ez", "es")
    moves["sz"](1).start()
    pass_on("sz", "ss")

    def collected(turn):
        total = keep[...]
        for k in (1, 2, 3) if turn else (1, 2):
            moves["r%d" % (turn + 1)](k).wait_recv()
            total = total + rrecv[turn, k - 1].astype(jnp.float32)
        return total

    first_in = xg[0].astype(jnp.float32) + collected(0) + vfull[2:3, :]
    normed, rate = normalize(first_in)
    norm1[...] = normed
    rate1[...] = jnp.broadcast_to(rate, rate1.shape)
    middle = normed * vfull[3:4, :] + vfull[4:5, :]
    mid[...] = middle
    mg[0] = middle.astype(jnp.bfloat16)
    offer("m")

    take_in("ez", "es")
    arrive("es")

    def feed(k, carry):
        take("m", k)

        low = mg[k]
        pre = vhid[0:1, :] + nn(low[:, :part], flat(ebuf[0, 0]))
        for zz in range(1, PLANES):
            pre = pre + nn(low[:, zz * part : (zz + 1) * part], flat(ebuf[zz // 2, zz % 2]))
        cdf = normal_cdf(pre)
        slope[k] = cdf + pre * jnp.exp(-0.5 * pre * pre) * INV_ROOT_TWO_PI
        active = (pre * cdf).astype(jnp.bfloat16)
        act[k] = active

        @pl.when(k == 0)
        def _():
            take_in("sz", "ss")
            arrive("ss")

        term = nn(active[:, :part], flat(sbuf[0]))
        for zz in range(1, PLANES):
            term = term + nn(active[:, zz * part : (zz + 1) * part], flat(sbuf[zz]))

        @pl.when(k > 0)
        def _():
            rsend[1, k - 1] = term.astype(jnp.bfloat16)
            moves["r2"](k).start()

        @pl.when(k == 0)
        def _():
            keep[...] = term

        return carry

    lax.fori_loop(0, 4, feed, 0)

    second_in = mid[...] + collected(1) + vfull[5:6, :]
    normed, rate = normalize(second_in)
    lo_ref[...] = (normed * vfull[6:7, :] + vfull[7:8, :]).astype(jnp.bfloat16)
    stores[0].start()
    loads[15].wait()
    d_second, gain_sum, shift_sum = normalize_back(
        ct_ref[...].astype(jnp.float32), normed, rate, vfull[6:7, :]
    )
    dtok[...] = d_second
    d2g[0] = d_second.astype(jnp.bfloat16)
    offer("d2")
    apart[0:2, :] = jnp.zeros((2, width), jnp.float32)
    apart[5:6, :] = jnp.sum(d_second, axis=0, keepdims=True)
    apart[6:7, :] = gain_sum
    apart[7:8, :] = shift_sum
    bpart[8:16, :] = jnp.zeros((8, width), jnp.float32)

    def feed_back(k, carry):
        take("d2", k)

        low = d2g[k]
        d_act = jnp.concatenate([nt(low, flat(sbuf[zz])) for zz in range(PLANES)], axis=1)
        d_pre = d_act * slope[k]
        bpart[8:9, :] += jnp.sum(d_pre, axis=0, keepdims=True)
        d_pre_low = d_pre.astype(jnp.bfloat16)
        dpre[k] = d_pre_low
        term = jnp.concatenate([nt(d_pre_low, flat(ebuf[zz // 2, zz % 2])) for zz in range(PLANES)], axis=1)

        @pl.when(k > 0)
        def _():
            rsend[2, k - 1] = term.astype(jnp.bfloat16)
            moves["r3"](k).start()

        @pl.when(k == 0)
        def _():
            keep[...] = term

        return carry

    lax.fori_loop(0, 4, feed_back, 0)

    def mine(term, axis):
        first, second = lax.index_in_dim(term, 0, axis, False), lax.index_in_dim(term, 1, axis, False)
        return (
            jnp.where(core == 0, first, second),
            jnp.where(core == 0, second, first).astype(jnp.bfloat16),
        )

    def weigh_hidden(left, right, own, out):
        for zz in range(PLANES):
            term = tn(flat(left[:, :, zz * part : (zz + 1) * part]), right)
            own[zz], out[zz] = mine(term.reshape(2, -1, term.shape[-1]), 0)

    def weigh_width(left, right, own, out, parts=range(PLANES)):
        for zz in parts:
            term = tn(flat(left[:, :, zz * part : (zz + 1) * part]), right)
            held, given = mine(term.reshape(2, 2, 2, -1, term.shape[-1]), 2)
            for y in range(2):
                spot = y + 2 * (zz // 2), slice(2 * (zz % 2), 2 * (zz % 2) + 2)
                own[spot], out[spot] = held[y], given[y]

    def across(own, came, zout, name, k, cut=slice(None)):
        zz = plane_at(k)
        total = own[zz, cut] + came[zz, cut].astype(jnp.float32)
        zout[k - 1, cut] = total.astype(jnp.bfloat16)
        moves[name](k).start()

    def across_far(own, came, zout, zin, name, cut=slice(None)):
        moves[name](3).wait_recv()
        zz = plane_at(2)
        total = own[zz, cut] + came[zz, cut].astype(jnp.float32)
        zout[1, cut] = (total + zin[2, cut].astype(jnp.float32)).astype(jnp.bfloat16)
        moves[name](2).start()

    def gathered_sum(own, came, zin, *names):
        total = own[plane] + came[plane].astype(jnp.float32)
        for k in (1, 2):
            for name in names:
                moves[name](k).wait_recv()
            total = total + zin[k - 1].astype(jnp.float32)
        return total

    weigh_hidden(act, flat(d2g[...]), gs_own, gs_out)
    start("gss")
    weigh_width(mg, flat(dpre[...]), ge_own, ge_out)
    start("ges")
    arrive("gss")
    across(gs_own, gs_in, gs_zout, "gsz", 3)
    arrive("ges")
    across(ge_own, ge_in, ge_zout, "gez", 3)

    d_mid = dtok[...] + collected(2)
    d_first, gain_sum, shift_sum = normalize_back(
        d_mid, norm1[...], rate1[:, 0:1], vfull[3:4, :]
    )
    dtok[...] = d_first
    d1g[0] = d_first.astype(jnp.bfloat16)
    offer("d1")
    apart[2:3, :] = jnp.sum(d_first, axis=0, keepdims=True)
    apart[3:4, :] = gain_sum
    apart[4:5, :] = shift_sum
    start("a")
    bpart[0:8, :] = jnp.zeros((8, width), jnp.float32)

    def attend_back(k, carry):
        take("d1", k)

        d_context = nt(d1g[k], flat(obuf[...])).astype(jnp.bfloat16)
        query, keys, values = (qkv[k, :, i * part : (i + 1) * part] for i in range(3))
        d_query, d_keys, d_values = [], [], []
        for h in heads:
            cols = slice(h * head, (h + 1) * head)
            probs = pbuf[k, h]
            d_values.append(tn(probs.astype(jnp.bfloat16), d_context[:, cols]))
            d_probs = nt(d_context[:, cols], values[:, cols])
            inner = jnp.sum(probs * d_probs, axis=-1, keepdims=True)
            d_scores = (probs * (d_probs - inner)).astype(jnp.bfloat16)
            d_query.append(factor * nn(d_scores, keys[:, cols]))
            d_keys.append(tn(d_scores, query[:, cols]))
        d_query = jnp.concatenate(d_query, axis=1)
        d_values = jnp.concatenate(d_values, axis=1)
        bpart[0:1, :part] += jnp.sum(d_query, axis=0, keepdims=True)
        bpart[1:2, :part] += jnp.sum(d_values, axis=0, keepdims=True)
        low = jnp.concatenate([d_query] + d_keys + [d_values], axis=1).astype(jnp.bfloat16)
        dproj[k] = low
        term = jnp.concatenate([nt(low, flat(tbuf[zz // 2, zz % 2])) for zz in range(PLANES)], axis=1)

        @pl.when(k > 0)
        def _():
            rsend[3, k - 1] = term.astype(jnp.bfloat16)
            moves["r4"](k).start()

        @pl.when(k == 0)
        def _():
            keep[...] = term
            across_far(gs_own, gs_in, gs_zout, gs_zin, "gsz")
            across(gs_own, gs_in, gs_zout, "gsz", 1)

        @pl.when(k == 1)
        def _():
            across_far(ge_own, ge_in, ge_zout, ge_zin, "gez")
            across(ge_own, ge_in, ge_zout, "gez", 1)

        return carry

    lax.fori_loop(0, 4, attend_back, 0)

    d_proj = flat(dproj[...])
    for half in range(2):
        weigh_width(xg, d_proj, gt_own, gt_out, (half, half + 2))
        moves["gts"](half).start()
    d_first_all = flat(d1g[...])
    for zz in range(PLANES):
        pair = flat(ctx[...])[:, zz * head : (zz + 1) * head]
        term = tn(pair, d_first_all)
        first, second = term[: head // 2], term[head // 2 :]
        go_own[zz] = jnp.where(core == 0, first, second)
        go_out[zz] = jnp.where(core == 0, second, first).astype(jnp.bfloat16)
    start("gos")
    total = apart[...]
    for k in (1, 2, 3):
        moves["a"](k).wait_recv()
        total = total + ain[k - 1]
    bpart[0:8, :] += total
    start("bz")
    halves = (("gtz", slice(0, 2)), ("gty", slice(2, 4)))
    for half, (name, cut) in enumerate(halves):
        moves["gts"](half).wait_recv()
        across(gt_own, gt_in, gt_zout, name, 3, cut)
    arrive("gos")
    across(go_own, go_in, go_zout, "goz", 3)
    for name, cut in halves:
        across_far(gt_own, gt_in, gt_zout, gt_zin, name, cut)
        across(gt_own, gt_in, gt_zout, name, 1, cut)
    across(go_own, go_in, go_zout, "goz", 1)
    across_far(go_own, go_in, go_zout, go_zin, "goz")

    ig_ref[...] = (dtok[...] + collected(3)).astype(jnp.bfloat16)
    stores[1].start()
    sg_ref[...] = gathered_sum(gs_own, gs_in, gs_zin, "gsz")
    stores[5].start()

    def hand_out(total, pout, pin, name):
        low = total.astype(jnp.bfloat16)
        pout[...] = low
        pin[chip] = pout[chip]
        start(name)

    hand_out(gathered_sum(ge_own, ge_in, ge_zin, "gez"), ge_pout, ge_pin, "gep")
    total = bpart[...]
    for k in (1, 2, 3):
        moves["bz"](k).wait_recv()
        total = total + bin_[k - 1]
    bsum[...] = total
    start("bs")
    hand_out(gathered_sum(gt_own, gt_in, gt_zin, "gtz", "gty"), gt_pout, gt_pin, "gtp")
    og_ref[...] = gathered_sum(go_own, go_in, go_zin, "goz")
    stores[3].start()
    arrive("bs")
    bsum_all = bsum.at[...]

    def own_lanes(rows, block, at):
        cols = pl.ds(pl.multiple_of(block * 128, 128), 128)
        wide = bsum_all[rows, cols] + bsib[rows, cols]
        out = jnp.zeros((wide.shape[0], 32), jnp.float32)
        for i in range(4):
            out = out + jnp.where(at == i, wide[:, 32 * i : 32 * i + 32], 0.0)
        return out

    by_rows = own_lanes(
        slice(0, 8), lax.rem(plane, 2) + 2 * (chip // 2) + 4 * (plane // 2), by_row
    )
    by_heads = own_lanes(slice(0, 8), plane // 2, by_head)
    rows = lax.broadcasted_iota(jnp.int32, (8, 32), 0)
    small_ref[...] = jnp.where(rows < 2, by_heads, by_rows)
    cols = pl.ds(pl.multiple_of((plane * 2 + core) * 128, 128), 128)
    ebg_ref[...] = bsum[8:9, cols] + bsib[8:9, cols]
    arrive("gep")
    for other in range(CHIPS):
        for zz in range(PLANES):
            at = share(zz, other) * part
            eg_ref[:, at : at + part] = ge_pin[
                other, :, zz * part : (zz + 1) * part
            ].astype(jnp.float32)
    stores[4].start()
    arrive("gtp")
    holder = {share(zz, other): (zz, other) for zz in range(PLANES) for other in range(CHIPS)}
    for kind in range(3):
        for first in range(0, HEADS, 2):
            at = kind * width + first * piece
            tg_ref[:, at : at + 2 * piece] = jnp.concatenate(
                [
                    gt_pin[other, :, kind * part + zz * piece :][:, :piece]
                    for zz, other in (holder[first], holder[first + 1])
                ],
                axis=1,
            ).astype(jnp.float32)
    stores[2].start()
    for name in COPIES:
        for k in span(name):
            moves[name](k).wait_send()
    for store in stores:
        store.wait()


def hand_over(*refs):
    small_ref, ebg_ref = refs[6:8]
    outs = refs[8:-1]
    moved = [
        pltpu.make_async_copy(refs[i], outs[i], refs[-1].at[i]) for i in range(6)
    ]
    for item in moved:
        item.start()
    for i in range(8):
        outs[6 + i][...] = small_ref[i : i + 1, :]
    outs[14][...] = ebg_ref[...]
    for item in moved:
        item.wait()


def plane_body(
    inputs,
    live_keys,
    triple_weight,
    query_bias,
    value_bias,
    output_weight,
    output_bias,
    first_gain,
    first_shift,
    expand_weight,
    expand_bias,
    shrink_weight,
    shrink_bias,
    second_gain,
    second_shift,
    cotangent,
):
    rows, width = inputs.shape
    own = triple_weight.shape[0]
    part = width // PLANES
    hidden = expand_weight.shape[1] // CHIPS
    low, full = jnp.bfloat16, jnp.float32
    vectors = (
        query_bias,
        value_bias,
        output_bias,
        first_gain,
        first_shift,
        shrink_bias,
        second_gain,
        second_shift,
    )
    shrink = shrink_weight.shape[0]
    outs = (
        ((rows, width), low),
        ((rows, width), low),
        (triple_weight.shape, full),
        (output_weight.shape, full),
        (expand_weight.shape, full),
        (shrink_weight.shape, full),
        ((8, own), full),
        ((1, 128), full),
    )
    P4, C4 = PLANES, CHIPS
    scratch = [
        (triple_weight.shape, low),
        (expand_weight.shape, low),
        ((rows, width), low),
        ((1, rows), jnp.int32),
    ]
    scratch += [((1, own), low)] * 8 + [((1, shrink), low)] + list(outs[:6])
    scratch += [
        ((P4, C4, 2, 16, 128), full),
        ((16, width), full),
        ((16, part), full),
        ((8, hidden), full),
        ((C4, own, 3 * part), low),
        ((2, 2, 2, 2, 2, own, 3 * part), low),
        ((C4, own, hidden), low),
        ((2, 2, 2, 2, 2, own, hidden), low),
        ((P4, 2, own, width), low),
        ((P4, 2, shrink, width), low),
        ((C4, rows, width), low),
        ((C4, rows, width), low),
        ((C4, rows, width), low),
        ((C4, rows, width), low),
        ((4, 3, rows, width), low),
        ((4, 3, rows, width), low),
        ((rows, width), full),
        ((C4, rows, 3 * part), low),
        ((C4, P4, rows, rows), full),
        ((C4, rows, part), low),
        ((C4, rows, hidden), full),
        ((C4, rows, hidden), low),
        ((C4, rows, hidden), low),
        ((C4, rows, 3 * part), low),
        ((rows, width), full),
        ((rows, 128), full),
        ((rows, width), full),
        ((rows, width), full),
        ((P4, shrink, width), full),
        ((P4, shrink, width), low),
        ((P4, shrink, width), low),
        ((3, shrink, width), low),
        ((3, shrink, width), low),
        ((P4, C4, own, hidden), full),
        ((P4, C4, own, hidden), low),
        ((P4, C4, own, hidden), low),
        ((3, C4, own, hidden), low),
        ((3, C4, own, hidden), low),
        ((C4, own, hidden), low),
        ((C4, own, hidden), low),
        ((P4, own, width), full),
        ((P4, own, width), low),
        ((P4, own, width), low),
        ((3, own, width), low),
        ((3, own, width), low),
        ((P4, C4, own, 3 * part), full),
        ((P4, C4, own, 3 * part), low),
        ((P4, C4, own, 3 * part), low),
        ((3, C4, own, 3 * part), low),
        ((3, C4, own, 3 * part), low),
        ((C4, own, 3 * part), low),
        ((C4, own, 3 * part), low),
        ((8, width), full),
        ((3, 8, width), full),
        ((16, width), full),
        ((3, 16, width), full),
        ((16, width), full),
        ((16, width), full),
    ]
    anywhere = pl.BlockSpec(memory_space=pl.ANY)
    inside = pl.BlockSpec(memory_space=pltpu.VMEM)
    given = (
        inputs,
        live_keys[None, :],
        triple_weight,
        output_weight,
        expand_weight,
        shrink_weight,
        cotangent,
    )
    given += tuple(vector[None, :] for vector in vectors) + (expand_bias[None, :],)
    result = pl.pallas_call(
        plane_kernel,
        out_shape=[jax.ShapeDtypeStruct(*item) for item in outs],
        in_specs=[anywhere] * len(given),
        out_specs=[anywhere] * 6 + [inside] * 2,
        scratch_shapes=[pltpu.VMEM(*item) for item in scratch]
        + [pltpu.SemaphoreType.DMA((COPY_COUNT,))] * 2
        + [pltpu.SemaphoreType.DMA((16,)), pltpu.SemaphoreType.DMA((6,))],
        compiler_params=pltpu.CompilerParams(
            collective_id=0, has_side_effects=True, vmem_limit_bytes=60 * 2**20
        ),
        cost_estimate=pl.CostEstimate(
            flops=6 * rows * width * 12 * width,
            bytes_accessed=16 * 2**20,
            transcendentals=rows * hidden * 8,
        ),
        name="plane_layer",
    )(*given)
    ends = list(outs[:6]) + [((1, own), full)] * 8 + [((1, shrink), full)]
    done = pl.pallas_call(
        hand_over,
        out_shape=[jax.ShapeDtypeStruct(*item) for item in ends],
        in_specs=[inside] * 8,
        out_specs=[anywhere] * 6 + [inside] * 9,
        scratch_shapes=[pltpu.SemaphoreType.DMA((6,))],
        name="hand_over",
    )(*result)
    layer_out, input_grad, triple_grad, output_grad, expand_grad, shrink_grad = done[:6]
    small = [item[0] for item in done[6:]]
    return (
        layer_out,
        input_grad,
        triple_grad,
        small[0],
        small[1],
        output_grad,
        small[2],
        small[3],
        small[4],
        expand_grad,
        small[8],
        shrink_grad,
        small[5],
        small[6],
        small[7],
    )


def solution(mesh):
    placed = (
        P("fsdp", None),
        P("fsdp"),
        P("fsdp", None),
        P("fsdp"),
        P("fsdp"),
        P("fsdp", None),
        P("fsdp"),
        P("fsdp"),
        P("fsdp"),
        P("fsdp", None),
        P("fsdp"),
        P("fsdp", None),
        P("fsdp"),
        P("fsdp"),
        P("fsdp"),
        P("fsdp", None),
    )
    return jax.shard_map(
        plane_body if mesh.shape["fsdp"] == PLANES * GROUP else body,
        mesh=mesh,
        in_specs=placed,
        out_specs=(
            P("fsdp", None),
            P("fsdp", None),
            P("fsdp", None),
            P("fsdp"),
            P("fsdp"),
            P("fsdp", None),
            P("fsdp"),
            P("fsdp"),
            P("fsdp"),
            P("fsdp", None),
            P("fsdp"),
            P("fsdp", None),
            P("fsdp"),
            P("fsdp"),
            P("fsdp"),
        ),
        check_vma=False,
    )
```

```python
import jax
import jax.numpy as jnp
from jax import lax
from jax.experimental import pallas as pl
from jax.experimental.pallas import tpu as pltpu
from jax.sharding import PartitionSpec as P

HEADS = 16


EPSILON = 1e-05
NEGATIVE = -1e30
ROOT_HALF = 0.7071067811865476
INV_ROOT_TWO_PI = 0.3989422804014327


def batched(form, left, right):
    return jnp.einsum(form, left, right, preferred_element_type=jnp.float32)


def layer_norm(hidden, gain, shift):
    center = hidden - jnp.mean(hidden, axis=-1, keepdims=True)
    inv_std = lax.rsqrt(jnp.mean(center * center, axis=-1, keepdims=True) + EPSILON)
    normed = center * inv_std
    return (normed * gain.astype(jnp.float32) + shift.astype(jnp.float32), normed, inv_std)


def layer_norm_back(upstream, normed, inv_std, gain):
    scaled = upstream * gain.astype(jnp.float32)
    inner = (
        scaled
        - jnp.mean(scaled, axis=-1, keepdims=True)
        - normed * jnp.mean(scaled * normed, axis=-1, keepdims=True)
    )
    return (inv_std * inner, jnp.sum(upstream * normed, axis=0), jnp.sum(upstream, axis=0))


def normal_cdf(values):
    return 0.5 * (1.0 + lax.erf(values * ROOT_HALF))


def masked_scores(query, keys, live):
    scores = batched("qhd,khd->hqk", query, keys)
    allowed = live == 1
    return jnp.where(allowed[None, None, :], scores, NEGATIVE)


def forward(params, tokens, live):
    (
        triple_weight,
        query_bias,
        value_bias,
        output_weight,
        output_bias,
        first_gain,
        first_shift,
        expand_weight,
        expand_bias,
        shrink_weight,
        shrink_bias,
        second_gain,
        second_shift,
    ) = params
    row_count = tokens.shape[0]
    width_all = tokens.shape[1]
    head_size = width_all // HEADS
    factor = head_size ** (-0.5)
    projected = jnp.dot(tokens, triple_weight, preferred_element_type=jnp.float32)
    query = ((projected[:, :width_all] + query_bias.astype(jnp.float32)) * factor).astype(
        jnp.bfloat16
    )
    keys = projected[:, width_all : 2 * width_all].astype(jnp.bfloat16)
    values = (projected[:, 2 * width_all :] + value_bias.astype(jnp.float32)).astype(jnp.bfloat16)
    query = query.reshape(row_count, HEADS, head_size)
    keys = keys.reshape(row_count, HEADS, head_size)
    values = values.reshape(row_count, HEADS, head_size)
    scores = masked_scores(query, keys, live)
    top = jnp.max(scores, axis=-1, keepdims=True)
    expo = jnp.exp(scores - top)
    total = jnp.sum(expo, axis=-1, keepdims=True)
    log_total = top + jnp.log(total)
    probs = (expo / total).astype(jnp.bfloat16)
    context = (
        batched("hqk,khd->qhd", probs, values).astype(jnp.bfloat16).reshape(row_count, width_all)
    )
    first_in = (
        tokens.astype(jnp.float32)
        + jnp.dot(context, output_weight, preferred_element_type=jnp.float32)
        + output_bias.astype(jnp.float32)
    )
    middle, first_norm, first_rate = layer_norm(first_in, first_gain, first_shift)
    mid_low = middle.astype(jnp.bfloat16)
    pre_act = jnp.dot(
        mid_low, expand_weight, preferred_element_type=jnp.float32
    ) + expand_bias.astype(jnp.float32)
    act_low = (pre_act * normal_cdf(pre_act)).astype(jnp.bfloat16)
    second_in = (
        middle
        + jnp.dot(act_low, shrink_weight, preferred_element_type=jnp.float32)
        + shrink_bias.astype(jnp.float32)
    )
    result, second_norm, second_rate = layer_norm(second_in, second_gain, second_shift)
    saved = (
        tokens,
        live,
        query,
        keys,
        values,
        log_total,
        context,
        first_norm,
        first_rate,
        mid_low,
        pre_act,
        act_low,
        second_norm,
        second_rate,
    )
    return (result.astype(jnp.bfloat16), saved)


def back_upper(params, saved, upstream):
    (
        triple_weight,
        query_bias,
        value_bias,
        output_weight,
        output_bias,
        first_gain,
        first_shift,
        expand_weight,
        expand_bias,
        shrink_weight,
        shrink_bias,
        second_gain,
        second_shift,
    ) = params
    (
        tokens,
        live,
        query,
        keys,
        values,
        log_total,
        context,
        first_norm,
        first_rate,
        mid_low,
        pre_act,
        act_low,
        second_norm,
        second_rate,
    ) = saved
    d_second, second_gain_grad, second_shift_grad = layer_norm_back(
        upstream.astype(jnp.float32), second_norm, second_rate, second_gain
    )
    d_second_low = d_second.astype(jnp.bfloat16)
    shrink_bias_grad = jnp.sum(d_second, axis=0)
    d_act = jnp.dot(d_second_low, shrink_weight.T, preferred_element_type=jnp.float32)
    slope = normal_cdf(pre_act) + pre_act * jnp.exp(-0.5 * pre_act * pre_act) * INV_ROOT_TWO_PI
    d_pre = d_act * slope
    expand_bias_grad = jnp.sum(d_pre, axis=0)
    d_pre_low = d_pre.astype(jnp.bfloat16)
    d_mid = d_second + jnp.dot(d_pre_low, expand_weight.T, preferred_element_type=jnp.float32)
    d_first, first_gain_grad, first_shift_grad = layer_norm_back(
        d_mid, first_norm, first_rate, first_gain
    )
    small = (
        first_gain_grad,
        first_shift_grad,
        expand_bias_grad,
        shrink_bias_grad,
        second_gain_grad,
        second_shift_grad,
    )
    pairs = ((mid_low, d_pre_low), (act_low, d_second_low))
    return (small, pairs, d_first)


def back_lower(params, saved, d_first):
    (
        triple_weight,
        query_bias,
        value_bias,
        output_weight,
        output_bias,
        first_gain,
        first_shift,
        expand_weight,
        expand_bias,
        shrink_weight,
        shrink_bias,
        second_gain,
        second_shift,
    ) = params
    (
        tokens,
        live,
        query,
        keys,
        values,
        log_total,
        context,
        first_norm,
        first_rate,
        mid_low,
        pre_act,
        act_low,
        second_norm,
        second_rate,
    ) = saved
    row_count = tokens.shape[0]
    width_all = tokens.shape[1]
    head_size = width_all // HEADS
    factor = head_size ** (-0.5)
    d_first_low = d_first.astype(jnp.bfloat16)
    output_bias_grad = jnp.sum(d_first, axis=0)
    d_context = jnp.dot(d_first_low, output_weight.T, preferred_element_type=jnp.float32).astype(
        jnp.bfloat16
    )
    d_context = d_context.reshape(row_count, HEADS, head_size)
    scores = masked_scores(query, keys, live)
    probs = jnp.exp(scores - log_total)
    probs_low = probs.astype(jnp.bfloat16)
    d_values = batched("hqk,qhd->khd", probs_low, d_context)
    d_probs = batched("qhd,khd->hqk", d_context, values)
    inner = jnp.sum(probs * d_probs, axis=-1, keepdims=True)
    d_scores = (probs * (d_probs - inner)).astype(jnp.bfloat16)
    d_query = factor * batched("hqk,khd->qhd", d_scores, keys)
    d_keys = batched("hqk,qhd->khd", d_scores, query)
    d_query = d_query.reshape(row_count, width_all)
    d_keys = d_keys.reshape(row_count, width_all)
    d_values = d_values.reshape(row_count, width_all)
    d_proj = jnp.concatenate([d_query, d_keys, d_values], axis=1).astype(jnp.bfloat16)
    query_bias_grad = jnp.sum(d_query, axis=0)
    value_bias_grad = jnp.sum(d_values, axis=0)
    input_grad = (
        d_first + jnp.dot(d_proj, triple_weight.T, preferred_element_type=jnp.float32)
    ).astype(jnp.bfloat16)
    small = (query_bias_grad, value_bias_grad, output_bias_grad)
    pairs = ((tokens, d_proj), (context, d_first_low))
    return (small, pairs, input_grad)


def swap(value, bit, count):
    return lax.ppermute(value, "fsdp", [(i, i ^ (1 << bit)) for i in range(count)])


def own_bit(bit):
    return (lax.axis_index("fsdp") >> bit) & 1


def place(base, value, places, levels):
    starts = [0] * base.ndim
    for bit, at in places:
        starts[levels - 1 - bit] = at
    return lax.dynamic_update_slice(base, value, starts)


def grown(value, bits, levels):
    shape = list(value.shape)
    for bit in bits:
        shape[levels - 1 - bit] = 2
    return jnp.zeros(shape, value.dtype)


def join(own, other, bit, levels):
    mine = own_bit(bit)
    base = place(grown(own, (bit,), levels), own, ((bit, mine),), levels)
    return place(base, other, ((bit, 1 - mine),), levels)


def orders(levels):
    ring = list(range(1, levels))
    return [ring[k * len(ring) // 3 :] + ring[: k * len(ring) // 3] for k in range(3)]


def collect(shard, order, count):
    levels = count.bit_length() - 1
    held = shard.reshape((1,) * levels + shard.shape)
    steps = list(reversed(order))
    for bit in steps[:-1]:
        held = join(held, swap(held, bit, count), bit, levels)
    bit = steps[-1]
    across = swap(held, bit, count)
    beside = swap(held, 0, count)
    corner = swap(across, 0, count)
    mine, core = own_bit(bit), own_bit(0)
    full = grown(held, (bit, 0), levels)
    full = place(full, held, ((bit, mine), (0, core)), levels)
    full = place(full, beside, ((bit, mine), (0, 1 - core)), levels)
    full = place(full, across, ((bit, 1 - mine), (0, core)), levels)
    held = place(full, corner, ((bit, 1 - mine), (0, 1 - core)), levels)
    return held.reshape((count * shard.shape[0],) + shard.shape[1:])


def halve(terms, order, count, last):
    levels = count.bit_length() - 1
    for bit in order:
        axis = terms.ndim - 3 - bit if last else terms.ndim - 2 - bit
        mine = own_bit(bit)
        keep = lax.dynamic_slice_in_dim(terms, mine, 1, axis)
        send = lax.dynamic_slice_in_dim(terms, 1 - mine, 1, axis)
        total = keep.astype(jnp.float32) + swap(send, bit, count).astype(jnp.float32)
        terms = total if bit == order[-1] else total.astype(terms.dtype)
    return terms.reshape(terms.shape[-2:])


def by_core(left, count):
    parts = left.reshape(left.shape[0], count // 2, 2, left.shape[1] // count)
    core = own_bit(0)
    pick = lambda at: lax.dynamic_index_in_dim(parts, at, 2, keepdims=False).reshape(
        left.shape[0], left.shape[1] // 2
    )
    return (pick(core), pick(1 - core))


def pair_up(left, right, count):
    mine, other = by_core(left, count)
    return (
        jnp.concatenate([mine, swap(other, 0, count)], axis=0),
        jnp.concatenate([right, swap(right, 0, count)], axis=0),
    )


def summed_grad(left, right, pieces, count):
    levels = count.bit_length() - 1
    results = []
    offset = 0
    for extent, order in pieces:
        term = jnp.einsum(
            "tk,tw->kw",
            left,
            right[:, offset : offset + extent],
            preferred_element_type=jnp.float32,
        ).astype(jnp.bfloat16)
        term = term.reshape((2,) * (levels - 1) + (left.shape[1] * 2 // count, extent))
        results.append(halve(term, order, count, False))
        offset = offset + extent
    return results[0] if len(results) == 1 else jnp.concatenate(results, axis=1)


def body(
    inputs,
    live_keys,
    triple_weight,
    query_bias,
    value_bias,
    output_weight,
    output_bias,
    first_gain,
    first_shift,
    expand_weight,
    expand_bias,
    shrink_weight,
    shrink_bias,
    second_gain,
    second_shift,
    cotangent,
):
    count = lax.axis_size("fsdp")
    levels = count.bit_length() - 1
    width = inputs.shape[1]
    ways = orders(levels)
    vectors = (
        query_bias,
        value_bias,
        output_bias,
        first_gain,
        first_shift,
        expand_bias,
        shrink_bias,
        second_gain,
        second_shift,
    )
    packed = collect(jnp.concatenate(vectors)[None, :], ways[0], count)
    wide = []
    offset = 0
    for vector in vectors:
        wide.append(packed[:, offset : offset + vector.shape[0]].reshape(-1))
        offset = offset + vector.shape[0]
    gathered = (
        collect(triple_weight, ways[2], count),
        wide[0],
        wide[1],
        collect(output_weight, ways[0], count),
        wide[2],
        wide[3],
        wide[4],
        collect(expand_weight, ways[0], count),
        wide[5],
        collect(shrink_weight, ways[1], count),
        wide[6],
        wide[7],
        wide[8],
    )
    layer_out, saved = forward(gathered, inputs, live_keys)
    upper_small, upper_pairs, d_first = back_upper(gathered, saved, cotangent)
    lower_small, lower_pairs, input_grad = back_lower(gathered, saved, d_first)
    hidden = expand_weight.shape[1]
    shrink_grad = summed_grad(
        *pair_up(*upper_pairs[1], count),
        ((width * 3 // 4, ways[1]), (width // 4, ways[2])),
        count,
    )
    expand_grad = summed_grad(
        *pair_up(*upper_pairs[0], count),
        ((hidden * 3 // 4, ways[0]), (hidden // 4, ways[2])),
        count,
    )
    output_grad = summed_grad(*pair_up(*lower_pairs[1], count), ((width, ways[1]),), count)
    triple_grad = summed_grad(
        *pair_up(*lower_pairs[0], count),
        ((width, ways[0]), (width, ways[1]), (width, ways[2])),
        count,
    )
    sums = lower_small + upper_small
    terms = jnp.concatenate([item.reshape(count, -1) for item in sums], axis=1)
    terms = terms.reshape((2,) * levels + (1, terms.shape[1]))
    owned = halve(terms, list(range(levels)), count, True)[0]
    small = []
    offset = 0
    for item in sums:
        extent = item.shape[0] // count
        small.append(owned[offset : offset + extent])
        offset = offset + extent
    return (
        layer_out,
        input_grad,
        triple_grad,
        small[0],
        small[1],
        output_grad,
        small[2],
        small[3],
        small[4],
        expand_grad,
        small[5],
        shrink_grad,
        small[6],
        small[7],
        small[8],
    )


PLANES = 4
CHIPS = 4
GROUP = 2 * CHIPS
MESH = pl.DeviceIdType.MESH


def nn(left, right):
    return lax.dot_general(
        left, right, (((1,), (0,)), ((), ())), preferred_element_type=jnp.float32
    )


def nt(left, right):
    return lax.dot_general(
        left, right, (((1,), (1,)), ((), ())), preferred_element_type=jnp.float32
    )


def tn(left, right):
    return lax.dot_general(
        left, right, (((0,), (0,)), ((), ())), preferred_element_type=jnp.float32
    )


def share(plane, chip):
    return chip % 2 + 2 * (plane % 2) + 4 * (chip // 2) + 8 * (plane // 2)


def flat(value):
    return value.reshape((-1, value.shape[-1]))


def normalize(hidden):
    center = hidden - jnp.mean(hidden, axis=-1, keepdims=True)
    rate = lax.rsqrt(jnp.mean(center * center, axis=-1, keepdims=True) + EPSILON)
    return center * rate, rate


def normalize_back(upstream, normed, rate, gain):
    scaled = upstream * gain
    inner = (
        scaled
        - jnp.mean(scaled, axis=-1, keepdims=True)
        - normed * jnp.mean(scaled * normed, axis=-1, keepdims=True)
    )
    return (
        rate * inner,
        jnp.sum(upstream * normed, axis=0, keepdims=True),
        jnp.sum(upstream, axis=0, keepdims=True),
    )


COPIES = {}
COPY_COUNT = 0
for _names, _ks in (
    (("v", "vz", "t", "tz", "tw", "e", "ez", "oz", "sz", "x"), (1, 2, 3)),
    (("r1", "r2", "r3", "r4", "gsz", "gez", "goz", "gtz", "gty", "gep", "gtp", "a", "bz"), (1, 2, 3)),
    (("m", "d2", "d1"), (1, 2, 3, 4, 5, 6)),
    (("ts", "es", "os", "ss", "gss", "ges"), (0, 1, 2, 3)),
    (("gts",), (0, 1)),
    (("vs", "gos", "bs"), (0,)),
):
    for _name in _names:
        COPIES[_name] = (COPY_COUNT - _ks[0], _ks)
        COPY_COUNT += len(_ks)


def plane_kernel(
    x_hbm, live_hbm, t_hbm, o_hbm, e_hbm, s_hbm, ct_hbm,
    vec0, vec1, vec2, vec3, vec4, vec5, vec6, vec7, eb_hbm,
    lo_hbm, ig_hbm, tg_hbm, og_hbm, eg_hbm, sg_hbm, small_ref, ebg_ref,
    t_ref, e_ref, ct_ref, live_ref, low0, low1, low2, low3, low4, low5, low6, low7, eb_ref,
    lo_ref, ig_ref, tg_ref, og_ref, eg_ref, sg_ref, vbuf, vfull, vchip, vhid, tsend, tbuf, esend, ebuf, obuf, sbuf, xg, mg, d2g, d1g,
    rsend, rrecv, keep, qkv, pbuf, ctx, slope, act, dpre, dproj, norm1, rate1, mid, dtok,
    gs_own, gs_out, gs_in, gs_zout, gs_zin,
    ge_own, ge_out, ge_in, ge_zout, ge_zin, ge_pout, ge_pin,
    go_own, go_out, go_in, go_zout, go_zin,
    gt_own, gt_out, gt_in, gt_zout, gt_zin, gt_pout, gt_pin,
    apart, ain, bpart, bin_, bsum, bsib, send_sem, recv_sem, load_sem, store_sem,
):
    me = lax.axis_index("fsdp")
    core = lax.rem(me, 2)
    chip = lax.rem(me // 2, 2) + 2 * lax.rem(me // 8, 2)
    plane = lax.rem(me // 4, 2) + 2 * (me // 16)
    sibling = me + 1 - 2 * core

    def flip(base, k):
        return lax.rem(base + k, 2) + 2 * lax.rem(base // 2 + k // 2, 2)

    def chip_at(k):
        return flip(chip, k)

    def plane_at(k):
        return flip(plane, k)

    def device_of(plane, chip, core):
        high = 16 * (plane // 2) + 8 * (chip // 2)
        return high + 4 * lax.rem(plane, 2) + 2 * lax.rem(chip, 2) + core

    def mate(k):
        return device_of(plane, chip_at(k), core)

    def above(k):
        return device_of(plane_at(k), chip, core)

    def rows_of(plane, chip):
        return plane // 2, chip // 2, lax.rem(plane, 2), lax.rem(chip, 2), core

    def plane_rows(plane, half=slice(None)):
        return plane // 2, half, lax.rem(plane, 2), slice(None), core

    def origin(k):
        return plane_at(2) if k == 3 else plane

    def onward(k):
        return above(1) if k == 3 else above(k)

    def copy(name, k, source, target, device):
        spot = COPIES[name][0] + k
        return pltpu.make_async_remote_copy(
            src_ref=source,
            dst_ref=target,
            send_sem=send_sem.at[spot],
            recv_sem=recv_sem.at[spot],
            device_id=(device,),
            device_id_type=MESH,
        )

    def shared(name, k, held):
        half = held.shape[1] // 2
        first, last = slice(0, half), slice(half, 2 * half)
        rows = first if k in (1, 3, 6) else last
        if k in (3, 4):
            return copy(name, k, held.at[k - 2, rows], held.at[3, rows], mate(5 - k))
        to = 1 if k in (1, 5) else 2
        return copy(name, k, held.at[0, rows], held.at[to, rows], mate(to))

    moves = {
        "v": lambda k: copy(
            "v", k, vbuf.at[plane, chip, core], vbuf.at[plane, chip, core], mate(k)
        ),
        "vz": lambda k: copy(
            "vz", k, vbuf.at[plane, :, core], vbuf.at[plane, :, core], above(k)
        ),
        "vs": lambda k: copy("vs", 0, vbuf.at[:, :, core], vbuf.at[:, :, core], sibling),
        "t": lambda k: copy(
            "t", k, tsend.at[chip_at(k)], tbuf.at[*rows_of(plane, chip)], mate(k)
        ),
        "tz": lambda k: copy(
            "tz",
            k,
            tbuf.at[*plane_rows(origin(k), 0)],
            tbuf.at[*plane_rows(origin(k), 0)],
            onward(k),
        ),
        "ts": lambda k: copy(
            "ts",
            k,
            tbuf.at[*plane_rows(plane_at(k))],
            tbuf.at[*plane_rows(plane_at(k))],
            sibling,
        ),
        "e": lambda k: copy(
            "e", k, esend.at[chip_at(k)], ebuf.at[*rows_of(plane, chip)], mate(k)
        ),
        "ez": lambda k: copy(
            "ez",
            k,
            ebuf.at[*plane_rows(origin(k))],
            ebuf.at[*plane_rows(origin(k))],
            onward(k),
        ),
        "es": lambda k: copy(
            "es",
            k,
            ebuf.at[*plane_rows(plane_at(k))],
            ebuf.at[*plane_rows(plane_at(k))],
            sibling,
        ),
        "oz": lambda k: copy(
            "oz", k, obuf.at[origin(k), core], obuf.at[origin(k), core], onward(k)
        ),
        "os": lambda k: copy(
            "os", k, obuf.at[plane_at(k), core], obuf.at[plane_at(k), core], sibling
        ),
        "sz": lambda k: copy(
            "sz", k, sbuf.at[origin(k), core], sbuf.at[origin(k), core], onward(k)
        ),
        "ss": lambda k: copy(
            "ss", k, sbuf.at[plane_at(k), core], sbuf.at[plane_at(k), core], sibling
        ),
        "tw": lambda k: copy(
            "tw",
            k,
            tbuf.at[*plane_rows(origin(k), 1)],
            tbuf.at[*plane_rows(origin(k), 1)],
            onward(k),
        ),
        "x": lambda k: copy(
            "x", k, xg.at[2 if k == 3 else 0], xg.at[k], mate(1 if k == 3 else k)
        ),
        "m": lambda k: shared("m", k, mg),
        "d2": lambda k: shared("d2", k, d2g),
        "d1": lambda k: shared("d1", k, d1g),
        "gss": lambda k: copy(
            "gss", k, gs_out.at[plane_at(k)], gs_in.at[plane_at(k)], sibling
        ),
        "ges": lambda k: copy(
            "ges", k, ge_out.at[plane_at(k)], ge_in.at[plane_at(k)], sibling
        ),
        "gos": lambda k: copy("gos", 0, go_out, go_in, sibling),
        "gts": lambda k: copy(
            "gts", k, gt_out.at[:, 2 * k : 2 * k + 2], gt_in.at[:, 2 * k : 2 * k + 2], sibling
        ),
        "gsz": lambda k: copy("gsz", k, gs_zout.at[k - 1], gs_zin.at[k - 1], onward(k)),
        "gez": lambda k: copy("gez", k, ge_zout.at[k - 1], ge_zin.at[k - 1], onward(k)),
        "goz": lambda k: copy("goz", k, go_zout.at[k - 1], go_zin.at[k - 1], onward(k)),
        "gtz": lambda k: copy(
            "gtz", k, gt_zout.at[k - 1, 0:2], gt_zin.at[k - 1, 0:2], onward(k)
        ),
        "gty": lambda k: copy(
            "gty", k, gt_zout.at[k - 1, 2:4], gt_zin.at[k - 1, 2:4], onward(k)
        ),
        "gep": lambda k: copy("gep", k, ge_pout.at[chip_at(k)], ge_pin.at[chip], mate(k)),
        "gtp": lambda k: copy("gtp", k, gt_pout.at[chip_at(k)], gt_pin.at[chip], mate(k)),
        "a": lambda k: copy("a", k, apart, ain.at[k - 1], mate(k)),
        "bz": lambda k: copy("bz", k, bpart, bin_.at[k - 1], above(k)),
        "bs": lambda k: copy("bs", 0, bsum, bsib, sibling),
    }
    for turn in range(4):
        name = "r%d" % (turn + 1)
        moves[name] = lambda k, name=name, turn=turn: copy(
            name, k, rsend.at[turn, k - 1], rrecv.at[turn, k - 1], mate(k)
        )
    moves["r1"] = lambda k: copy(
        "r1", k, rsend.at[0, k - 1], rrecv.at[0, k - 1], mate(1 if k == 3 else k)
    )

    def span(name):
        return COPIES[name][1]

    def start(name):
        for k in span(name):
            moves[name](k).start()

    def arrive(name):
        for k in span(name):
            moves[name](k).wait_recv()

    def send_out(name):
        moves[name](2).start()
        moves[name](1).start()

    def pass_on(name, beside):
        moves[name](2).wait_recv()
        moves[name](3).start()
        moves[beside](2).start()

    def take_in(name, beside):
        for k in (1, 3):
            moves[name](k).wait_recv()
            moves[beside](k).start()

    def take(name, k):
        @pl.when(k == 1)
        def _():
            for i in (1, 2):
                moves[name](i).wait_recv()
                moves[name](i + 2).start()
            moves[name](5).wait_recv()

        @pl.when(k == 2)
        def _():
            moves[name](6).wait_recv()

        @pl.when(k == 3)
        def _():
            moves[name](3).wait_recv()
            moves[name](4).wait_recv()

    def offer(name):
        for k in (1, 2, 5, 6):
            moves[name](k).start()

    barrier = pltpu.get_barrier_semaphore()
    for k in range(1, 4):
        for device in (mate(k), above(k)):
            pl.semaphore_signal(barrier, inc=1, device_id=(device,), device_id_type=MESH)
    pl.semaphore_signal(barrier, inc=1, device_id=(sibling,), device_id_type=MESH)

    sources = (
        t_hbm, vec0, vec1, vec2, vec3, vec4, vec5, vec6, vec7, eb_hbm, live_hbm,
        e_hbm, x_hbm, o_hbm, s_hbm, ct_hbm,
    )
    targets = (
        t_ref, low0, low1, low2, low3, low4, low5, low6, low7, eb_ref, live_ref,
        e_ref, xg.at[0], obuf.at[plane, core], sbuf.at[plane, core], ct_ref,
    )
    loads = [
        pltpu.make_async_copy(source, target, load_sem.at[i])
        for i, (source, target) in enumerate(zip(sources, targets))
    ]
    for load in loads:
        load.start()
    pairs = (
        (lo_ref, lo_hbm), (ig_ref, ig_hbm), (tg_ref, tg_hbm), (og_ref, og_hbm),
        (eg_ref, eg_hbm), (sg_ref, sg_hbm),
    )
    stores = [
        pltpu.make_async_copy(source, target, store_sem.at[i])
        for i, (source, target) in enumerate(pairs)
    ]

    for load in loads[:11]:
        load.wait()
    row = lax.broadcasted_iota(jnp.int32, (8, 32), 0)
    vec = jnp.zeros((8, 32), jnp.float32)
    for i, item in enumerate((low0, low1, low2, low3, low4, low5, low6, low7)):
        vec = jnp.where(row == i, item[...].astype(jnp.float32), vec)
    lane = lax.broadcasted_iota(jnp.int32, (8, 128), 1) // 32
    row = lax.broadcasted_iota(jnp.int32, (8, 128), 0)
    by_row = lax.rem(chip, 2) * 2 + core
    by_head = lax.rem(plane, 2) * 2 + core
    spread = jnp.concatenate([vec, vec, vec, vec], axis=1)
    spread = jnp.where(lane == jnp.where(row < 2, by_head, by_row), spread, 0.0)
    own_rows = vbuf.at[plane, chip, core]
    own_rows[0:8, :] = spread
    own_rows[8:9, :] = eb_ref[...].astype(jnp.float32)
    own_rows[9:10, :] = live_ref[...].astype(jnp.float32)
    own_rows[10:16, :] = jnp.zeros((6, 128), jnp.float32)
    width = x_hbm.shape[1]
    part = width // PLANES
    piece = part // CHIPS
    for other in range(CHIPS):
        tsend[other] = jnp.concatenate(
            [
                t_ref[:, kind * width + share(zz, other) * piece :][:, :piece]
                for kind in range(3)
                for zz in range(PLANES)
            ],
            axis=1,
        )
    tbuf[rows_of(plane, chip)] = tsend[chip]
    for load in loads[12:15]:
        load.wait()
    pl.semaphore_wait(barrier, 7)

    start("t")
    start("v")
    loads[11].wait()
    for other in range(CHIPS):
        for zz in range(PLANES):
            esend[other, :, zz * part : (zz + 1) * part] = e_ref[
                :, share(zz, other) * part : (share(zz, other) + 1) * part
            ]
    ebuf[rows_of(plane, chip)] = esend[chip]
    moves["os"](0).start()
    moves["ss"](0).start()
    arrive("t")
    send_out("tz")
    send_out("tw")
    moves["x"](1).start()
    moves["x"](2).start()
    moves["ts"](0).start()
    start("e")
    arrive("v")
    start("vz")
    moves["tz"](2).wait_recv()
    moves["tz"](3).start()
    moves["x"](2).wait_recv()
    moves["x"](3).start()
    moves["tw"](2).wait_recv()
    moves["tw"](3).start()
    moves["ts"](2).start()
    send_out("oz")
    arrive("e")
    moves["ez"](2).start()
    moves["es"](0).start()
    arrive("vz")
    start("vs")
    for k in (1, 3):
        moves["tz"](k).wait_recv()
        moves["tw"](k).wait_recv()
        moves["ts"](k).start()
    pass_on("oz", "os")
    moves["ez"](1).start()
    moves["sz"](2).start()
    moves["sz"](1).start()
    arrive("vs")
    for block in range(8):
        total = None
        for i in range(4):
            near = block % 2 + 2 * (block // 4)
            term = vbuf[near, i // 2 + 2 * (block // 2 % 2), i % 2]
            total = term if total is None else total + term
        vfull[:, 128 * block : 128 * block + 128] = total
        vhid[:, 128 * block : 128 * block + 128] = vbuf[block // 2, chip, block % 2][8:16]
    for half in range(2):
        vchip[:, 128 * half : 128 * half + 128] = (
            vbuf[2 * half, chip, 0]
            + vbuf[2 * half, chip, 1]
            + vbuf[2 * half + 1, chip, 0]
            + vbuf[2 * half + 1, chip, 1]
        )
    take_in("oz", "os")
    arrive("os")
    arrive("ts")

    head = width // HEADS
    factor = head ** (-0.5)
    heads = range(PLANES)

    moves["x"](1).wait_recv()
    moves["x"](3).wait_recv()

    def attend(step, carry):
        k = 3 - step
        tokens = xg[k]
        proj = nn(tokens[:, :part], flat(tbuf[0, 0]))
        for zz in range(1, PLANES):
            proj = proj + nn(tokens[:, zz * part : (zz + 1) * part], flat(tbuf[zz // 2, zz % 2]))
        query = ((proj[:, :part] + vchip[0:1, :]) * factor).astype(jnp.bfloat16)
        keys = proj[:, part : 2 * part].astype(jnp.bfloat16)
        values = (proj[:, 2 * part :] + vchip[1:2, :]).astype(jnp.bfloat16)
        qkv[k, :, :part] = query
        qkv[k, :, part : 2 * part] = keys
        qkv[k, :, 2 * part :] = values
        live = vbuf[plane, chip_at(k), core][9:10, :] > 0.5
        joined = []
        for h in heads:
            cols = slice(h * head, (h + 1) * head)
            scores = jnp.where(live, nt(query[:, cols], keys[:, cols]), NEGATIVE)
            expo = jnp.exp(scores - jnp.max(scores, axis=-1, keepdims=True))
            probs = expo / jnp.sum(expo, axis=-1, keepdims=True)
            pbuf[k, h] = probs
            joined.append(nn(probs.astype(jnp.bfloat16), values[:, cols]))
        context = jnp.concatenate(joined, axis=1).astype(jnp.bfloat16)
        ctx[k] = context
        term = nn(context, flat(obuf[...]))

        @pl.when(k == 0)
        def _():
            keep[...] = term

        @pl.when(k == 1)
        def _():
            rsend[0, 0] = term.astype(jnp.bfloat16)
            moves["r1"](1).start()
            pass_on("ez", "es")

        @pl.when(k == 2)
        def _():
            mid[...] = term

        @pl.when(k == 3)
        def _():
            rsend[0, 2] = term.astype(jnp.bfloat16)
            moves["r1"](3).start()

        return carry

    lax.fori_loop(0, 4, attend, 0)
    moves["r1"](3).wait_recv()
    rsend[0, 1] = (mid[...] + rrecv[0, 2].astype(jnp.float32)).astype(jnp.bfloat16)
    moves["r1"](2).start()
    pass_on("sz", "ss")

    def collected(turn):
        total = keep[...]
        for k in (1, 2, 3) if turn else (1, 2):
            moves["r%d" % (turn + 1)](k).wait_recv()
            total = total + rrecv[turn, k - 1].astype(jnp.float32)
        return total

    first_in = xg[0].astype(jnp.float32) + collected(0) + vfull[2:3, :]
    normed, rate = normalize(first_in)
    norm1[...] = normed
    rate1[...] = jnp.broadcast_to(rate, rate1.shape)
    middle = normed * vfull[3:4, :] + vfull[4:5, :]
    mid[...] = middle
    mg[0] = middle.astype(jnp.bfloat16)
    offer("m")

    take_in("ez", "es")
    arrive("es")

    def feed(k, carry):
        take("m", k)

        low = mg[k]
        pre = vhid[0:1, :] + nn(low[:, :part], flat(ebuf[0, 0]))
        for zz in range(1, PLANES):
            pre = pre + nn(low[:, zz * part : (zz + 1) * part], flat(ebuf[zz // 2, zz % 2]))
        cdf = normal_cdf(pre)
        slope[k] = cdf + pre * jnp.exp(-0.5 * pre * pre) * INV_ROOT_TWO_PI
        active = (pre * cdf).astype(jnp.bfloat16)
        act[k] = active

        @pl.when(k == 0)
        def _():
            take_in("sz", "ss")
            arrive("ss")

        term = nn(active[:, :part], flat(sbuf[0]))
        for zz in range(1, PLANES):
            term = term + nn(active[:, zz * part : (zz + 1) * part], flat(sbuf[zz]))

        @pl.when(k > 0)
        def _():
            rsend[1, k - 1] = term.astype(jnp.bfloat16)
            moves["r2"](k).start()

        @pl.when(k == 0)
        def _():
            keep[...] = term

        return carry

    lax.fori_loop(0, 4, feed, 0)

    second_in = mid[...] + collected(1) + vfull[5:6, :]
    normed, rate = normalize(second_in)
    lo_ref[...] = (normed * vfull[6:7, :] + vfull[7:8, :]).astype(jnp.bfloat16)
    stores[0].start()
    loads[15].wait()
    d_second, gain_sum, shift_sum = normalize_back(
        ct_ref[...].astype(jnp.float32), normed, rate, vfull[6:7, :]
    )
    dtok[...] = d_second
    d2g[0] = d_second.astype(jnp.bfloat16)
    offer("d2")
    apart[0:2, :] = jnp.zeros((2, width), jnp.float32)
    apart[5:6, :] = jnp.sum(d_second, axis=0, keepdims=True)
    apart[6:7, :] = gain_sum
    apart[7:8, :] = shift_sum
    bpart[8:16, :] = jnp.zeros((8, width), jnp.float32)

    def feed_back(k, carry):
        take("d2", k)

        low = d2g[k]
        d_act = jnp.concatenate([nt(low, flat(sbuf[zz])) for zz in range(PLANES)], axis=1)
        d_pre = d_act * slope[k]
        bpart[8:9, :] += jnp.sum(d_pre, axis=0, keepdims=True)
        d_pre_low = d_pre.astype(jnp.bfloat16)
        dpre[k] = d_pre_low
        term = jnp.concatenate([nt(d_pre_low, flat(ebuf[zz // 2, zz % 2])) for zz in range(PLANES)], axis=1)

        @pl.when(k > 0)
        def _():
            rsend[2, k - 1] = term.astype(jnp.bfloat16)
            moves["r3"](k).start()

        @pl.when(k == 0)
        def _():
            keep[...] = term

        return carry

    lax.fori_loop(0, 4, feed_back, 0)

    def mine(term, axis):
        first, second = lax.index_in_dim(term, 0, axis, False), lax.index_in_dim(term, 1, axis, False)
        return (
            jnp.where(core == 0, first, second),
            jnp.where(core == 0, second, first).astype(jnp.bfloat16),
        )

    def columns(left, zz):
        return flat(left[:, :, pl.ds(pl.multiple_of(zz * part, 128), part)])

    def weigh_hidden(left, right, own, out, name):
        for k in (3, 2, 1, 0):
            zz = plane_at(k)
            term = tn(columns(left, zz), right)
            own[zz], out[zz] = mine(term.reshape(2, -1, term.shape[-1]), 0)
            moves[name](k).start()

    def weigh_width(left, right, own, out, high, low):
        term = tn(columns(left, 2 * high + low), right)
        held, given = mine(term.reshape(2, 2, 2, -1, term.shape[-1]), 2)
        for y in range(2):
            spot = y + 2 * high, slice(2 * low, 2 * low + 2)
            own[spot], out[spot] = held[y], given[y]

    def across(own, came, zout, name, k, cut=slice(None)):
        zz = plane_at(k)
        total = own[zz, cut] + came[zz, cut].astype(jnp.float32)
        zout[k - 1, cut] = total.astype(jnp.bfloat16)
        moves[name](k).start()

    def across_far(own, came, zout, zin, name, cut=slice(None)):
        moves[name](3).wait_recv()
        zz = plane_at(2)
        total = own[zz, cut] + came[zz, cut].astype(jnp.float32)
        zout[1, cut] = (total + zin[2, cut].astype(jnp.float32)).astype(jnp.bfloat16)
        moves[name](2).start()

    def gathered_sum(own, came, zin, *names):
        total = own[plane] + came[plane].astype(jnp.float32)
        for k in (1, 2):
            for name in names:
                moves[name](k).wait_recv()
            total = total + zin[k - 1].astype(jnp.float32)
        return total

    weigh_hidden(act, flat(d2g[...]), gs_own, gs_out, "gss")
    moves["gss"](3).wait_recv()
    across(gs_own, gs_in, gs_zout, "gsz", 3)
    d_pre_all = flat(dpre[...])
    for high, ks in ((1 - plane // 2, (3, 2)), (plane // 2, (1, 0))):
        for low in range(2):
            weigh_width(mg, d_pre_all, ge_own, ge_out, high, low)
        for k in ks:
            moves["ges"](k).start()
    moves["ges"](3).wait_recv()
    across(ge_own, ge_in, ge_zout, "gez", 3)
    for k in (2, 1, 0):
        moves["gss"](k).wait_recv()
        moves["ges"](k).wait_recv()

    d_mid = dtok[...] + collected(2)
    d_first, gain_sum, shift_sum = normalize_back(
        d_mid, norm1[...], rate1[:, 0:1], vfull[3:4, :]
    )
    dtok[...] = d_first
    d1g[0] = d_first.astype(jnp.bfloat16)
    offer("d1")
    apart[2:3, :] = jnp.sum(d_first, axis=0, keepdims=True)
    apart[3:4, :] = gain_sum
    apart[4:5, :] = shift_sum
    start("a")
    bpart[0:8, :] = jnp.zeros((8, width), jnp.float32)

    def attend_back(k, carry):
        take("d1", k)

        d_context = nt(d1g[k], flat(obuf[...])).astype(jnp.bfloat16)
        query, keys, values = (qkv[k, :, i * part : (i + 1) * part] for i in range(3))
        d_query, d_keys, d_values = [], [], []
        for h in heads:
            cols = slice(h * head, (h + 1) * head)
            probs = pbuf[k, h]
            d_values.append(tn(probs.astype(jnp.bfloat16), d_context[:, cols]))
            d_probs = nt(d_context[:, cols], values[:, cols])
            inner = jnp.sum(probs * d_probs, axis=-1, keepdims=True)
            d_scores = (probs * (d_probs - inner)).astype(jnp.bfloat16)
            d_query.append(factor * nn(d_scores, keys[:, cols]))
            d_keys.append(tn(d_scores, query[:, cols]))
        d_query = jnp.concatenate(d_query, axis=1)
        d_values = jnp.concatenate(d_values, axis=1)
        bpart[0:1, :part] += jnp.sum(d_query, axis=0, keepdims=True)
        bpart[1:2, :part] += jnp.sum(d_values, axis=0, keepdims=True)
        low = jnp.concatenate([d_query] + d_keys + [d_values], axis=1).astype(jnp.bfloat16)
        dproj[k] = low
        term = jnp.concatenate([nt(low, flat(tbuf[zz // 2, zz % 2])) for zz in range(PLANES)], axis=1)

        @pl.when(k > 0)
        def _():
            rsend[3, k - 1] = term.astype(jnp.bfloat16)
            moves["r4"](k).start()

        @pl.when(k == 0)
        def _():
            keep[...] = term
            across_far(gs_own, gs_in, gs_zout, gs_zin, "gsz")
            across(gs_own, gs_in, gs_zout, "gsz", 1)

        @pl.when(k == 1)
        def _():
            across_far(ge_own, ge_in, ge_zout, ge_zin, "gez")
            across(ge_own, ge_in, ge_zout, "gez", 1)

        return carry

    lax.fori_loop(0, 4, attend_back, 0)

    d_proj = flat(dproj[...])
    for half in range(2):
        for high in range(2):
            weigh_width(xg, d_proj, gt_own, gt_out, high, half)
        moves["gts"](half).start()
    d_first_all = flat(d1g[...])
    for zz in range(PLANES):
        pair = flat(ctx[...])[:, zz * head : (zz + 1) * head]
        term = tn(pair, d_first_all)
        first, second = term[: head // 2], term[head // 2 :]
        go_own[zz] = jnp.where(core == 0, first, second)
        go_out[zz] = jnp.where(core == 0, second, first).astype(jnp.bfloat16)
    start("gos")
    total = apart[...]
    for k in (1, 2, 3):
        moves["a"](k).wait_recv()
        total = total + ain[k - 1]
    bpart[0:8, :] += total
    start("bz")
    halves = (("gtz", slice(0, 2)), ("gty", slice(2, 4)))
    for half, (name, cut) in enumerate(halves):
        moves["gts"](half).wait_recv()
        across(gt_own, gt_in, gt_zout, name, 3, cut)
    arrive("gos")
    across(go_own, go_in, go_zout, "goz", 3)
    for name, cut in halves:
        across_far(gt_own, gt_in, gt_zout, gt_zin, name, cut)
        across(gt_own, gt_in, gt_zout, name, 1, cut)
    across(go_own, go_in, go_zout, "goz", 1)
    across_far(go_own, go_in, go_zout, go_zin, "goz")

    ig_ref[...] = (dtok[...] + collected(3)).astype(jnp.bfloat16)
    stores[1].start()
    sg_ref[...] = gathered_sum(gs_own, gs_in, gs_zin, "gsz")
    stores[5].start()

    def hand_out(total, pout, pin, name):
        low = total.astype(jnp.bfloat16)
        pout[...] = low
        pin[chip] = pout[chip]
        start(name)

    hand_out(gathered_sum(ge_own, ge_in, ge_zin, "gez"), ge_pout, ge_pin, "gep")
    total = bpart[...]
    for k in (1, 2, 3):
        moves["bz"](k).wait_recv()
        total = total + bin_[k - 1]
    bsum[...] = total
    start("bs")
    hand_out(gathered_sum(gt_own, gt_in, gt_zin, "gtz", "gty"), gt_pout, gt_pin, "gtp")
    og_ref[...] = gathered_sum(go_own, go_in, go_zin, "goz")
    stores[3].start()
    arrive("bs")
    bsum_all = bsum.at[...]

    def own_lanes(rows, block, at):
        cols = pl.ds(pl.multiple_of(block * 128, 128), 128)
        wide = bsum_all[rows, cols] + bsib[rows, cols]
        out = jnp.zeros((wide.shape[0], 32), jnp.float32)
        for i in range(4):
            out = out + jnp.where(at == i, wide[:, 32 * i : 32 * i + 32], 0.0)
        return out

    by_rows = own_lanes(
        slice(0, 8), lax.rem(plane, 2) + 2 * (chip // 2) + 4 * (plane // 2), by_row
    )
    by_heads = own_lanes(slice(0, 8), plane // 2, by_head)
    rows = lax.broadcasted_iota(jnp.int32, (8, 32), 0)
    small_ref[...] = jnp.where(rows < 2, by_heads, by_rows)
    cols = pl.ds(pl.multiple_of((plane * 2 + core) * 128, 128), 128)
    ebg_ref[...] = bsum[8:9, cols] + bsib[8:9, cols]
    arrive("gep")
    for other in range(CHIPS):
        for zz in range(PLANES):
            at = share(zz, other) * part
            eg_ref[:, at : at + part] = ge_pin[
                other, :, zz * part : (zz + 1) * part
            ].astype(jnp.float32)
    stores[4].start()
    arrive("gtp")
    holder = {share(zz, other): (zz, other) for zz in range(PLANES) for other in range(CHIPS)}
    for kind in range(3):
        for first in range(0, HEADS, 2):
            at = kind * width + first * piece
            tg_ref[:, at : at + 2 * piece] = jnp.concatenate(
                [
                    gt_pin[other, :, kind * part + zz * piece :][:, :piece]
                    for zz, other in (holder[first], holder[first + 1])
                ],
                axis=1,
            ).astype(jnp.float32)
    stores[2].start()
    for name in COPIES:
        for k in span(name):
            moves[name](k).wait_send()
    for store in stores:
        store.wait()


def hand_over(*refs):
    small_ref, ebg_ref = refs[6:8]
    outs = refs[8:-1]
    moved = [
        pltpu.make_async_copy(refs[i], outs[i], refs[-1].at[i]) for i in range(6)
    ]
    for item in moved:
        item.start()
    for i in range(8):
        outs[6 + i][...] = small_ref[i : i + 1, :]
    outs[14][...] = ebg_ref[...]
    for item in moved:
        item.wait()


def plane_body(
    inputs,
    live_keys,
    triple_weight,
    query_bias,
    value_bias,
    output_weight,
    output_bias,
    first_gain,
    first_shift,
    expand_weight,
    expand_bias,
    shrink_weight,
    shrink_bias,
    second_gain,
    second_shift,
    cotangent,
):
    rows, width = inputs.shape
    own = triple_weight.shape[0]
    part = width // PLANES
    hidden = expand_weight.shape[1] // CHIPS
    low, full = jnp.bfloat16, jnp.float32
    vectors = (
        query_bias,
        value_bias,
        output_bias,
        first_gain,
        first_shift,
        shrink_bias,
        second_gain,
        second_shift,
    )
    shrink = shrink_weight.shape[0]
    outs = (
        ((rows, width), low),
        ((rows, width), low),
        (triple_weight.shape, full),
        (output_weight.shape, full),
        (expand_weight.shape, full),
        (shrink_weight.shape, full),
        ((8, own), full),
        ((1, 128), full),
    )
    P4, C4 = PLANES, CHIPS
    scratch = [
        (triple_weight.shape, low),
        (expand_weight.shape, low),
        ((rows, width), low),
        ((1, rows), jnp.int32),
    ]
    scratch += [((1, own), low)] * 8 + [((1, shrink), low)] + list(outs[:6])
    scratch += [
        ((P4, C4, 2, 16, 128), full),
        ((16, width), full),
        ((16, part), full),
        ((8, hidden), full),
        ((C4, own, 3 * part), low),
        ((2, 2, 2, 2, 2, own, 3 * part), low),
        ((C4, own, hidden), low),
        ((2, 2, 2, 2, 2, own, hidden), low),
        ((P4, 2, own, width), low),
        ((P4, 2, shrink, width), low),
        ((C4, rows, width), low),
        ((C4, rows, width), low),
        ((C4, rows, width), low),
        ((C4, rows, width), low),
        ((4, 3, rows, width), low),
        ((4, 3, rows, width), low),
        ((rows, width), full),
        ((C4, rows, 3 * part), low),
        ((C4, P4, rows, rows), full),
        ((C4, rows, part), low),
        ((C4, rows, hidden), full),
        ((C4, rows, hidden), low),
        ((C4, rows, hidden), low),
        ((C4, rows, 3 * part), low),
        ((rows, width), full),
        ((rows, 128), full),
        ((rows, width), full),
        ((rows, width), full),
        ((P4, shrink, width), full),
        ((P4, shrink, width), low),
        ((P4, shrink, width), low),
        ((3, shrink, width), low),
        ((3, shrink, width), low),
        ((P4, C4, own, hidden), full),
        ((P4, C4, own, hidden), low),
        ((P4, C4, own, hidden), low),
        ((3, C4, own, hidden), low),
        ((3, C4, own, hidden), low),
        ((C4, own, hidden), low),
        ((C4, own, hidden), low),
        ((P4, own, width), full),
        ((P4, own, width), low),
        ((P4, own, width), low),
        ((3, own, width), low),
        ((3, own, width), low),
        ((P4, C4, own, 3 * part), full),
        ((P4, C4, own, 3 * part), low),
        ((P4, C4, own, 3 * part), low),
        ((3, C4, own, 3 * part), low),
        ((3, C4, own, 3 * part), low),
        ((C4, own, 3 * part), low),
        ((C4, own, 3 * part), low),
        ((8, width), full),
        ((3, 8, width), full),
        ((16, width), full),
        ((3, 16, width), full),
        ((16, width), full),
        ((16, width), full),
    ]
    anywhere = pl.BlockSpec(memory_space=pl.ANY)
    inside = pl.BlockSpec(memory_space=pltpu.VMEM)
    given = (
        inputs,
        live_keys[None, :],
        triple_weight,
        output_weight,
        expand_weight,
        shrink_weight,
        cotangent,
    )
    given += tuple(vector[None, :] for vector in vectors) + (expand_bias[None, :],)
    result = pl.pallas_call(
        plane_kernel,
        out_shape=[jax.ShapeDtypeStruct(*item) for item in outs],
        in_specs=[anywhere] * len(given),
        out_specs=[anywhere] * 6 + [inside] * 2,
        scratch_shapes=[pltpu.VMEM(*item) for item in scratch]
        + [pltpu.SemaphoreType.DMA((COPY_COUNT,))] * 2
        + [pltpu.SemaphoreType.DMA((16,)), pltpu.SemaphoreType.DMA((6,))],
        compiler_params=pltpu.CompilerParams(
            collective_id=0, has_side_effects=True, vmem_limit_bytes=60 * 2**20
        ),
        cost_estimate=pl.CostEstimate(
            flops=6 * rows * width * 12 * width,
            bytes_accessed=16 * 2**20,
            transcendentals=rows * hidden * 8,
        ),
        name="plane_layer",
    )(*given)
    ends = list(outs[:6]) + [((1, own), full)] * 8 + [((1, shrink), full)]
    done = pl.pallas_call(
        hand_over,
        out_shape=[jax.ShapeDtypeStruct(*item) for item in ends],
        in_specs=[inside] * 8,
        out_specs=[anywhere] * 6 + [inside] * 9,
        scratch_shapes=[pltpu.SemaphoreType.DMA((6,))],
        name="hand_over",
    )(*result)
    layer_out, input_grad, triple_grad, output_grad, expand_grad, shrink_grad = done[:6]
    small = [item[0] for item in done[6:]]
    return (
        layer_out,
        input_grad,
        triple_grad,
        small[0],
        small[1],
        output_grad,
        small[2],
        small[3],
        small[4],
        expand_grad,
        small[8],
        shrink_grad,
        small[5],
        small[6],
        small[7],
    )


def solution(mesh):
    placed = (
        P("fsdp", None),
        P("fsdp"),
        P("fsdp", None),
        P("fsdp"),
        P("fsdp"),
        P("fsdp", None),
        P("fsdp"),
        P("fsdp"),
        P("fsdp"),
        P("fsdp", None),
        P("fsdp"),
        P("fsdp", None),
        P("fsdp"),
        P("fsdp"),
        P("fsdp"),
        P("fsdp", None),
    )
    return jax.shard_map(
        plane_body if mesh.shape["fsdp"] == PLANES * GROUP else body,
        mesh=mesh,
        in_specs=placed,
        out_specs=(
            P("fsdp", None),
            P("fsdp", None),
            P("fsdp", None),
            P("fsdp"),
            P("fsdp"),
            P("fsdp", None),
            P("fsdp"),
            P("fsdp"),
            P("fsdp"),
            P("fsdp", None),
            P("fsdp"),
            P("fsdp", None),
            P("fsdp"),
            P("fsdp"),
            P("fsdp"),
        ),
        check_vma=False,
    )
```

```python
import jax
import jax.numpy as jnp
from jax import lax
from jax.experimental import pallas as pl
from jax.experimental.pallas import tpu as pltpu
from jax.sharding import PartitionSpec as P

HEADS = 16


EPSILON = 1e-05
NEGATIVE = -1e30
ROOT_HALF = 0.7071067811865476
INV_ROOT_TWO_PI = 0.3989422804014327


def batched(form, left, right):
    return jnp.einsum(form, left, right, preferred_element_type=jnp.float32)


def layer_norm(hidden, gain, shift):
    center = hidden - jnp.mean(hidden, axis=-1, keepdims=True)
    inv_std = lax.rsqrt(jnp.mean(center * center, axis=-1, keepdims=True) + EPSILON)
    normed = center * inv_std
    return (normed * gain.astype(jnp.float32) + shift.astype(jnp.float32), normed, inv_std)


def layer_norm_back(upstream, normed, inv_std, gain):
    scaled = upstream * gain.astype(jnp.float32)
    inner = (
        scaled
        - jnp.mean(scaled, axis=-1, keepdims=True)
        - normed * jnp.mean(scaled * normed, axis=-1, keepdims=True)
    )
    return (inv_std * inner, jnp.sum(upstream * normed, axis=0), jnp.sum(upstream, axis=0))


def normal_cdf(values):
    return 0.5 * (1.0 + lax.erf(values * ROOT_HALF))


def masked_scores(query, keys, live):
    scores = batched("qhd,khd->hqk", query, keys)
    allowed = live == 1
    return jnp.where(allowed[None, None, :], scores, NEGATIVE)


def forward(params, tokens, live):
    (
        triple_weight,
        query_bias,
        value_bias,
        output_weight,
        output_bias,
        first_gain,
        first_shift,
        expand_weight,
        expand_bias,
        shrink_weight,
        shrink_bias,
        second_gain,
        second_shift,
    ) = params
    row_count = tokens.shape[0]
    width_all = tokens.shape[1]
    head_size = width_all // HEADS
    factor = head_size ** (-0.5)
    projected = jnp.dot(tokens, triple_weight, preferred_element_type=jnp.float32)
    query = ((projected[:, :width_all] + query_bias.astype(jnp.float32)) * factor).astype(
        jnp.bfloat16
    )
    keys = projected[:, width_all : 2 * width_all].astype(jnp.bfloat16)
    values = (projected[:, 2 * width_all :] + value_bias.astype(jnp.float32)).astype(jnp.bfloat16)
    query = query.reshape(row_count, HEADS, head_size)
    keys = keys.reshape(row_count, HEADS, head_size)
    values = values.reshape(row_count, HEADS, head_size)
    scores = masked_scores(query, keys, live)
    top = jnp.max(scores, axis=-1, keepdims=True)
    expo = jnp.exp(scores - top)
    total = jnp.sum(expo, axis=-1, keepdims=True)
    log_total = top + jnp.log(total)
    probs = (expo / total).astype(jnp.bfloat16)
    context = (
        batched("hqk,khd->qhd", probs, values).astype(jnp.bfloat16).reshape(row_count, width_all)
    )
    first_in = (
        tokens.astype(jnp.float32)
        + jnp.dot(context, output_weight, preferred_element_type=jnp.float32)
        + output_bias.astype(jnp.float32)
    )
    middle, first_norm, first_rate = layer_norm(first_in, first_gain, first_shift)
    mid_low = middle.astype(jnp.bfloat16)
    pre_act = jnp.dot(
        mid_low, expand_weight, preferred_element_type=jnp.float32
    ) + expand_bias.astype(jnp.float32)
    act_low = (pre_act * normal_cdf(pre_act)).astype(jnp.bfloat16)
    second_in = (
        middle
        + jnp.dot(act_low, shrink_weight, preferred_element_type=jnp.float32)
        + shrink_bias.astype(jnp.float32)
    )
    result, second_norm, second_rate = layer_norm(second_in, second_gain, second_shift)
    saved = (
        tokens,
        live,
        query,
        keys,
        values,
        log_total,
        context,
        first_norm,
        first_rate,
        mid_low,
        pre_act,
        act_low,
        second_norm,
        second_rate,
    )
    return (result.astype(jnp.bfloat16), saved)


def back_upper(params, saved, upstream):
    (
        triple_weight,
        query_bias,
        value_bias,
        output_weight,
        output_bias,
        first_gain,
        first_shift,
        expand_weight,
        expand_bias,
        shrink_weight,
        shrink_bias,
        second_gain,
        second_shift,
    ) = params
    (
        tokens,
        live,
        query,
        keys,
        values,
        log_total,
        context,
        first_norm,
        first_rate,
        mid_low,
        pre_act,
        act_low,
        second_norm,
        second_rate,
    ) = saved
    d_second, second_gain_grad, second_shift_grad = layer_norm_back(
        upstream.astype(jnp.float32), second_norm, second_rate, second_gain
    )
    d_second_low = d_second.astype(jnp.bfloat16)
    shrink_bias_grad = jnp.sum(d_second, axis=0)
    d_act = jnp.dot(d_second_low, shrink_weight.T, preferred_element_type=jnp.float32)
    slope = normal_cdf(pre_act) + pre_act * jnp.exp(-0.5 * pre_act * pre_act) * INV_ROOT_TWO_PI
    d_pre = d_act * slope
    expand_bias_grad = jnp.sum(d_pre, axis=0)
    d_pre_low = d_pre.astype(jnp.bfloat16)
    d_mid = d_second + jnp.dot(d_pre_low, expand_weight.T, preferred_element_type=jnp.float32)
    d_first, first_gain_grad, first_shift_grad = layer_norm_back(
        d_mid, first_norm, first_rate, first_gain
    )
    small = (
        first_gain_grad,
        first_shift_grad,
        expand_bias_grad,
        shrink_bias_grad,
        second_gain_grad,
        second_shift_grad,
    )
    pairs = ((mid_low, d_pre_low), (act_low, d_second_low))
    return (small, pairs, d_first)


def back_lower(params, saved, d_first):
    (
        triple_weight,
        query_bias,
        value_bias,
        output_weight,
        output_bias,
        first_gain,
        first_shift,
        expand_weight,
        expand_bias,
        shrink_weight,
        shrink_bias,
        second_gain,
        second_shift,
    ) = params
    (
        tokens,
        live,
        query,
        keys,
        values,
        log_total,
        context,
        first_norm,
        first_rate,
        mid_low,
        pre_act,
        act_low,
        second_norm,
        second_rate,
    ) = saved
    row_count = tokens.shape[0]
    width_all = tokens.shape[1]
    head_size = width_all // HEADS
    factor = head_size ** (-0.5)
    d_first_low = d_first.astype(jnp.bfloat16)
    output_bias_grad = jnp.sum(d_first, axis=0)
    d_context = jnp.dot(d_first_low, output_weight.T, preferred_element_type=jnp.float32).astype(
        jnp.bfloat16
    )
    d_context = d_context.reshape(row_count, HEADS, head_size)
    scores = masked_scores(query, keys, live)
    probs = jnp.exp(scores - log_total)
    probs_low = probs.astype(jnp.bfloat16)
    d_values = batched("hqk,qhd->khd", probs_low, d_context)
    d_probs = batched("qhd,khd->hqk", d_context, values)
    inner = jnp.sum(probs * d_probs, axis=-1, keepdims=True)
    d_scores = (probs * (d_probs - inner)).astype(jnp.bfloat16)
    d_query = factor * batched("hqk,khd->qhd", d_scores, keys)
    d_keys = batched("hqk,qhd->khd", d_scores, query)
    d_query = d_query.reshape(row_count, width_all)
    d_keys = d_keys.reshape(row_count, width_all)
    d_values = d_values.reshape(row_count, width_all)
    d_proj = jnp.concatenate([d_query, d_keys, d_values], axis=1).astype(jnp.bfloat16)
    query_bias_grad = jnp.sum(d_query, axis=0)
    value_bias_grad = jnp.sum(d_values, axis=0)
    input_grad = (
        d_first + jnp.dot(d_proj, triple_weight.T, preferred_element_type=jnp.float32)
    ).astype(jnp.bfloat16)
    small = (query_bias_grad, value_bias_grad, output_bias_grad)
    pairs = ((tokens, d_proj), (context, d_first_low))
    return (small, pairs, input_grad)


def swap(value, bit, count):
    return lax.ppermute(value, "fsdp", [(i, i ^ (1 << bit)) for i in range(count)])


def own_bit(bit):
    return (lax.axis_index("fsdp") >> bit) & 1


def place(base, value, places, levels):
    starts = [0] * base.ndim
    for bit, at in places:
        starts[levels - 1 - bit] = at
    return lax.dynamic_update_slice(base, value, starts)


def grown(value, bits, levels):
    shape = list(value.shape)
    for bit in bits:
        shape[levels - 1 - bit] = 2
    return jnp.zeros(shape, value.dtype)


def join(own, other, bit, levels):
    mine = own_bit(bit)
    base = place(grown(own, (bit,), levels), own, ((bit, mine),), levels)
    return place(base, other, ((bit, 1 - mine),), levels)


def orders(levels):
    ring = list(range(1, levels))
    return [ring[k * len(ring) // 3 :] + ring[: k * len(ring) // 3] for k in range(3)]


def collect(shard, order, count):
    levels = count.bit_length() - 1
    held = shard.reshape((1,) * levels + shard.shape)
    steps = list(reversed(order))
    for bit in steps[:-1]:
        held = join(held, swap(held, bit, count), bit, levels)
    bit = steps[-1]
    across = swap(held, bit, count)
    beside = swap(held, 0, count)
    corner = swap(across, 0, count)
    mine, core = own_bit(bit), own_bit(0)
    full = grown(held, (bit, 0), levels)
    full = place(full, held, ((bit, mine), (0, core)), levels)
    full = place(full, beside, ((bit, mine), (0, 1 - core)), levels)
    full = place(full, across, ((bit, 1 - mine), (0, core)), levels)
    held = place(full, corner, ((bit, 1 - mine), (0, 1 - core)), levels)
    return held.reshape((count * shard.shape[0],) + shard.shape[1:])


def halve(terms, order, count, last):
    levels = count.bit_length() - 1
    for bit in order:
        axis = terms.ndim - 3 - bit if last else terms.ndim - 2 - bit
        mine = own_bit(bit)
        keep = lax.dynamic_slice_in_dim(terms, mine, 1, axis)
        send = lax.dynamic_slice_in_dim(terms, 1 - mine, 1, axis)
        total = keep.astype(jnp.float32) + swap(send, bit, count).astype(jnp.float32)
        terms = total if bit == order[-1] else total.astype(terms.dtype)
    return terms.reshape(terms.shape[-2:])


def by_core(left, count):
    parts = left.reshape(left.shape[0], count // 2, 2, left.shape[1] // count)
    core = own_bit(0)
    pick = lambda at: lax.dynamic_index_in_dim(parts, at, 2, keepdims=False).reshape(
        left.shape[0], left.shape[1] // 2
    )
    return (pick(core), pick(1 - core))


def pair_up(left, right, count):
    mine, other = by_core(left, count)
    return (
        jnp.concatenate([mine, swap(other, 0, count)], axis=0),
        jnp.concatenate([right, swap(right, 0, count)], axis=0),
    )


def summed_grad(left, right, pieces, count):
    levels = count.bit_length() - 1
    results = []
    offset = 0
    for extent, order in pieces:
        term = jnp.einsum(
            "tk,tw->kw",
            left,
            right[:, offset : offset + extent],
            preferred_element_type=jnp.float32,
        ).astype(jnp.bfloat16)
        term = term.reshape((2,) * (levels - 1) + (left.shape[1] * 2 // count, extent))
        results.append(halve(term, order, count, False))
        offset = offset + extent
    return results[0] if len(results) == 1 else jnp.concatenate(results, axis=1)


def body(
    inputs,
    live_keys,
    triple_weight,
    query_bias,
    value_bias,
    output_weight,
    output_bias,
    first_gain,
    first_shift,
    expand_weight,
    expand_bias,
    shrink_weight,
    shrink_bias,
    second_gain,
    second_shift,
    cotangent,
):
    count = lax.axis_size("fsdp")
    levels = count.bit_length() - 1
    width = inputs.shape[1]
    ways = orders(levels)
    vectors = (
        query_bias,
        value_bias,
        output_bias,
        first_gain,
        first_shift,
        expand_bias,
        shrink_bias,
        second_gain,
        second_shift,
    )
    packed = collect(jnp.concatenate(vectors)[None, :], ways[0], count)
    wide = []
    offset = 0
    for vector in vectors:
        wide.append(packed[:, offset : offset + vector.shape[0]].reshape(-1))
        offset = offset + vector.shape[0]
    gathered = (
        collect(triple_weight, ways[2], count),
        wide[0],
        wide[1],
        collect(output_weight, ways[0], count),
        wide[2],
        wide[3],
        wide[4],
        collect(expand_weight, ways[0], count),
        wide[5],
        collect(shrink_weight, ways[1], count),
        wide[6],
        wide[7],
        wide[8],
    )
    layer_out, saved = forward(gathered, inputs, live_keys)
    upper_small, upper_pairs, d_first = back_upper(gathered, saved, cotangent)
    lower_small, lower_pairs, input_grad = back_lower(gathered, saved, d_first)
    hidden = expand_weight.shape[1]
    shrink_grad = summed_grad(
        *pair_up(*upper_pairs[1], count),
        ((width * 3 // 4, ways[1]), (width // 4, ways[2])),
        count,
    )
    expand_grad = summed_grad(
        *pair_up(*upper_pairs[0], count),
        ((hidden * 3 // 4, ways[0]), (hidden // 4, ways[2])),
        count,
    )
    output_grad = summed_grad(*pair_up(*lower_pairs[1], count), ((width, ways[1]),), count)
    triple_grad = summed_grad(
        *pair_up(*lower_pairs[0], count),
        ((width, ways[0]), (width, ways[1]), (width, ways[2])),
        count,
    )
    sums = lower_small + upper_small
    terms = jnp.concatenate([item.reshape(count, -1) for item in sums], axis=1)
    terms = terms.reshape((2,) * levels + (1, terms.shape[1]))
    owned = halve(terms, list(range(levels)), count, True)[0]
    small = []
    offset = 0
    for item in sums:
        extent = item.shape[0] // count
        small.append(owned[offset : offset + extent])
        offset = offset + extent
    return (
        layer_out,
        input_grad,
        triple_grad,
        small[0],
        small[1],
        output_grad,
        small[2],
        small[3],
        small[4],
        expand_grad,
        small[5],
        shrink_grad,
        small[6],
        small[7],
        small[8],
    )


PLANES = 4
CHIPS = 4
GROUP = 2 * CHIPS
MESH = pl.DeviceIdType.MESH


def nn(left, right):
    return lax.dot_general(
        left, right, (((1,), (0,)), ((), ())), preferred_element_type=jnp.float32
    )


def nt(left, right):
    return lax.dot_general(
        left, right, (((1,), (1,)), ((), ())), preferred_element_type=jnp.float32
    )


def tn(left, right):
    return lax.dot_general(
        left, right, (((0,), (0,)), ((), ())), preferred_element_type=jnp.float32
    )


def share(plane, chip):
    return chip % 2 + 2 * (plane % 2) + 4 * (chip // 2) + 8 * (plane // 2)


def flat(value):
    return value.reshape((-1, value.shape[-1]))


def normalize(hidden):
    center = hidden - jnp.mean(hidden, axis=-1, keepdims=True)
    rate = lax.rsqrt(jnp.mean(center * center, axis=-1, keepdims=True) + EPSILON)
    return center * rate, rate


def normalize_back(upstream, normed, rate, gain):
    scaled = upstream * gain
    inner = (
        scaled
        - jnp.mean(scaled, axis=-1, keepdims=True)
        - normed * jnp.mean(scaled * normed, axis=-1, keepdims=True)
    )
    return (
        rate * inner,
        jnp.sum(upstream * normed, axis=0, keepdims=True),
        jnp.sum(upstream, axis=0, keepdims=True),
    )


COPIES = {}
COPY_COUNT = 0
for _names, _ks in (
    (("v", "vz", "t", "tz", "tw", "e", "ez", "oz", "sz", "x"), (1, 2, 3)),
    (("r1", "r2", "r3", "r4", "gsz", "gez", "goz", "gtz", "gty", "gep", "gtp", "a", "bz"), (1, 2, 3)),
    (("m", "d2", "d1"), (1, 2, 3, 4, 5, 6)),
    (("ts", "es", "os", "ss", "gss", "ges"), (0, 1, 2, 3)),
    (("gts",), (0, 1)),
    (("vs", "gos", "bs"), (0,)),
):
    for _name in _names:
        COPIES[_name] = (COPY_COUNT - _ks[0], _ks)
        COPY_COUNT += len(_ks)


def plane_kernel(
    x_hbm, live_hbm, t_hbm, o_hbm, e_hbm, s_hbm, ct_hbm,
    vec0, vec1, vec2, vec3, vec4, vec5, vec6, vec7, eb_hbm,
    lo_hbm, ig_hbm, tg_hbm, og_hbm, eg_hbm, sg_hbm, small_ref, ebg_ref,
    t_ref, e_ref, ct_ref, live_ref, low0, low1, low2, low3, low4, low5, low6, low7, eb_ref,
    lo_ref, ig_ref, tg_ref, og_ref, eg_ref, sg_ref, vbuf, vfull, vchip, vhid, tsend, tbuf, esend, ebuf, obuf, sbuf, xg, mg, d2g, d1g,
    rsend, rrecv, keep, qkv, pbuf, ctx, slope, act, dpre, dproj, norm1, rate1, mid, dtok,
    gs_own, gs_out, gs_in, gs_zout, gs_zin,
    ge_own, ge_out, ge_in, ge_zout, ge_zin, ge_pout, ge_pin,
    go_own, go_out, go_in, go_zout, go_zin,
    gt_own, gt_out, gt_in, gt_zout, gt_zin, gt_pout, gt_pin,
    apart, ain, bpart, bin_, bsum, bsib, send_sem, recv_sem, load_sem, store_sem,
):
    me = lax.axis_index("fsdp")
    core = lax.rem(me, 2)
    chip = lax.rem(me // 2, 2) + 2 * lax.rem(me // 8, 2)
    plane = lax.rem(me // 4, 2) + 2 * (me // 16)
    sibling = me + 1 - 2 * core

    def flip(base, k):
        return lax.rem(base + k, 2) + 2 * lax.rem(base // 2 + k // 2, 2)

    def chip_at(k):
        return flip(chip, k)

    def plane_at(k):
        return flip(plane, k)

    def device_of(plane, chip, core):
        high = 16 * (plane // 2) + 8 * (chip // 2)
        return high + 4 * lax.rem(plane, 2) + 2 * lax.rem(chip, 2) + core

    def mate(k):
        return device_of(plane, chip_at(k), core)

    def above(k):
        return device_of(plane_at(k), chip, core)

    def rows_of(plane, chip):
        return plane // 2, chip // 2, lax.rem(plane, 2), lax.rem(chip, 2), core

    def plane_rows(plane, half=slice(None)):
        return plane // 2, half, lax.rem(plane, 2), slice(None), core

    def origin(k):
        return plane_at(2) if k == 3 else plane

    def onward(k):
        return above(1) if k == 3 else above(k)

    def copy(name, k, source, target, device):
        spot = COPIES[name][0] + k
        return pltpu.make_async_remote_copy(
            src_ref=source,
            dst_ref=target,
            send_sem=send_sem.at[spot],
            recv_sem=recv_sem.at[spot],
            device_id=(device,),
            device_id_type=MESH,
        )

    def shared(name, k, held):
        half = held.shape[1] // 2
        first, last = slice(0, half), slice(half, 2 * half)
        rows = first if k in (1, 3, 6) else last
        if k in (3, 4):
            return copy(name, k, held.at[k - 2, rows], held.at[3, rows], mate(5 - k))
        to = 1 if k in (1, 5) else 2
        return copy(name, k, held.at[0, rows], held.at[to, rows], mate(to))

    moves = {
        "v": lambda k: copy(
            "v", k, vbuf.at[plane, chip, core], vbuf.at[plane, chip, core], mate(k)
        ),
        "vz": lambda k: copy(
            "vz", k, vbuf.at[plane, :, core], vbuf.at[plane, :, core], above(k)
        ),
        "vs": lambda k: copy("vs", 0, vbuf.at[:, :, core], vbuf.at[:, :, core], sibling),
        "t": lambda k: copy(
            "t", k, tsend.at[chip_at(k)], tbuf.at[*rows_of(plane, chip)], mate(k)
        ),
        "tz": lambda k: copy(
            "tz",
            k,
            tbuf.at[*plane_rows(origin(k), 0)],
            tbuf.at[*plane_rows(origin(k), 0)],
            onward(k),
        ),
        "ts": lambda k: copy(
            "ts",
            k,
            tbuf.at[*plane_rows(plane_at(k))],
            tbuf.at[*plane_rows(plane_at(k))],
            sibling,
        ),
        "e": lambda k: copy(
            "e", k, esend.at[chip_at(k)], ebuf.at[*rows_of(plane, chip)], mate(k)
        ),
        "ez": lambda k: copy(
            "ez",
            k,
            ebuf.at[*plane_rows(origin(k))],
            ebuf.at[*plane_rows(origin(k))],
            onward(k),
        ),
        "es": lambda k: copy(
            "es",
            k,
            ebuf.at[*plane_rows(plane_at(k))],
            ebuf.at[*plane_rows(plane_at(k))],
            sibling,
        ),
        "oz": lambda k: copy(
            "oz", k, obuf.at[origin(k), core], obuf.at[origin(k), core], onward(k)
        ),
        "os": lambda k: copy(
            "os", k, obuf.at[plane_at(k), core], obuf.at[plane_at(k), core], sibling
        ),
        "sz": lambda k: copy(
            "sz", k, sbuf.at[origin(k), core], sbuf.at[origin(k), core], onward(k)
        ),
        "ss": lambda k: copy(
            "ss", k, sbuf.at[plane_at(k), core], sbuf.at[plane_at(k), core], sibling
        ),
        "tw": lambda k: copy(
            "tw",
            k,
            tbuf.at[*plane_rows(origin(k), 1)],
            tbuf.at[*plane_rows(origin(k), 1)],
            onward(k),
        ),
        "x": lambda k: copy(
            "x", k, xg.at[2 if k == 3 else 0], xg.at[k], mate(1 if k == 3 else k)
        ),
        "m": lambda k: shared("m", k, mg),
        "d2": lambda k: shared("d2", k, d2g),
        "d1": lambda k: shared("d1", k, d1g),
        "gss": lambda k: copy(
            "gss", k, gs_out.at[plane_at(k)], gs_in.at[plane_at(k)], sibling
        ),
        "ges": lambda k: copy(
            "ges", k, ge_out.at[plane_at(k)], ge_in.at[plane_at(k)], sibling
        ),
        "gos": lambda k: copy("gos", 0, go_out, go_in, sibling),
        "gts": lambda k: copy(
            "gts", k, gt_out.at[:, 2 * k : 2 * k + 2], gt_in.at[:, 2 * k : 2 * k + 2], sibling
        ),
        "gsz": lambda k: copy("gsz", k, gs_zout.at[k - 1], gs_zin.at[k - 1], onward(k)),
        "gez": lambda k: copy("gez", k, ge_zout.at[k - 1], ge_zin.at[k - 1], onward(k)),
        "goz": lambda k: copy("goz", k, go_zout.at[k - 1], go_zin.at[k - 1], onward(k)),
        "gtz": lambda k: copy(
            "gtz", k, gt_zout.at[k - 1, 0:2], gt_zin.at[k - 1, 0:2], onward(k)
        ),
        "gty": lambda k: copy(
            "gty", k, gt_zout.at[k - 1, 2:4], gt_zin.at[k - 1, 2:4], onward(k)
        ),
        "gep": lambda k: copy("gep", k, ge_pout.at[chip_at(k)], ge_pin.at[chip], mate(k)),
        "gtp": lambda k: copy("gtp", k, gt_pout.at[chip_at(k)], gt_pin.at[chip], mate(k)),
        "a": lambda k: copy("a", k, apart, ain.at[k - 1], mate(k)),
        "bz": lambda k: copy("bz", k, bpart, bin_.at[k - 1], above(k)),
        "bs": lambda k: copy("bs", 0, bsum, bsib, sibling),
    }
    for turn in range(4):
        name = "r%d" % (turn + 1)
        moves[name] = lambda k, name=name, turn=turn: copy(
            name, k, rsend.at[turn, k - 1], rrecv.at[turn, k - 1], mate(k)
        )
    moves["r1"] = lambda k: copy(
        "r1", k, rsend.at[0, k - 1], rrecv.at[0, k - 1], mate(1 if k == 3 else k)
    )

    def span(name):
        return COPIES[name][1]

    def start(name):
        for k in span(name):
            moves[name](k).start()

    def arrive(name):
        for k in span(name):
            moves[name](k).wait_recv()

    def send_out(name):
        moves[name](2).start()
        moves[name](1).start()

    def pass_on(name, beside):
        moves[name](2).wait_recv()
        moves[name](3).start()
        moves[beside](2).start()

    def take_in(name, beside):
        for k in (1, 3):
            moves[name](k).wait_recv()
            moves[beside](k).start()

    def take(name, k):
        @pl.when(k == 1)
        def _():
            for i in (1, 2):
                moves[name](i).wait_recv()
                moves[name](i + 2).start()
            moves[name](5).wait_recv()

        @pl.when(k == 2)
        def _():
            moves[name](6).wait_recv()

        @pl.when(k == 3)
        def _():
            moves[name](3).wait_recv()
            moves[name](4).wait_recv()

    def offer(name):
        for k in (1, 2, 5, 6):
            moves[name](k).start()

    barrier = pltpu.get_barrier_semaphore()
    for k in range(1, 4):
        for device in (mate(k), above(k)):
            pl.semaphore_signal(barrier, inc=1, device_id=(device,), device_id_type=MESH)
    pl.semaphore_signal(barrier, inc=1, device_id=(sibling,), device_id_type=MESH)

    sources = (
        t_hbm, vec0, vec1, vec2, vec3, vec4, vec5, vec6, vec7, eb_hbm, live_hbm,
        e_hbm, x_hbm, o_hbm, s_hbm, ct_hbm,
    )
    targets = (
        t_ref, low0, low1, low2, low3, low4, low5, low6, low7, eb_ref, live_ref,
        e_ref, xg.at[0], obuf.at[plane, core], sbuf.at[plane, core], ct_ref,
    )
    loads = [
        pltpu.make_async_copy(source, target, load_sem.at[i])
        for i, (source, target) in enumerate(zip(sources, targets))
    ]
    for load in loads:
        load.start()
    pairs = (
        (lo_ref, lo_hbm), (ig_ref, ig_hbm), (tg_ref, tg_hbm), (og_ref, og_hbm),
        (eg_ref, eg_hbm), (sg_ref, sg_hbm),
    )
    stores = [
        pltpu.make_async_copy(source, target, store_sem.at[i])
        for i, (source, target) in enumerate(pairs)
    ]

    for load in loads[:11]:
        load.wait()
    row = lax.broadcasted_iota(jnp.int32, (8, 32), 0)
    vec = jnp.zeros((8, 32), jnp.float32)
    for i, item in enumerate((low0, low1, low2, low3, low4, low5, low6, low7)):
        vec = jnp.where(row == i, item[...].astype(jnp.float32), vec)
    lane = lax.broadcasted_iota(jnp.int32, (8, 128), 1) // 32
    row = lax.broadcasted_iota(jnp.int32, (8, 128), 0)
    by_row = lax.rem(chip, 2) * 2 + core
    by_head = lax.rem(plane, 2) * 2 + core
    spread = jnp.concatenate([vec, vec, vec, vec], axis=1)
    spread = jnp.where(lane == jnp.where(row < 2, by_head, by_row), spread, 0.0)
    own_rows = vbuf.at[plane, chip, core]
    own_rows[0:8, :] = spread
    own_rows[8:9, :] = eb_ref[...].astype(jnp.float32)
    own_rows[9:10, :] = live_ref[...].astype(jnp.float32)
    own_rows[10:16, :] = jnp.zeros((6, 128), jnp.float32)
    width = x_hbm.shape[1]
    part = width // PLANES
    piece = part // CHIPS
    for other in range(CHIPS):
        tsend[other] = jnp.concatenate(
            [
                t_ref[:, kind * width + share(zz, other) * piece :][:, :piece]
                for kind in range(3)
                for zz in range(PLANES)
            ],
            axis=1,
        )
    tbuf[rows_of(plane, chip)] = tsend[chip]
    for load in loads[12:15]:
        load.wait()
    pl.semaphore_wait(barrier, 7)

    start("t")
    start("v")
    loads[11].wait()
    for other in range(CHIPS):
        for zz in range(PLANES):
            esend[other, :, zz * part : (zz + 1) * part] = e_ref[
                :, share(zz, other) * part : (share(zz, other) + 1) * part
            ]
    ebuf[rows_of(plane, chip)] = esend[chip]
    moves["os"](0).start()
    moves["ss"](0).start()
    arrive("t")
    send_out("tz")
    send_out("tw")
    moves["x"](1).start()
    moves["x"](2).start()
    moves["ts"](0).start()
    start("e")
    arrive("v")
    start("vz")
    moves["tz"](2).wait_recv()
    moves["tz"](3).start()
    moves["x"](2).wait_recv()
    moves["x"](3).start()
    moves["tw"](2).wait_recv()
    moves["tw"](3).start()
    moves["ts"](2).start()
    send_out("oz")
    arrive("e")
    moves["ez"](2).start()
    moves["sz"](2).start()
    moves["es"](0).start()
    arrive("vz")
    start("vs")
    for k in (1, 3):
        moves["tz"](k).wait_recv()
        moves["tw"](k).wait_recv()
        moves["ts"](k).start()
    pass_on("oz", "os")
    moves["ez"](1).start()
    moves["sz"](1).start()
    arrive("vs")
    for block in range(8):
        total = None
        for i in range(4):
            near = block % 2 + 2 * (block // 4)
            term = vbuf[near, i // 2 + 2 * (block // 2 % 2), i % 2]
            total = term if total is None else total + term
        vfull[:, 128 * block : 128 * block + 128] = total
        vhid[:, 128 * block : 128 * block + 128] = vbuf[block // 2, chip, block % 2][8:16]
    for half in range(2):
        vchip[:, 128 * half : 128 * half + 128] = (
            vbuf[2 * half, chip, 0]
            + vbuf[2 * half, chip, 1]
            + vbuf[2 * half + 1, chip, 0]
            + vbuf[2 * half + 1, chip, 1]
        )
    take_in("oz", "os")
    arrive("os")
    arrive("ts")

    head = width // HEADS
    factor = head ** (-0.5)
    heads = range(PLANES)

    moves["x"](1).wait_recv()
    moves["x"](3).wait_recv()

    def attend(step, carry):
        k = 3 - step
        tokens = xg[k]
        proj = nn(tokens[:, :part], flat(tbuf[0, 0]))
        for zz in range(1, PLANES):
            proj = proj + nn(tokens[:, zz * part : (zz + 1) * part], flat(tbuf[zz // 2, zz % 2]))
        query = ((proj[:, :part] + vchip[0:1, :]) * factor).astype(jnp.bfloat16)
        keys = proj[:, part : 2 * part].astype(jnp.bfloat16)
        values = (proj[:, 2 * part :] + vchip[1:2, :]).astype(jnp.bfloat16)
        qkv[k, :, :part] = query
        qkv[k, :, part : 2 * part] = keys
        qkv[k, :, 2 * part :] = values
        live = vbuf[plane, chip_at(k), core][9:10, :] > 0.5
        joined = []
        for h in heads:
            cols = slice(h * head, (h + 1) * head)
            scores = jnp.where(live, nt(query[:, cols], keys[:, cols]), NEGATIVE)
            expo = jnp.exp(scores - jnp.max(scores, axis=-1, keepdims=True))
            probs = expo / jnp.sum(expo, axis=-1, keepdims=True)
            pbuf[k, h] = probs
            joined.append(nn(probs.astype(jnp.bfloat16), values[:, cols]))
        context = jnp.concatenate(joined, axis=1).astype(jnp.bfloat16)
        ctx[k] = context
        term = nn(context, flat(obuf[...]))

        @pl.when(k == 0)
        def _():
            keep[...] = term

        @pl.when(k == 1)
        def _():
            rsend[0, 0] = term.astype(jnp.bfloat16)
            moves["r1"](1).start()

        @pl.when(k == 2)
        def _():
            mid[...] = term
            pass_on("ez", "es")

        @pl.when(k == 3)
        def _():
            rsend[0, 2] = term.astype(jnp.bfloat16)
            moves["r1"](3).start()

        return carry

    lax.fori_loop(0, 4, attend, 0)
    moves["r1"](3).wait_recv()
    rsend[0, 1] = (mid[...] + rrecv[0, 2].astype(jnp.float32)).astype(jnp.bfloat16)
    moves["r1"](2).start()
    pass_on("sz", "ss")

    def collected(turn):
        total = keep[...]
        for k in (1, 2, 3) if turn else (1, 2):
            moves["r%d" % (turn + 1)](k).wait_recv()
            total = total + rrecv[turn, k - 1].astype(jnp.float32)
        return total

    first_in = xg[0].astype(jnp.float32) + collected(0) + vfull[2:3, :]
    normed, rate = normalize(first_in)
    norm1[...] = normed
    rate1[...] = jnp.broadcast_to(rate, rate1.shape)
    middle = normed * vfull[3:4, :] + vfull[4:5, :]
    mid[...] = middle
    mg[0] = middle.astype(jnp.bfloat16)
    offer("m")

    take_in("ez", "es")
    arrive("es")

    def feed(k, carry):
        take("m", k)

        low = mg[k]
        pre = vhid[0:1, :] + nn(low[:, :part], flat(ebuf[0, 0]))
        for zz in range(1, PLANES):
            pre = pre + nn(low[:, zz * part : (zz + 1) * part], flat(ebuf[zz // 2, zz % 2]))
        cdf = normal_cdf(pre)
        slope[k] = cdf + pre * jnp.exp(-0.5 * pre * pre) * INV_ROOT_TWO_PI
        active = (pre * cdf).astype(jnp.bfloat16)
        act[k] = active

        @pl.when(k == 0)
        def _():
            take_in("sz", "ss")
            arrive("ss")

        term = nn(active[:, :part], flat(sbuf[0]))
        for zz in range(1, PLANES):
            term = term + nn(active[:, zz * part : (zz + 1) * part], flat(sbuf[zz]))

        @pl.when(k > 0)
        def _():
            rsend[1, k - 1] = term.astype(jnp.bfloat16)
            moves["r2"](k).start()

        @pl.when(k == 0)
        def _():
            keep[...] = term

        return carry

    lax.fori_loop(0, 4, feed, 0)

    second_in = mid[...] + collected(1) + vfull[5:6, :]
    normed, rate = normalize(second_in)
    lo_ref[...] = (normed * vfull[6:7, :] + vfull[7:8, :]).astype(jnp.bfloat16)
    stores[0].start()
    loads[15].wait()
    d_second, gain_sum, shift_sum = normalize_back(
        ct_ref[...].astype(jnp.float32), normed, rate, vfull[6:7, :]
    )
    dtok[...] = d_second
    d2g[0] = d_second.astype(jnp.bfloat16)
    offer("d2")
    apart[0:2, :] = jnp.zeros((2, width), jnp.float32)
    apart[5:6, :] = jnp.sum(d_second, axis=0, keepdims=True)
    apart[6:7, :] = gain_sum
    apart[7:8, :] = shift_sum
    bpart[8:16, :] = jnp.zeros((8, width), jnp.float32)

    def feed_back(k, carry):
        take("d2", k)

        low = d2g[k]
        d_act = jnp.concatenate([nt(low, flat(sbuf[zz])) for zz in range(PLANES)], axis=1)
        d_pre = d_act * slope[k]
        bpart[8:9, :] += jnp.sum(d_pre, axis=0, keepdims=True)
        d_pre_low = d_pre.astype(jnp.bfloat16)
        dpre[k] = d_pre_low
        term = jnp.concatenate([nt(d_pre_low, flat(ebuf[zz // 2, zz % 2])) for zz in range(PLANES)], axis=1)

        @pl.when(k > 0)
        def _():
            rsend[2, k - 1] = term.astype(jnp.bfloat16)
            moves["r3"](k).start()

        @pl.when(k == 0)
        def _():
            keep[...] = term

        return carry

    lax.fori_loop(0, 4, feed_back, 0)

    def mine(term, axis):
        first, second = lax.index_in_dim(term, 0, axis, False), lax.index_in_dim(term, 1, axis, False)
        return (
            jnp.where(core == 0, first, second),
            jnp.where(core == 0, second, first).astype(jnp.bfloat16),
        )

    def columns(left, zz):
        return flat(left[:, :, pl.ds(pl.multiple_of(zz * part, 128), part)])

    def weigh_hidden(left, right, own, out, name):
        for k in (3, 2, 1, 0):
            zz = plane_at(k)
            term = tn(columns(left, zz), right)
            own[zz], out[zz] = mine(term.reshape(2, -1, term.shape[-1]), 0)
            moves[name](k).start()

    def weigh_width(left, right, own, out, high, low):
        term = tn(columns(left, 2 * high + low), right)
        held, given = mine(term.reshape(2, 2, 2, -1, term.shape[-1]), 2)
        for y in range(2):
            spot = y + 2 * high, slice(2 * low, 2 * low + 2)
            own[spot], out[spot] = held[y], given[y]

    def across(own, came, zout, name, k, cut=slice(None)):
        zz = plane_at(k)
        total = own[zz, cut] + came[zz, cut].astype(jnp.float32)
        zout[k - 1, cut] = total.astype(jnp.bfloat16)
        moves[name](k).start()

    def across_far(own, came, zout, zin, name, cut=slice(None)):
        moves[name](3).wait_recv()
        zz = plane_at(2)
        total = own[zz, cut] + came[zz, cut].astype(jnp.float32)
        zout[1, cut] = (total + zin[2, cut].astype(jnp.float32)).astype(jnp.bfloat16)
        moves[name](2).start()

    def gathered_sum(own, came, zin, *names):
        total = own[plane] + came[plane].astype(jnp.float32)
        for k in (1, 2):
            for name in names:
                moves[name](k).wait_recv()
            total = total + zin[k - 1].astype(jnp.float32)
        return total

    weigh_hidden(act, flat(d2g[...]), gs_own, gs_out, "gss")
    moves["gss"](3).wait_recv()
    across(gs_own, gs_in, gs_zout, "gsz", 3)
    d_pre_all = flat(dpre[...])
    for high, ks in ((1 - plane // 2, (3, 2)), (plane // 2, (1, 0))):
        for low in range(2):
            weigh_width(mg, d_pre_all, ge_own, ge_out, high, low)
        for k in ks:
            moves["ges"](k).start()
    moves["ges"](3).wait_recv()
    across(ge_own, ge_in, ge_zout, "gez", 3)
    for k in (2, 1, 0):
        moves["gss"](k).wait_recv()
        moves["ges"](k).wait_recv()

    d_mid = dtok[...] + collected(2)
    d_first, gain_sum, shift_sum = normalize_back(
        d_mid, norm1[...], rate1[:, 0:1], vfull[3:4, :]
    )
    dtok[...] = d_first
    d1g[0] = d_first.astype(jnp.bfloat16)
    offer("d1")
    apart[2:3, :] = jnp.sum(d_first, axis=0, keepdims=True)
    apart[3:4, :] = gain_sum
    apart[4:5, :] = shift_sum
    start("a")
    bpart[0:8, :] = jnp.zeros((8, width), jnp.float32)

    def attend_back(k, carry):
        take("d1", k)

        d_context = nt(d1g[k], flat(obuf[...])).astype(jnp.bfloat16)
        query, keys, values = (qkv[k, :, i * part : (i + 1) * part] for i in range(3))
        d_query, d_keys, d_values = [], [], []
        for h in heads:
            cols = slice(h * head, (h + 1) * head)
            probs = pbuf[k, h]
            d_values.append(tn(probs.astype(jnp.bfloat16), d_context[:, cols]))
            d_probs = nt(d_context[:, cols], values[:, cols])
            inner = jnp.sum(probs * d_probs, axis=-1, keepdims=True)
            d_scores = (probs * (d_probs - inner)).astype(jnp.bfloat16)
            d_query.append(factor * nn(d_scores, keys[:, cols]))
            d_keys.append(tn(d_scores, query[:, cols]))
        d_query = jnp.concatenate(d_query, axis=1)
        d_values = jnp.concatenate(d_values, axis=1)
        bpart[0:1, :part] += jnp.sum(d_query, axis=0, keepdims=True)
        bpart[1:2, :part] += jnp.sum(d_values, axis=0, keepdims=True)
        low = jnp.concatenate([d_query] + d_keys + [d_values], axis=1).astype(jnp.bfloat16)
        dproj[k] = low
        term = jnp.concatenate([nt(low, flat(tbuf[zz // 2, zz % 2])) for zz in range(PLANES)], axis=1)

        @pl.when(k > 0)
        def _():
            rsend[3, k - 1] = term.astype(jnp.bfloat16)
            moves["r4"](k).start()

        @pl.when(k == 0)
        def _():
            keep[...] = term
            across_far(gs_own, gs_in, gs_zout, gs_zin, "gsz")
            across(gs_own, gs_in, gs_zout, "gsz", 1)

        @pl.when(k == 1)
        def _():
            across_far(ge_own, ge_in, ge_zout, ge_zin, "gez")
            across(ge_own, ge_in, ge_zout, "gez", 1)

        return carry

    lax.fori_loop(0, 4, attend_back, 0)

    d_proj = flat(dproj[...])
    for half in range(2):
        for high in range(2):
            weigh_width(xg, d_proj, gt_own, gt_out, high, half)
        moves["gts"](half).start()
    d_first_all = flat(d1g[...])
    for zz in range(PLANES):
        pair = flat(ctx[...])[:, zz * head : (zz + 1) * head]
        term = tn(pair, d_first_all)
        first, second = term[: head // 2], term[head // 2 :]
        go_own[zz] = jnp.where(core == 0, first, second)
        go_out[zz] = jnp.where(core == 0, second, first).astype(jnp.bfloat16)
    start("gos")
    total = apart[...]
    for k in (1, 2, 3):
        moves["a"](k).wait_recv()
        total = total + ain[k - 1]
    bpart[0:8, :] += total
    start("bz")
    halves = (("gtz", slice(0, 2)), ("gty", slice(2, 4)))
    for half, (name, cut) in enumerate(halves):
        moves["gts"](half).wait_recv()
        across(gt_own, gt_in, gt_zout, name, 3, cut)
    arrive("gos")
    across(go_own, go_in, go_zout, "goz", 3)
    for name, cut in halves:
        across_far(gt_own, gt_in, gt_zout, gt_zin, name, cut)
        across(gt_own, gt_in, gt_zout, name, 1, cut)
    across(go_own, go_in, go_zout, "goz", 1)
    across_far(go_own, go_in, go_zout, go_zin, "goz")

    ig_ref[...] = (dtok[...] + collected(3)).astype(jnp.bfloat16)
    stores[1].start()
    sg_ref[...] = gathered_sum(gs_own, gs_in, gs_zin, "gsz")
    stores[5].start()

    def hand_out(total, pout, pin, name):
        low = total.astype(jnp.bfloat16)
        pout[...] = low
        pin[chip] = pout[chip]
        start(name)

    hand_out(gathered_sum(ge_own, ge_in, ge_zin, "gez"), ge_pout, ge_pin, "gep")
    total = bpart[...]
    for k in (1, 2, 3):
        moves["bz"](k).wait_recv()
        total = total + bin_[k - 1]
    bsum[...] = total
    start("bs")
    hand_out(gathered_sum(gt_own, gt_in, gt_zin, "gtz", "gty"), gt_pout, gt_pin, "gtp")
    og_ref[...] = gathered_sum(go_own, go_in, go_zin, "goz")
    stores[3].start()
    arrive("bs")
    bsum_all = bsum.at[...]

    def own_lanes(rows, block, at):
        cols = pl.ds(pl.multiple_of(block * 128, 128), 128)
        wide = bsum_all[rows, cols] + bsib[rows, cols]
        out = jnp.zeros((wide.shape[0], 32), jnp.float32)
        for i in range(4):
            out = out + jnp.where(at == i, wide[:, 32 * i : 32 * i + 32], 0.0)
        return out

    by_rows = own_lanes(
        slice(0, 8), lax.rem(plane, 2) + 2 * (chip // 2) + 4 * (plane // 2), by_row
    )
    by_heads = own_lanes(slice(0, 8), plane // 2, by_head)
    rows = lax.broadcasted_iota(jnp.int32, (8, 32), 0)
    small_ref[...] = jnp.where(rows < 2, by_heads, by_rows)
    cols = pl.ds(pl.multiple_of((plane * 2 + core) * 128, 128), 128)
    ebg_ref[...] = bsum[8:9, cols] + bsib[8:9, cols]
    arrive("gep")
    for other in range(CHIPS):
        for zz in range(PLANES):
            at = share(zz, other) * part
            eg_ref[:, at : at + part] = ge_pin[
                other, :, zz * part : (zz + 1) * part
            ].astype(jnp.float32)
    stores[4].start()
    arrive("gtp")
    holder = {share(zz, other): (zz, other) for zz in range(PLANES) for other in range(CHIPS)}
    for kind in range(3):
        for first in range(0, HEADS, 2):
            at = kind * width + first * piece
            tg_ref[:, at : at + 2 * piece] = jnp.concatenate(
                [
                    gt_pin[other, :, kind * part + zz * piece :][:, :piece]
                    for zz, other in (holder[first], holder[first + 1])
                ],
                axis=1,
            ).astype(jnp.float32)
    stores[2].start()
    for name in COPIES:
        for k in span(name):
            moves[name](k).wait_send()
    for store in stores:
        store.wait()


def hand_over(*refs):
    small_ref, ebg_ref = refs[6:8]
    outs = refs[8:-1]
    moved = [
        pltpu.make_async_copy(refs[i], outs[i], refs[-1].at[i]) for i in range(6)
    ]
    for item in moved:
        item.start()
    for i in range(8):
        outs[6 + i][...] = small_ref[i : i + 1, :]
    outs[14][...] = ebg_ref[...]
    for item in moved:
        item.wait()


def plane_body(
    inputs,
    live_keys,
    triple_weight,
    query_bias,
    value_bias,
    output_weight,
    output_bias,
    first_gain,
    first_shift,
    expand_weight,
    expand_bias,
    shrink_weight,
    shrink_bias,
    second_gain,
    second_shift,
    cotangent,
):
    rows, width = inputs.shape
    own = triple_weight.shape[0]
    part = width // PLANES
    hidden = expand_weight.shape[1] // CHIPS
    low, full = jnp.bfloat16, jnp.float32
    vectors = (
        query_bias,
        value_bias,
        output_bias,
        first_gain,
        first_shift,
        shrink_bias,
        second_gain,
        second_shift,
    )
    shrink = shrink_weight.shape[0]
    outs = (
        ((rows, width), low),
        ((rows, width), low),
        (triple_weight.shape, full),
        (output_weight.shape, full),
        (expand_weight.shape, full),
        (shrink_weight.shape, full),
        ((8, own), full),
        ((1, 128), full),
    )
    P4, C4 = PLANES, CHIPS
    scratch = [
        (triple_weight.shape, low),
        (expand_weight.shape, low),
        ((rows, width), low),
        ((1, rows), jnp.int32),
    ]
    scratch += [((1, own), low)] * 8 + [((1, shrink), low)] + list(outs[:6])
    scratch += [
        ((P4, C4, 2, 16, 128), full),
        ((16, width), full),
        ((16, part), full),
        ((8, hidden), full),
        ((C4, own, 3 * part), low),
        ((2, 2, 2, 2, 2, own, 3 * part), low),
        ((C4, own, hidden), low),
        ((2, 2, 2, 2, 2, own, hidden), low),
        ((P4, 2, own, width), low),
        ((P4, 2, shrink, width), low),
        ((C4, rows, width), low),
        ((C4, rows, width), low),
        ((C4, rows, width), low),
        ((C4, rows, width), low),
        ((4, 3, rows, width), low),
        ((4, 3, rows, width), low),
        ((rows, width), full),
        ((C4, rows, 3 * part), low),
        ((C4, P4, rows, rows), full),
        ((C4, rows, part), low),
        ((C4, rows, hidden), full),
        ((C4, rows, hidden), low),
        ((C4, rows, hidden), low),
        ((C4, rows, 3 * part), low),
        ((rows, width), full),
        ((rows, 128), full),
        ((rows, width), full),
        ((rows, width), full),
        ((P4, shrink, width), full),
        ((P4, shrink, width), low),
        ((P4, shrink, width), low),
        ((3, shrink, width), low),
        ((3, shrink, width), low),
        ((P4, C4, own, hidden), full),
        ((P4, C4, own, hidden), low),
        ((P4, C4, own, hidden), low),
        ((3, C4, own, hidden), low),
        ((3, C4, own, hidden), low),
        ((C4, own, hidden), low),
        ((C4, own, hidden), low),
        ((P4, own, width), full),
        ((P4, own, width), low),
        ((P4, own, width), low),
        ((3, own, width), low),
        ((3, own, width), low),
        ((P4, C4, own, 3 * part), full),
        ((P4, C4, own, 3 * part), low),
        ((P4, C4, own, 3 * part), low),
        ((3, C4, own, 3 * part), low),
        ((3, C4, own, 3 * part), low),
        ((C4, own, 3 * part), low),
        ((C4, own, 3 * part), low),
        ((8, width), full),
        ((3, 8, width), full),
        ((16, width), full),
        ((3, 16, width), full),
        ((16, width), full),
        ((16, width), full),
    ]
    anywhere = pl.BlockSpec(memory_space=pl.ANY)
    inside = pl.BlockSpec(memory_space=pltpu.VMEM)
    given = (
        inputs,
        live_keys[None, :],
        triple_weight,
        output_weight,
        expand_weight,
        shrink_weight,
        cotangent,
    )
    given += tuple(vector[None, :] for vector in vectors) + (expand_bias[None, :],)
    result = pl.pallas_call(
        plane_kernel,
        out_shape=[jax.ShapeDtypeStruct(*item) for item in outs],
        in_specs=[anywhere] * len(given),
        out_specs=[anywhere] * 6 + [inside] * 2,
        scratch_shapes=[pltpu.VMEM(*item) for item in scratch]
        + [pltpu.SemaphoreType.DMA((COPY_COUNT,))] * 2
        + [pltpu.SemaphoreType.DMA((16,)), pltpu.SemaphoreType.DMA((6,))],
        compiler_params=pltpu.CompilerParams(
            collective_id=0, has_side_effects=True, vmem_limit_bytes=60 * 2**20
        ),
        cost_estimate=pl.CostEstimate(
            flops=6 * rows * width * 12 * width,
            bytes_accessed=16 * 2**20,
            transcendentals=rows * hidden * 8,
        ),
        name="plane_layer",
    )(*given)
    ends = list(outs[:6]) + [((1, own), full)] * 8 + [((1, shrink), full)]
    done = pl.pallas_call(
        hand_over,
        out_shape=[jax.ShapeDtypeStruct(*item) for item in ends],
        in_specs=[inside] * 8,
        out_specs=[anywhere] * 6 + [inside] * 9,
        scratch_shapes=[pltpu.SemaphoreType.DMA((6,))],
        name="hand_over",
    )(*result)
    layer_out, input_grad, triple_grad, output_grad, expand_grad, shrink_grad = done[:6]
    small = [item[0] for item in done[6:]]
    return (
        layer_out,
        input_grad,
        triple_grad,
        small[0],
        small[1],
        output_grad,
        small[2],
        small[3],
        small[4],
        expand_grad,
        small[8],
        shrink_grad,
        small[5],
        small[6],
        small[7],
    )


def solution(mesh):
    placed = (
        P("fsdp", None),
        P("fsdp"),
        P("fsdp", None),
        P("fsdp"),
        P("fsdp"),
        P("fsdp", None),
        P("fsdp"),
        P("fsdp"),
        P("fsdp"),
        P("fsdp", None),
        P("fsdp"),
        P("fsdp", None),
        P("fsdp"),
        P("fsdp"),
        P("fsdp"),
        P("fsdp", None),
    )
    return jax.shard_map(
        plane_body if mesh.shape["fsdp"] == PLANES * GROUP else body,
        mesh=mesh,
        in_specs=placed,
        out_specs=(
            P("fsdp", None),
            P("fsdp", None),
            P("fsdp", None),
            P("fsdp"),
            P("fsdp"),
            P("fsdp", None),
            P("fsdp"),
            P("fsdp"),
            P("fsdp"),
            P("fsdp", None),
            P("fsdp"),
            P("fsdp", None),
            P("fsdp"),
            P("fsdp"),
            P("fsdp"),
        ),
        check_vma=False,
    )
```
